32 devices in a mesh: cores: 2 (over y), gz: 4 (over z), gy: 2 (over x), col: 2 (over core).
Axes of the slice: x: 2, y: 2, z: 4, core: 2. Of those that a mesh axis runs over, the one named last changes fastest.
Arguments:
- density: bfloat16 [32, 64, 512], P(('cores', 'gz'), 'gy', 'col'), parts along dimension 0, may hold values from -6 to 6
- first_kernel: bfloat16 [27, 8, 1], replicated, may hold values from -1.25 to 1.25
- first_bias: float32 [8], replicated, may hold values from -3 to 3
- second_kernel: bfloat16 [27, 2, 8], replicated, may hold values from -0.625 to 0.625
- second_bias: float32 [2], replicated, may hold values from -3 to 3
- owners: int32 [8, 2, 2, 16, 1], P(('cores', 'gz'), 'gy', 'col'), parts along dimension 0, may hold values from 0 to 3; in each aligned block of 16 rows (0 to 15, 16 to 31, ..., all dimensions but the last counted through in order) at most 8 rows name the same one
- solutes: float32 [8, 2, 2, 32, 2, 4, 4, 128], P(('cores', 'gz'), 'gy', 'col'), parts along dimension 0, may hold values from 0.2 to 2
- biomass: bfloat16 [8, 2, 2, 32, 4, 4, 128], P(('cores', 'gz'), 'gy', 'col'), parts along dimension 0, may hold values from 0.099609375 to 1
Outputs:
- fractions: bfloat16 [2, 32, 64, 512], P(None, ('cores', 'gz'), 'gy', 'col'), parts along dimension 1
- solutes_next: float32 [8, 2, 2, 32, 2, 4, 4, 128], P(('cores', 'gz'), 'gy', 'col'), parts along dimension 0
The draws below stay inside these ranges and needn't reach their ends.
There are 2 independent parts, one for each index of `cores`. The reference program is written for one: setup_inputs(seed, part) draws one part's arguments, and reference() takes and returns one part's arrays. A program takes and returns all parts, laid end to end along the dimension named above; an argument that names none is the same for every part. Nothing has to cross between parts.
Inputs may be any that keep to these rules, and one draw needn't show every extreme that they name: `owners`: among the 16 bricks of one device at most 8 name the same owner, and some device reaches 8.
All inputs are finite; a program needn't handle non-finite values.
Results may differ from the reference program's by a relative error of at most 0.0034.
Values may be sent and summed in bfloat16 or wider, within the bound.
A program may use at most 64 MiB of HBM per device.

```python
import math
import jax
import jax.numpy as jnp
import numpy as np

CH = 8
CZ = 4
CY = 32
CX = 256
BY = 4
BX = 128
STEPS = 4
NB = 16
CAP = 8
SLOTS = 32
NZ = 16
NY = 64
NX = 512
N_GZ = 4
N_GY = 2
N_COL = 2


def block_levels(own_key, dims, pieces, least, largest):
    gain = 1.0
    for position, blocks in pieces:
        steps = jax.random.uniform(jax.random.fold_in(jax.random.fold_in(own_key, 6), position), (blocks,), jnp.float32, least / len(pieces), largest / len(pieces))
        gain = gain * jnp.repeat(jnp.exp(steps), dims[position] // blocks).reshape((-1,) + (1,) * (len(dims) - 1 - position))
    return gain


def routed_block(own_key, own, number, rows, number_of, top, bound, slope):
    sequence = jax.random.permutation(own_key, number_of)
    heavy_load, ordinary = shares(number_of, rows * top, bound, slope, True), shares(number_of, rows * top, bound, slope, False)
    places = jnp.arange(number_of)

    def named(sizes, offset_by):
        used = int((sizes > 0).sum())
        fixed = max(1, used // 4)
        passed = fixed + (places - fixed + offset_by * (used - fixed)) % max(1, number_of - fixed)
        return jnp.zeros((number_of,), jnp.int32).at[sequence[jnp.where(places < fixed, places, passed)]].set(jnp.asarray(sizes, jnp.int32))

    sizes = jnp.where(number % 4 == 0, named(heavy_load, number // 4), named(ordinary, number - number // 4 - 1))
    mixed = jax.random.permutation(jax.random.fold_in(own, 3), number_of)
    donor, taker = mixed[0:number_of // 2 * 2:2], mixed[1:number_of // 2 * 2:2]
    slack = jnp.minimum(sizes[donor] - 1, bound - sizes[taker]) // 2
    slack = jnp.where((donor == sequence[0]) | (taker == sequence[0]) | (sizes[taker] == 0), 0, jnp.maximum(slack, 0))
    passed = jax.random.randint(jax.random.fold_in(own, 4), (number_of // 2,), 0, 1 << 20) % (slack + 1)
    sizes = sizes.at[donor].add(-passed).at[taker].add(passed)
    items = jnp.searchsorted(jnp.cumsum(sizes), jnp.arange(rows * top), side="right").astype(jnp.int32)
    table = items.reshape(top, rows).T
    table = table[jax.random.permutation(jax.random.fold_in(own, 1), rows)]
    offset_by = jax.random.randint(jax.random.fold_in(own, 2), (rows, 1), 0, top)
    return jnp.take_along_axis(table, (jnp.arange(top)[None, :] + offset_by) % top, axis=1)


def shares(count, total, reach, lean, full):
    loads = [(1 << 20) // math.isqrt(grade ** lean) + 1 for grade in range(1, count + 1)]
    largest = reach if full else min(reach, max(-(-total // count), total * loads[0] // sum(loads)))
    least = 1 if total - largest >= count - 1 else 0
    holding, spare = [largest] + [least] * (count - 1), total - largest - least * (count - 1)
    while spare > 0:
        candidates = [i for i in range(1, count) if holding[i] < largest] or [i for i in range(1, count) if holding[i] < reach]
        pool, remaining = sum([loads[i] for i in candidates]), spare
        for i in candidates:
            more = min(reach - holding[i], max(1, remaining * loads[i] // pool), spare)
            holding[i] = holding[i] + more
            spare = spare - more
    return np.array(holding)


def bell_draw(own_key, dims, scale, reach, pieces=(), held_as=jnp.bfloat16):
    loudness = block_levels(own_key, dims, pieces, -0.22, 0.18) if pieces else 1.0
    result = jax.random.normal(own_key, dims, jnp.float32) * scale * loudness
    return jnp.minimum(jnp.maximum(result, -reach), reach).astype(held_as)


def setup_inputs(seed: int = 0, part: int = 0) -> dict:
    keys = jax.random.split(jax.random.key(seed), 9)
    part_keys = jax.random.split(jax.random.fold_in(keys[8], part), 9)
    density = bell_draw(part_keys[0], (NZ, NY, NX), 1.0, 6.0, ((0, 4), (1, 2), (2, 2)))
    first_kernel = bell_draw(keys[1], (27, CH, 1), 27 ** -0.5, 1.25)
    first_bias = bell_draw(keys[2], (CH,), 1.0, 3.0, (), jnp.float32)
    second_kernel = bell_draw(keys[3], (27, 2, CH), (27 * CH // 2) ** -0.5, 0.625)
    second_bias = bell_draw(keys[4], (2,), 1.0, 3.0, (), jnp.float32)
    owners_keys = jax.random.split(jax.random.fold_in(part_keys[5], 1), N_GZ * N_GY * N_COL * NB // NB)
    owners_turns = jax.random.permutation(jax.random.fold_in(part_keys[5], 3), N_GZ * N_GY * N_COL * NB // NB)
    owners = jax.vmap(lambda own, number: routed_block(jax.random.fold_in(part_keys[5], 2), own, number, NB, N_GZ, 1, CAP, 2))(owners_keys, owners_turns).reshape((N_GZ, N_GY, N_COL, NB, 1))
    solutes = jnp.clip(jnp.exp(math.log(2.0) - 2.3025851 * jax.random.uniform(part_keys[6], (N_GZ, N_GY, N_COL, SLOTS, 2, CZ, BY, BX), jnp.float32) ** block_levels(part_keys[6], (N_GZ, N_GY, N_COL, SLOTS, 2, CZ, BY, BX), ((0, 4), (1, 2), (2, 2)), -0.2, 0.2)), 0.2, 2.0)
    biomass = jnp.clip(jnp.exp(math.log(1.0) - 2.306499 * jax.random.uniform(part_keys[7], (N_GZ, N_GY, N_COL, SLOTS, CZ, BY, BX), jnp.float32) ** block_levels(part_keys[7], (N_GZ, N_GY, N_COL, SLOTS, CZ, BY, BX), ((0, 4), (1, 2), (2, 2)), -0.2, 0.2)), 0.099609375, 1.0).astype(jnp.bfloat16)
    return dict(density=density, first_kernel=first_kernel, first_bias=first_bias, second_kernel=second_kernel, second_bias=second_bias, owners=owners, solutes=solutes, biomass=biomass)


def conv_layer(padded, weights, depth, rows, columns):
    total = jnp.zeros((weights.shape[1], depth, rows, columns), jnp.float32)
    for offset in range(27):
        shift_z = offset // 9
        shift_y = (offset // 3) % 3
        shift_x = offset % 3
        window = padded[:, shift_z:shift_z + depth, shift_y:shift_y + rows, shift_x:shift_x + columns]
        total = total + jnp.einsum("oc,czyx->ozyx", weights[offset].astype(jnp.float32), window.astype(jnp.float32))
    return total


def laplace(field):
    padded = jnp.pad(field, [(0, 0)] * (field.ndim - 3) + [(1, 1), (1, 1), (1, 1)], mode="edge")
    centre = padded[..., 1:-1, 1:-1, 1:-1]
    beside_all = padded[..., 2:, 1:-1, 1:-1] + padded[..., :-2, 1:-1, 1:-1]
    beside_all = beside_all + padded[..., 1:-1, 2:, 1:-1] + padded[..., 1:-1, :-2, 1:-1]
    beside_all = beside_all + padded[..., 1:-1, 1:-1, 2:] + padded[..., 1:-1, 1:-1, :-2]
    return beside_all - 6.0 * centre


def advance(state, arrived, biomass):
    pore = arrived[..., 0, :, :, :].astype(jnp.float32)
    organic = arrived[..., 1, :, :, :].astype(jnp.float32)
    mass = biomass.astype(jnp.float32)
    carbon = state[..., 0, :, :, :]
    oxygen = state[..., 1, :, :, :]
    for step in range(STEPS):
        uptake = 0.25 * mass * carbon / (0.5 + jnp.abs(carbon)) * oxygen / (0.3 + jnp.abs(oxygen))
        carbon_new = carbon + 0.12 * pore * laplace(carbon) + 0.3 * organic - uptake
        oxygen_new = oxygen + 0.16 * pore * laplace(oxygen) - uptake
        carbon, oxygen = carbon_new, oxygen_new
    return jnp.stack([carbon, oxygen], axis=-4)


def reference(density, first_kernel, first_bias, second_kernel, second_bias, owners, solutes, biomass):
    padded = jnp.pad(density[None], ((0, 0), (1, 1), (1, 1), (1, 1)))
    first = conv_layer(padded, first_kernel, NZ, NY, NX)
    hidden = jnp.maximum(first + first_bias[:, None, None, None], 0.0).astype(jnp.bfloat16)
    padded = jnp.pad(hidden, ((0, 0), (1, 1), (1, 1), (1, 1)))
    second = conv_layer(padded, second_kernel, NZ, NY, NX)
    fractions = jax.nn.sigmoid(second + second_bias[:, None, None, None]).astype(jnp.bfloat16)
    bricks = fractions.reshape(2, N_GZ, CZ, N_GY, CY // BY, BY, N_COL, CX // BX, BX)
    bricks = bricks.transpose(1, 3, 6, 4, 7, 0, 2, 5, 8).reshape(N_GZ, N_GY, N_COL, NB, 2, CZ, BY, BX)
    target = owners[..., 0].astype(jnp.int32)
    onehot = (target[..., None] == jnp.arange(N_GZ, dtype=jnp.int32)).astype(jnp.int32)
    before = jnp.cumsum(onehot, axis=3) - onehot
    rank = jnp.sum(before * onehot, axis=-1).astype(jnp.int32)
    source = jnp.broadcast_to(jnp.arange(N_GZ, dtype=jnp.int32)[:, None, None, None], target.shape)
    row_index = jnp.broadcast_to(jnp.arange(N_GY, dtype=jnp.int32)[None, :, None, None], target.shape)
    col_index = jnp.broadcast_to(jnp.arange(N_COL, dtype=jnp.int32)[None, None, :, None], target.shape)
    slot_index = source * CAP + rank
    arrived = jnp.zeros((N_GZ, N_GY, N_COL, SLOTS, 2, CZ, BY, BX), jnp.bfloat16)
    arrived = arrived.at[target, row_index, col_index, slot_index].set(bricks)
    solutes_next = advance(solutes, arrived, biomass)
    return fractions, solutes_next
```

```python
import functools
import itertools

import jax
import jax.numpy as jnp
from jax import lax
from jax.experimental import pallas as pl
from jax.experimental.pallas import tpu as pltpu
from jax.sharding import PartitionSpec as P

BY = 4
BX = 128
STEPS = 4
MESH = pl.DeviceIdType.MESH
F32 = jnp.float32
BF16 = jnp.bfloat16
AROUND = [d for d in itertools.product((-1, 0, 1), repeat=3) if d != (0, 0, 0)]
PLACE_Z = {0: (0, 4), 1: (4, 2), -1: (6, 2)}
PLACE_Y = {0: (0, 32), 1: (32, 16), -1: (48, 16)}
PLACE_X = {0: (0, 256), 1: (256, 128), -1: (384, 128)}
TAKE_Z = {0: (0, 4), 1: (0, 2), -1: (2, 2)}
TAKE_Y = {0: (0, 32), 1: (0, 16), -1: (16, 16)}
TAKE_X = {0: (0, 256), 1: (0, 128), -1: (128, 128)}
KR = 48
HR = 34
LANES = 384


def region(ref, tables, offset):
    return ref.at[tuple(pl.ds(*table[o]) for table, o in zip(tables, offset))]


def iota(shape, dim):
    return lax.broadcasted_iota(jnp.int32, shape, dim)


def onehot(condition):
    return jnp.where(condition, 1.0, 0.0).astype(BF16)


def dot(a, b):
    return jnp.dot(a, b, preferred_element_type=F32)


def build_first(w1):
    hidden = w1.shape[0]
    rows, cols = hidden * HR, 9 * KR
    i = iota((rows, 1), 0)
    channel, yi = lax.div(i, HR), lax.rem(i, HR)
    expand = onehot(channel == iota((rows, hidden), 1))
    by_row = dot(expand, w1).astype(BF16)
    j = iota((1, cols), 1)
    tap, r = lax.div(j, KR), lax.rem(j, KR)
    y = jnp.where(r < 40, r, r - KR)
    tap_offset = lax.div(tap, 3) * 9 + lax.rem(tap, 3)
    total = jnp.zeros((rows, cols), F32)
    for dy in range(3):
        pick = onehot(iota((27, cols), 0) == tap_offset + 3 * dy)
        total = total + jnp.where(y == yi + (dy - 2), dot(by_row, pick), 0.0)
    return total.astype(BF16)


def build_second(w2, first_row, last_row):
    hidden = w2.shape[0] // 2
    rows, cols = 192, hidden * HR
    i = iota((rows, 1), 0)
    group, y = lax.div(i, 32), lax.rem(i, 32)
    j = iota((1, cols), 1)
    yi = lax.rem(j, HR)
    inside = jnp.logical_not(((yi == 0) & first_row) | ((yi == HR - 1) & last_row))
    yi = jnp.where(inside, yi, -100)
    pick = onehot(lax.rem(iota((2 * hidden, cols), 0), hidden) == lax.div(j, HR))
    same = lax.rem(group, 2) == lax.div(iota((1, 2 * hidden), 1), hidden)
    blocks = []
    for dz in range(3):
        total = jnp.zeros((rows, cols), F32)
        for dy in range(3):
            select = onehot(iota((rows, 27), 1) == 9 * dz + 3 * dy + lax.div(group, 2))
            values = lax.dot_general(
                select, w2, (((1,), (1,)), ((), ())), preferred_element_type=F32
            )
            values = dot(jnp.where(same, values, 0.0).astype(BF16), pick)
            total = total + jnp.where(yi == y + dy, values, 0.0)
        blocks.append(total.astype(BF16))
    return blocks


def build_placing(owners_ref, slots, capacity):
    count = owners_ref.shape[0]
    target = [owners_ref[b] for b in range(count)]
    j = iota((1, 128), 1)
    brick = ((j & 31) >> 2) * 2 + (j >> 6)
    slot = jnp.zeros((1, 128), jnp.int32)
    for b in range(count):
        rank = jnp.int32(0)
        for other in range(b):
            rank = rank + jnp.where(target[other] == target[b], 1, 0)
        slot = jnp.where(brick == b, target[b] * capacity + rank, slot)
    column = slot * 8 + ((j >> 5) & 1) * 4 + (j & 3)
    i = iota((slots * 8, 1), 0)
    owner = lax.div(i, capacity * 8)
    row = (owner * capacity + lax.rem(i, capacity)) * 8 + lax.rem(lax.div(i, capacity), 8)
    return onehot(row == column)


def diffuse(carbon, oxygen, pore, organic, mass, lane):
    low, high = lane == 0, lane == BX - 1
    pore_c = [0.12 * v for v in pore]
    pore_o = [0.16 * v for v in pore]
    gain = [0.3 * v for v in organic]
    mass = [0.25 * v for v in mass]

    def laplace(field, q):
        z, y = q // 4, q % 4
        v = field[q]
        total = jnp.where(low, v, pltpu.roll(v, 1, 1)) + jnp.where(high, v, pltpu.roll(v, BX - 1, 1))
        near = 2
        for ok, at in ((z > 0, q - 4), (z < 3, q + 4), (y > 0, q - 1), (y < 3, q + 1)):
            if ok:
                total = total + field[at]
                near += 1
        return total - float(near) * v

    for _ in range(STEPS):
        carbon_new, oxygen_new = [], []
        for q in range(16):
            c, o = carbon[q], oxygen[q]
            uptake = mass[q] * c * o / ((0.5 + jnp.abs(c)) * (0.3 + jnp.abs(o)))
            carbon_new.append(c + pore_c[q] * laplace(carbon, q) + gain[q] - uptake)
            oxygen_new.append(o + pore_o[q] * laplace(oxygen, q) - uptake)
        carbon, oxygen = carbon_new, oxygen_new
    return carbon, oxygen


def kernel(
    sizes, capacity,
    density, w1_hbm, b1_hbm, w2_hbm, b2_hbm, owners_hbm, solutes, biomass,
    frac, state_new,
    w1_ref, b1_ref, w2_ref, b2_ref, owners_ref, tile, first, second, shifted, hidden, out, arrived, state, mass_in, mass, gathered,
    halo_send, halo_recv, brick_send, brick_recv, local_sem, group_sem,
):
    n, n_gy, n_col = sizes
    slots = n * capacity
    here = (lax.axis_index("gz"), lax.axis_index("gy"), lax.axis_index("col"))
    me = here[0]

    def exists(offset):
        ok = None
        for position, size, o in zip(here, sizes, offset):
            test = None if o == 0 else (position + o >= 0) & (position + o < size)
            ok = test if ok is None else ok if test is None else ok & test
        return ok

    def device(offset):
        return {"gz": here[0] + offset[0], "gy": here[1] + offset[1], "col": here[2] + offset[2]}

    def halo(offset, index, receiver):
        seen = tuple(-o for o in offset) if not receiver else offset
        return pltpu.make_async_remote_copy(
            src_ref=region(density, (TAKE_Z, TAKE_Y, TAKE_X), seen),
            dst_ref=region(tile, (PLACE_Z, PLACE_Y, PLACE_X), seen),
            send_sem=halo_send.at[index],
            recv_sem=halo_recv.at[AROUND.index(seen)],
            device_id=device(offset),
            device_id_type=MESH,
        )

    small = [
        pltpu.make_async_copy(source, target, local_sem.at[4 + i])
        for i, (source, target) in enumerate(
            (
                (w1_hbm, w1_ref), (w2_hbm, w2_ref), (b1_hbm, b1_ref), (b2_hbm, b2_ref),
                (owners_hbm, owners_ref),
            )
        )
    ]
    for copy in small:
        copy.start()
    tile[...] = jnp.zeros_like(tile)
    barrier = pltpu.get_barrier_semaphore()
    expected = jnp.int32(n - 1)
    for offset in AROUND:
        ok = exists(offset)
        expected = expected + jnp.where(ok, 1, 0)

        @pl.when(ok)
        def _():
            pl.semaphore_signal(barrier, inc=1, device_id=device(offset), device_id_type=MESH)

    for j in range(1, n):
        pl.semaphore_signal(
            barrier, inc=1, device_id={"gz": lax.rem(me + j, n)}, device_id_type=MESH
        )
    own = pltpu.make_async_copy(
        density, region(tile, (PLACE_Z, PLACE_Y, PLACE_X), (0, 0, 0)), local_sem.at[0]
    )
    own.start()
    load_state = pltpu.make_async_copy(solutes, state, local_sem.at[1])
    load_mass = pltpu.make_async_copy(biomass, mass_in, local_sem.at[2])
    pl.semaphore_wait(barrier, expected)

    for index, offset in enumerate(AROUND):

        @pl.when(exists(offset))
        def _():
            halo(offset, index, False).start()

    load_state.start()
    load_mass.start()

    for copy in small:
        copy.wait()
    first[...] = build_first(w1_ref[...])
    for dz, block in enumerate(build_second(w2_ref[...], here[1] == 0, here[1] == n_gy - 1)):
        second[dz] = block
    placing = build_placing(owners_ref, slots, capacity)
    channel = lax.div(iota((272, 1), 0), HR)
    bias1 = jnp.zeros((272, 1), F32)
    for o in range(8):
        bias1 = jnp.where(channel == o, b1_ref[o], bias1)
    bias2 = jnp.where(iota((64, 1), 0) < 32, b2_ref[0], b2_ref[1])
    lane = iota((1, BX), 1)
    keep = jnp.where(
        ((lane == 0) & (here[2] < n_col - 1)) | ((lane == BX - 1) & (here[2] > 0)), 1.0, 0.0
    )
    load_mass.wait()
    for g in range(slots // 8):
        mass[g] = mass_in[g].astype(F32)

    own.wait()
    for index, offset in enumerate(AROUND):

        @pl.when(exists(offset))
        def _():
            halo(offset, index, True).wait_recv()

    half_row = iota((16, 512), 0) < 8
    half_lane = iota((KR, BX), 1) < 64
    for zz in range(8):
        z = (zz + 6) % 8
        side = jnp.where(half_row, tile[z, 32:48, :].astype(F32), tile[z, 48:64, :].astype(F32))
        whole = jnp.concatenate([tile[z, 0:32, :].astype(F32), side], axis=0)
        edge = jnp.where(half_lane, whole[:, 256:384], whole[:, 384:512])
        whole = jnp.concatenate([whole[:, :256], edge], axis=1)
        base = zz * 3 * KR
        shifted[base : base + KR, :] = pltpu.roll(whole, 1, 1).astype(BF16)
        shifted[base + KR : base + 2 * KR, :] = whole.astype(BF16)
        shifted[base + 2 * KR : base + 3 * KR, :] = pltpu.roll(whole, LANES - 1, 1).astype(BF16)

    def hidden_slice(zi):
        value = dot(first[...], shifted[zi * 3 * KR : (zi + 3) * 3 * KR, :])
        value = jnp.maximum(value + bias1, 0.0)
        hidden[zi, :, 0:256] = value[:, :256].astype(BF16)
        hidden[zi, :, 256:384] = (value[:, 256:] * keep).astype(BF16)

    def brick_copy(j, z):
        to = lax.rem(me + j, n)
        return pltpu.make_async_remote_copy(
            src_ref=out.at[to, z],
            dst_ref=arrived.at[me, z],
            send_sem=brick_send.at[j, z],
            recv_sem=brick_recv.at[j, z],
            device_id={"gz": to},
            device_id_type=MESH,
        )

    hidden_slice(0)

    @pl.when(me == 0)
    def _():
        hidden[0] = jnp.zeros_like(hidden[0])

    hidden_slice(1)
    per = 8 * capacity
    for z in range(4):
        hidden_slice(z + 2)
        if z == 3:

            @pl.when(me == n - 1)
            def _():
                hidden[5] = jnp.zeros_like(hidden[5])

        total = jnp.zeros((192, LANES), F32)
        for dz in range(3):
            total = total + dot(second[dz], hidden[z + dz])
        value = (
            pltpu.roll(total[0:64], 1, 1) + total[64:128] + pltpu.roll(total[128:192], LANES - 1, 1)
        )[:, :256]
        value = (1.0 / (1.0 + jnp.exp(-(value + bias2)))).astype(BF16)
        frac[0, z] = value[:32]
        frac[1, z] = value[32:]
        placed = dot(placing, jnp.concatenate([value[:, :128], value[:, 128:]], axis=0)).astype(BF16)
        for d in range(n):
            out[d, z] = placed[d * per : (d + 1) * per]
        for j in range(1, n):
            brick_copy(j, z).start()

    load_state.wait()

    def received(j, z):
        source = lax.rem(me - j + n, n)
        pltpu.make_async_remote_copy(
            src_ref=out.at[source, z],
            dst_ref=arrived.at[source, z],
            send_sem=brick_send.at[j, z],
            recv_sem=brick_recv.at[j, z],
            device_id={"gz": source},
            device_id_type=MESH,
        ).wait_recv()


    def group(g, pore, organic):
        carbon = [state[g, pl.ds(q, 8, stride=32), :] for q in range(16)]
        oxygen = [state[g, pl.ds(16 + q, 8, stride=32), :] for q in range(16)]
        held = [mass[g, pl.ds(q, 8, stride=16), :] for q in range(16)]
        carbon, oxygen = diffuse(carbon, oxygen, pore, organic, held, iota((8, BX), 1))
        for q in range(16):
            state_new[g, pl.ds(q, 8, stride=32), :] = carbon[q]
            state_new[g, pl.ds(16 + q, 8, stride=32), :] = oxygen[q]

    if capacity == 8:
        for j in range(n):
            source = lax.rem(me - j + n, n)
            values = [[None] * 16, [None] * 16]
            for z in range(4):
                if j:
                    received(j, z)
                ref = arrived if j else out
                for o in range(2):
                    for pair in range(2):
                        at = o * 32 + pair * 16
                        both = ref[source, z, at : at + 16, :].astype(F32)
                        values[o][z * 4 + pair * 2] = both[:8]
                        values[o][z * 4 + pair * 2 + 1] = both[8:]
            group(source, *values)
    else:
        for z in range(4):
            arrived[me, z] = out[me, z]
        for j in range(1, n):
            for z in range(4):
                received(j, z)
        for s in range(n):
            for z in range(4):
                block = arrived[s, z].astype(F32)
                for o in range(2):
                    for y in range(4):
                        at = (o * 4 + y) * capacity
                        gathered[o * 16 + z * 4 + y, s * capacity : (s + 1) * capacity, :] = block[
                            at : at + capacity
                        ]

        @pl.loop(0, slots // 8)
        def _(g):
            start = pl.multiple_of(g * 8, 8)
            group(
                g,
                [gathered[q, pl.ds(start, 8), :] for q in range(16)],
                [gathered[16 + q, pl.ds(start, 8), :] for q in range(16)],
            )

    for index, offset in enumerate(AROUND):

        @pl.when(exists(offset))
        def _():
            halo(offset, index, False).wait_send()

    for j in range(1, n):
        for z in range(4):
            brick_copy(j, z).wait_send()


def write_out(frac, state, fractions, solutes_next, sem):
    copies = [
        pltpu.make_async_copy(frac, fractions, sem.at[0]),
        pltpu.make_async_copy(state, solutes_next, sem.at[1]),
    ]
    for copy in copies:
        copy.start()
    for copy in copies:
        copy.wait()


def per_device(
    sizes, density, first_kernel, first_bias, second_kernel, second_bias, owners, solutes, biomass
):
    n = sizes[0]
    slots = solutes.shape[3]
    capacity = slots // n
    per = 8 * capacity
    anywhere = pl.BlockSpec(memory_space=pltpu.HBM)
    groups = slots // 8
    inside = pl.BlockSpec(memory_space=pltpu.VMEM)
    frac, state_new = pl.pallas_call(
        functools.partial(kernel, sizes, capacity),
        out_shape=(
            pltpu.VMEM((2,) + density.shape, BF16),
            pltpu.VMEM((groups, 256, BX), F32),
        ),
        in_specs=[anywhere] * 8,
        out_specs=(inside, inside),
        scratch_shapes=[
            pltpu.VMEM((8, 27), BF16),
            pltpu.SMEM((8,), F32),
            pltpu.VMEM((16, 27), BF16),
            pltpu.SMEM((2,), F32),
            pltpu.SMEM((16,), jnp.int32),
            pltpu.VMEM((8, 64, 512), BF16),
            pltpu.VMEM((272, 9 * KR), BF16),
            pltpu.VMEM((3, 192, 272), BF16),
            pltpu.VMEM((8 * 3 * KR, LANES), BF16),
            pltpu.VMEM((6, 272, LANES), BF16),
            pltpu.VMEM((n, 4, per, BX), BF16),
            pltpu.VMEM((n, 4, per, BX), BF16),
            pltpu.VMEM((groups, 256, BX), F32),
            pltpu.VMEM((groups, 128, BX), BF16),
            pltpu.VMEM((groups, 128, BX), F32),
            pltpu.VMEM((32, slots if capacity != 8 else 8, BX), F32),
            pltpu.SemaphoreType.DMA((26,)),
            pltpu.SemaphoreType.DMA((26,)),
            pltpu.SemaphoreType.DMA((n, 4)),
            pltpu.SemaphoreType.DMA((n, 4)),
            pltpu.SemaphoreType.DMA((9,)),
            pltpu.SemaphoreType.DMA((groups,)),
        ],
        compiler_params=pltpu.CompilerParams(
            collective_id=0, has_side_effects=True, vmem_limit_bytes=(65344 - 128 - groups * 128) * 1024
        ),
    )(
        density,
        first_kernel.transpose(2, 1, 0).reshape(8, 27),
        first_bias,
        second_kernel.transpose(1, 2, 0).reshape(16, 27),
        second_bias,
        owners.reshape(-1),
        solutes.reshape(groups, 256, BX),
        biomass.reshape(groups, 128, BX),
    )
    fractions, solutes_next = pl.pallas_call(
        write_out,
        out_shape=(
            jax.ShapeDtypeStruct((2,) + density.shape, BF16),
            jax.ShapeDtypeStruct((groups, 256, BX), F32),
        ),
        in_specs=[inside, inside],
        out_specs=(anywhere, anywhere),
        scratch_shapes=[pltpu.SemaphoreType.DMA((2,))],
        compiler_params=pltpu.CompilerParams(vmem_limit_bytes=16 * 1024 * 1024),
    )(frac, state_new)
    return fractions, solutes_next.reshape(solutes.shape)


def solution(mesh):
    sizes = tuple(mesh.shape[axis] for axis in ("gz", "gy", "col"))
    return jax.shard_map(
        functools.partial(per_device, sizes),
        mesh=mesh,
        in_specs=(
            P(("cores", "gz"), "gy", "col"),
            P(),
            P(),
            P(),
            P(),
            P(("cores", "gz"), "gy", "col", None, None),
            P(("cores", "gz"), "gy", "col", None, None, None, None, None),
            P(("cores", "gz"), "gy", "col", None, None, None, None),
        ),
        out_specs=(
            P(None, ("cores", "gz"), "gy", "col"),
            P(("cores", "gz"), "gy", "col", None, None, None, None, None),
        ),
        check_vma=False,
    )
```

```python
import functools
import itertools

import jax
import jax.numpy as jnp
from jax import lax
from jax.experimental import pallas as pl
from jax.experimental.pallas import tpu as pltpu
from jax.sharding import PartitionSpec as P

BY = 4
BX = 128
STEPS = 4
MESH = pl.DeviceIdType.MESH
F32 = jnp.float32
BF16 = jnp.bfloat16
AROUND = [d for d in itertools.product((-1, 0, 1), repeat=3) if d != (0, 0, 0)]
PLACE_Z = {0: (0, 4), 1: (4, 2), -1: (6, 2)}
PLACE_Y = {0: (0, 32), 1: (32, 16), -1: (48, 16)}
PLACE_X = {0: (0, 256), 1: (256, 128), -1: (384, 128)}
TAKE_Z = {0: (0, 4), 1: (0, 2), -1: (2, 2)}
TAKE_Y = {0: (0, 32), 1: (0, 16), -1: (16, 16)}
TAKE_X = {0: (0, 256), 1: (0, 128), -1: (128, 128)}
KR = 48
HR = 34
LANES = 384
RBS = 2
EDGE = 2048
OFF = -1e30


def region(ref, tables, offset):
    return ref.at[tuple(pl.ds(*table[o]) for table, o in zip(tables, offset))]


def iota(shape, dim):
    return lax.broadcasted_iota(jnp.int32, shape, dim)


def onehot(condition):
    return jnp.where(condition, 1.0, 0.0).astype(BF16)


def dot(a, b):
    return jnp.dot(a, b, preferred_element_type=F32)


def build_first(w1):
    hidden = w1.shape[0]
    rows, cols = hidden * HR, 9 * KR
    i = iota((rows, 1), 0)
    channel, yi = lax.div(i, HR), lax.rem(i, HR)
    expand = onehot(channel == iota((rows, hidden), 1))
    by_row = dot(expand, w1).astype(BF16)
    j = iota((1, cols), 1)
    tap, r = lax.div(j, KR), lax.rem(j, KR)
    y = jnp.where(r < 40, r, r - KR)
    tap_offset = lax.div(tap, 3) * 9 + lax.rem(tap, 3)
    total = jnp.zeros((rows, cols), F32)
    for dy in range(3):
        pick = onehot(iota((27, cols), 0) == tap_offset + 3 * dy)
        total = total + jnp.where(y == yi + (dy - 2), dot(by_row, pick), 0.0)
    return total.astype(BF16)


def build_second(w2, first_row, last_row):
    hidden = w2.shape[0] // 2
    rows, cols = 192, hidden * HR
    i = iota((rows, 1), 0)
    group, y = lax.div(i, 32), lax.rem(i, 32)
    j = iota((1, cols), 1)
    yi = lax.rem(j, HR)
    inside = jnp.logical_not(((yi == 0) & first_row) | ((yi == HR - 1) & last_row))
    yi = jnp.where(inside, yi, -100)
    pick = onehot(lax.rem(iota((2 * hidden, cols), 0), hidden) == lax.div(j, HR))
    same = lax.rem(group, 2) == lax.div(iota((1, 2 * hidden), 1), hidden)
    blocks = []
    for dz in range(3):
        total = jnp.zeros((rows, cols), F32)
        for dy in range(3):
            select = onehot(iota((rows, 27), 1) == 9 * dz + 3 * dy + lax.div(group, 2))
            values = lax.dot_general(
                select, w2, (((1,), (1,)), ((), ())), preferred_element_type=F32
            )
            values = dot(jnp.where(same, values, 0.0).astype(BF16), pick)
            total = total + jnp.where(yi == y + dy, values, 0.0)
        blocks.append(total.astype(BF16))
    return blocks


def build_placing(owners_ref, slots, capacity):
    count = owners_ref.shape[0]
    target = [owners_ref[b] for b in range(count)]
    j = iota((1, 128), 1)
    brick = ((j & 31) >> 2) * 2 + (j >> 6)
    slot = jnp.zeros((1, 128), jnp.int32)
    for b in range(count):
        rank = jnp.int32(0)
        for other in range(b):
            rank = rank + jnp.where(target[other] == target[b], 1, 0)
        slot = jnp.where(brick == b, target[b] * capacity + rank, slot)
    column = slot * 8 + ((j >> 5) & 1) * 4 + (j & 3)
    i = iota((slots * 8, 1), 0)
    owner = lax.div(i, capacity * 8)
    row = (owner * capacity + lax.rem(i, capacity)) * 8 + lax.rem(lax.div(i, capacity), 8)
    return onehot(row == column)


def diffuse(carbon, oxygen, pore, organic, mass, lane):
    low, high = lane == 0, lane == BX - 1
    pore_c = [0.12 * v for v in pore]
    pore_o = [0.16 * v for v in pore]
    gain = [0.3 * v for v in organic]
    mass = [0.25 * v for v in mass]

    def laplace(field, q):
        z, y = q // 4, q % 4
        v = field[q]
        total = jnp.where(low, v, pltpu.roll(v, 1, 1)) + jnp.where(high, v, pltpu.roll(v, BX - 1, 1))
        near = 2
        for ok, at in ((z > 0, q - 4), (z < 3, q + 4), (y > 0, q - 1), (y < 3, q + 1)):
            if ok:
                total = total + field[at]
                near += 1
        return total - float(near) * v

    for _ in range(STEPS):
        carbon_new, oxygen_new = [], []
        for q in range(16):
            c, o = carbon[q], oxygen[q]
            uptake = mass[q] * c * o / ((0.5 + jnp.abs(c)) * (0.3 + jnp.abs(o)))
            carbon_new.append(c + pore_c[q] * laplace(carbon, q) + gain[q] - uptake)
            oxygen_new.append(o + pore_o[q] * laplace(oxygen, q) - uptake)
        carbon, oxygen = carbon_new, oxygen_new
    return carbon, oxygen


def kernel(
    sizes, capacity,
    density, w1_hbm, b1_hbm, w2_hbm, b2_hbm, owners_hbm, solutes, biomass,
    frac, state_new,
    w1_ref, b1_ref, w2_ref, b2_ref, owners_ref, tile, first, second, shifted, hidden, out, arrived, state, mass_in, mass, gathered,
    halo_send, halo_recv, brick_send, brick_recv, local_sem, group_sem,
):
    n, n_gy, n_col = sizes
    slots = n * capacity
    here = (lax.axis_index("gz"), lax.axis_index("gy"), lax.axis_index("col"))
    me = here[0]

    def exists(offset):
        ok = None
        for position, size, o in zip(here, sizes, offset):
            test = None if o == 0 else (position + o >= 0) & (position + o < size)
            ok = test if ok is None else ok if test is None else ok & test
        return ok

    def device(offset):
        return {"gz": here[0] + offset[0], "gy": here[1] + offset[1], "col": here[2] + offset[2]}

    def halo(offset, index, receiver):
        seen = tuple(-o for o in offset) if not receiver else offset
        return pltpu.make_async_remote_copy(
            src_ref=region(density, (TAKE_Z, TAKE_Y, TAKE_X), seen),
            dst_ref=region(tile, (PLACE_Z, PLACE_Y, PLACE_X), seen),
            send_sem=halo_send.at[index],
            recv_sem=halo_recv.at[AROUND.index(seen)],
            device_id=device(offset),
            device_id_type=MESH,
        )

    small = [
        pltpu.make_async_copy(source, target, local_sem.at[4 + i])
        for i, (source, target) in enumerate(
            (
                (w1_hbm, w1_ref), (w2_hbm, w2_ref), (b1_hbm, b1_ref), (b2_hbm, b2_ref),
                (owners_hbm, owners_ref),
            )
        )
    ]
    for copy in small:
        copy.start()
    tile[...] = jnp.zeros_like(tile)
    barrier = pltpu.get_barrier_semaphore()
    expected = jnp.int32(n - 1)
    for offset in AROUND:
        ok = exists(offset)
        expected = expected + jnp.where(ok, 1, 0)

        @pl.when(ok)
        def _():
            pl.semaphore_signal(barrier, inc=1, device_id=device(offset), device_id_type=MESH)

    for j in range(1, n):
        pl.semaphore_signal(
            barrier, inc=1, device_id={"gz": lax.rem(me + j, n)}, device_id_type=MESH
        )
    own = pltpu.make_async_copy(
        density, region(tile, (PLACE_Z, PLACE_Y, PLACE_X), (0, 0, 0)), local_sem.at[0]
    )
    own.start()
    load_state = pltpu.make_async_copy(solutes, state, local_sem.at[1])
    load_mass = pltpu.make_async_copy(biomass, mass_in, local_sem.at[2])
    pl.semaphore_wait(barrier, expected)

    for index, offset in enumerate(AROUND):

        @pl.when(exists(offset))
        def _():
            halo(offset, index, False).start()

    load_state.start()
    load_mass.start()

    for copy in small:
        copy.wait()
    first[...] = build_first(w1_ref[...])
    for dz, block in enumerate(build_second(w2_ref[...], here[1] == 0, here[1] == n_gy - 1)):
        second[dz] = block
    placing = build_placing(owners_ref, slots, capacity)
    channel = lax.div(iota((272, 1), 0), HR)
    bias1 = jnp.zeros((272, 1), F32)
    for o in range(8):
        bias1 = jnp.where(channel == o, b1_ref[o], bias1)
    bias2 = jnp.where(iota((64, 1), 0) < 32, b2_ref[0], b2_ref[1])
    lane = iota((1, BX), 1)
    keep = jnp.where(
        ((lane == 0) & (here[2] < n_col - 1)) | ((lane == BX - 1) & (here[2] > 0)), 1.0, 0.0
    )
    load_mass.wait()
    for g in range(slots // 8):
        mass[g] = mass_in[g].astype(F32)

    own.wait()
    for index, offset in enumerate(AROUND):

        @pl.when(exists(offset))
        def _():
            halo(offset, index, True).wait_recv()

    half_row = iota((16, 512), 0) < 8
    half_lane = iota((KR, BX), 1) < 64
    for zz in range(8):
        z = (zz + 6) % 8
        side = jnp.where(half_row, tile[z, 32:48, :].astype(F32), tile[z, 48:64, :].astype(F32))
        whole = jnp.concatenate([tile[z, 0:32, :].astype(F32), side], axis=0)
        edge = jnp.where(half_lane, whole[:, 256:384], whole[:, 384:512])
        whole = jnp.concatenate([whole[:, :256], edge], axis=1)
        base = zz * 3 * KR
        shifted[base : base + KR, :] = pltpu.roll(whole, 1, 1).astype(BF16)
        shifted[base + KR : base + 2 * KR, :] = whole.astype(BF16)
        shifted[base + 2 * KR : base + 3 * KR, :] = pltpu.roll(whole, LANES - 1, 1).astype(BF16)

    def hidden_slice(zi):
        value = dot(first[...], shifted[zi * 3 * KR : (zi + 3) * 3 * KR, :])
        value = jnp.maximum(value + bias1, 0.0)
        hidden[zi, :, 0:256] = value[:, :256].astype(BF16)
        hidden[zi, :, 256:384] = (value[:, 256:] * keep).astype(BF16)

    def brick_copy(j, z):
        to = lax.rem(me + j, n)
        return pltpu.make_async_remote_copy(
            src_ref=out.at[to, z],
            dst_ref=arrived.at[me, z],
            send_sem=brick_send.at[j, z],
            recv_sem=brick_recv.at[j, z],
            device_id={"gz": to},
            device_id_type=MESH,
        )

    hidden_slice(0)

    @pl.when(me == 0)
    def _():
        hidden[0] = jnp.zeros_like(hidden[0])

    hidden_slice(1)
    per = 8 * capacity
    for z in range(4):
        hidden_slice(z + 2)
        if z == 3:

            @pl.when(me == n - 1)
            def _():
                hidden[5] = jnp.zeros_like(hidden[5])

        total = jnp.zeros((192, LANES), F32)
        for dz in range(3):
            total = total + dot(second[dz], hidden[z + dz])
        value = (
            pltpu.roll(total[0:64], 1, 1) + total[64:128] + pltpu.roll(total[128:192], LANES - 1, 1)
        )[:, :256]
        value = (1.0 / (1.0 + jnp.exp(-(value + bias2)))).astype(BF16)
        frac[0, z] = value[:32]
        frac[1, z] = value[32:]
        placed = dot(placing, jnp.concatenate([value[:, :128], value[:, 128:]], axis=0)).astype(BF16)
        for d in range(n):
            out[d, z] = placed[d * per : (d + 1) * per]
        for j in range(1, n):
            brick_copy(j, z).start()

    load_state.wait()

    def received(j, z):
        source = lax.rem(me - j + n, n)
        pltpu.make_async_remote_copy(
            src_ref=out.at[source, z],
            dst_ref=arrived.at[source, z],
            send_sem=brick_send.at[j, z],
            recv_sem=brick_recv.at[j, z],
            device_id={"gz": source},
            device_id_type=MESH,
        ).wait_recv()


    def group(g, pore, organic):
        carbon = [state[g, pl.ds(q, 8, stride=32), :] for q in range(16)]
        oxygen = [state[g, pl.ds(16 + q, 8, stride=32), :] for q in range(16)]
        held = [mass[g, pl.ds(q, 8, stride=16), :] for q in range(16)]
        carbon, oxygen = diffuse(carbon, oxygen, pore, organic, held, iota((8, BX), 1))
        for q in range(16):
            state_new[g, pl.ds(q, 8, stride=32), :] = carbon[q]
            state_new[g, pl.ds(16 + q, 8, stride=32), :] = oxygen[q]

    if capacity == 8:
        for j in range(n):
            source = lax.rem(me - j + n, n)
            values = [[None] * 16, [None] * 16]
            for z in range(4):
                if j:
                    received(j, z)
                ref = arrived if j else out
                for o in range(2):
                    for pair in range(2):
                        at = o * 32 + pair * 16
                        both = ref[source, z, at : at + 16, :].astype(F32)
                        values[o][z * 4 + pair * 2] = both[:8]
                        values[o][z * 4 + pair * 2 + 1] = both[8:]
            group(source, *values)
    else:
        for z in range(4):
            arrived[me, z] = out[me, z]
        for j in range(1, n):
            for z in range(4):
                received(j, z)
        for s in range(n):
            for z in range(4):
                block = arrived[s, z].astype(F32)
                for o in range(2):
                    for y in range(4):
                        at = (o * 4 + y) * capacity
                        gathered[o * 16 + z * 4 + y, s * capacity : (s + 1) * capacity, :] = block[
                            at : at + capacity
                        ]

        @pl.loop(0, slots // 8)
        def _(g):
            start = pl.multiple_of(g * 8, 8)
            group(
                g,
                [gathered[q, pl.ds(start, 8), :] for q in range(16)],
                [gathered[16 + q, pl.ds(start, 8), :] for q in range(16)],
            )

    for index, offset in enumerate(AROUND):

        @pl.when(exists(offset))
        def _():
            halo(offset, index, False).wait_send()

    for j in range(1, n):
        for z in range(4):
            brick_copy(j, z).wait_send()


def build_first_block(w1, b1_ref):
    rows, cols = 288, 192
    m = iota((rows, 1), 0)
    zh, yh, channel = lax.div(m, 48), lax.rem(lax.div(m, 8), 6), m & 7
    by_row = dot(onehot(channel == iota((rows, 8), 1)), w1).astype(BF16)
    k = iota((1, cols), 1)
    pair, dx, part = lax.div(k, 48), lax.rem(lax.div(k, 16), 3), k & 15
    z, y = pair * 2 + (part >> 3), part & 7
    total = jnp.zeros((rows, cols), F32)
    for dz in range(3):
        for dy in range(3):
            pick = onehot(iota((27, cols), 0) == 9 * dz + 3 * dy + dx)
            total = total + jnp.where((z == zh + dz) & (y == yh + dy), dot(by_row, pick), 0.0)
    bias = jnp.zeros((rows, 1), F32)
    for o in range(8):
        bias = jnp.where(channel == o, b1_ref[o], bias)
    high = bias.astype(BF16).astype(F32)
    middle = (bias - high).astype(BF16).astype(F32)
    low = bias - high - middle
    c = iota((1, 16), 1)
    extra = jnp.where(c == 0, high, jnp.where(c == 1, middle, jnp.where(c == 2, low, 0.0)))
    off = (
        ((c == 3) & (zh == 0)) | ((c == 4) & (zh == 5)) | ((c == 5) & (yh == 0))
        | ((c == 6) & (yh == 5)) | (c == 7)
    )
    extra = jnp.where(off, OFF, extra)
    return total.astype(BF16), extra.astype(BF16)


def build_second_block(w2):
    rows, cols = 96, 288
    m = iota((rows, 1), 0)
    dx, o, z, y = lax.div(m, 32), (m >> 4) & 1, (m >> 2) & 3, m & 3
    k = iota((1, cols), 1)
    zh, yh, channel = lax.div(k, 48), lax.rem(lax.div(k, 8), 6), k & 7
    pick = onehot((iota((16, cols), 0) & 7) == channel)
    same = o == (iota((1, 16), 1) >> 3)
    total = jnp.zeros((rows, cols), F32)
    for dz in range(3):
        for dy in range(3):
            select = onehot(iota((rows, 27), 1) == 9 * dz + 3 * dy + dx)
            values = lax.dot_general(
                select, w2, (((1,), (1,)), ((), ())), preferred_element_type=F32
            )
            values = dot(jnp.where(same, values, 0.0).astype(BF16), pick)
            total = total + jnp.where((zh == z + dz) & (yh == y + dy), values, 0.0)
    return total.astype(BF16)


def build_codes(owners_ref, capacity):
    target = [owners_ref[b] for b in range(16)]
    r, lane = iota((8, 128), 0), iota((8, 128), 1)
    brick = 2 * ((r & 1) * 4 + (lane >> 5)) + (r >> 1)
    codes = jnp.full((8, 128), -1, jnp.int32)
    for b in range(16):
        rank = jnp.int32(0)
        for other in range(b):
            rank = rank + jnp.where(target[other] == target[b], 1, 0)
        codes = jnp.where(brick == b, target[b] * capacity + rank, codes)
    return codes


def column_kernel(
    n,
    density, w1_hbm, b1_hbm, w2_hbm, b2_hbm, owners_hbm, solutes, biomass,
    frac, state_new,
    w1_ref, b1_ref, w2_ref, b2_ref, owners_ref, tiles, yedge_out, xedge_out, codes_out,
    yedge_in, xedge_in, corner_in, codes_in, win, first, second, order, values_ref,
    state, mass_in, mass,
    tile_send, tile_recv, code_send, code_recv, y_send, y_recv, x_send, x_recv, c_send, c_recv,
    local_sem, ready,
):
    me, gy, col = lax.axis_index("gz"), lax.axis_index("gy"), lax.axis_index("col")
    small = [
        pltpu.make_async_copy(source, target, local_sem.at[3 + i])
        for i, (source, target) in enumerate(
            (
                (w1_hbm, w1_ref), (w2_hbm, w2_ref), (b1_hbm, b1_ref), (b2_hbm, b2_ref),
                (owners_hbm, owners_ref),
            )
        )
    ]
    own = pltpu.make_async_copy(density, tiles.at[me], local_sem.at[0])
    own.start()
    for copy in small:
        copy.start()
    barrier = pltpu.get_barrier_semaphore()

    across = ({"gy": 1 - gy}, {"col": 1 - col}, {"gy": 1 - gy, "col": 1 - col})
    for where in across:
        pl.semaphore_signal(barrier, inc=1, device_id=where, device_id_type=MESH)
    for k in range(1, n):

        @pl.when(me < k)
        def _():
            for where in ({},) + across:
                pl.semaphore_signal(barrier, inc=1, device_id={"gz": k, **where}, device_id_type=MESH)

    load_state = pltpu.make_async_copy(solutes, state, local_sem.at[1])
    load_mass = pltpu.make_async_copy(biomass, mass_in, local_sem.at[2])

    def tile_copy(k):
        return pltpu.make_async_remote_copy(
            src_ref=density, dst_ref=tiles.at[me], send_sem=tile_send.at[k], recv_sem=tile_recv.at[me],
            device_id={"gz": k}, device_id_type=MESH,
        )

    def code_copy(k):
        return pltpu.make_async_remote_copy(
            src_ref=codes_out, dst_ref=codes_in.at[me], send_sem=code_send.at[k],
            recv_sem=code_recv.at[me], device_id={"gz": k}, device_id_type=MESH,
        )

    def edge_copy(k, source, target, send, recv, across):
        return pltpu.make_async_remote_copy(
            src_ref=source, dst_ref=target.at[me], send_sem=send.at[k], recv_sem=recv.at[me],
            device_id={"gz": k, **across}, device_id_type=MESH,
        )

    def edge_copies(k):
        return (
            edge_copy(k, xedge_out, xedge_in, x_send, x_recv, {"col": 1 - col}),
            edge_copy(k, yedge_out, yedge_in, y_send, y_recv, {"gy": 1 - gy}),
            edge_copy(k, yedge_out, corner_in, c_send, c_recv, {"gy": 1 - gy, "col": 1 - col}),
        )

    def arrival(source, target, send, recv):
        return pltpu.make_async_remote_copy(
            src_ref=source, dst_ref=target, send_sem=send, recv_sem=recv,
            device_id={"col": 1 - col}, device_id_type=MESH,
        )

    pl.semaphore_wait(barrier, 4 * me + 3)
    for k in range(n - 1):

        @pl.when(k < me)
        def _():
            tile_copy(k).start()
            for where in ({},) + across:
                pl.semaphore_signal(ready.at[me], inc=1, device_id={"gz": k, **where}, device_id_type=MESH)

    row8 = iota((8, 1), 0)
    lane = iota((1, BX), 1)

    own.wait()
    packed = jnp.zeros((8, 256), F32)
    for z in range(4):
        top = tiles[me, z, 0:16, :].astype(F32)[0:8]
        bottom = tiles[me, z, 16:32, :].astype(F32)[8:16]
        pair = jnp.where(gy == 0, pltpu.roll(bottom, 2, 0), top)
        packed = jnp.where((row8 >> 1) == z, pltpu.roll(pair, 2 * z, 0) if z else pair, packed)
    yedge_out[...] = jnp.concatenate([packed[:, :128], packed[:, 128:]], axis=0).astype(BF16)
    packed = jnp.zeros((8, BX), F32)
    place = ((lane + jnp.where(col == 0, 2, 0)) & (BX - 1)) >> 1
    for z in range(4):
        whole = tiles[me, z].astype(F32)
        side = jnp.where(col == 0, whole[:, 128:], whole[:, :128])
        for i in range(4):
            p = z * 4 + i
            block = side[i * 8 : i * 8 + 8]
            packed = jnp.where(place == p, pltpu.roll(block, 2 * p, 1) if p else block, packed)
    xedge_out[...] = jnp.concatenate([packed, packed], axis=0).astype(BF16)
    for k in range(n):

        @pl.when(k <= me)
        def _():
            for copy in edge_copies(k):
                copy.start()

    for copy in small:
        copy.wait()
    codes_out[...] = build_codes(owners_ref, 8)
    codes_in[me] = codes_out[...]
    for k in range(n - 1):

        @pl.when(k < me)
        def _():
            code_copy(k).start()

    load_state.start()
    load_mass.start()

    banded, extra = build_first_block(w1_ref[...], b1_ref)
    first[:, 0:192] = banded
    first[:, 192:208] = extra
    second[...] = build_second_block(w2_ref[...])
    i = iota((256, 1), 0)
    j = iota((1, 256), 1)
    wanted = (lax.rem(i, 32) >> 2) * 32 + (i >> 5) * 4 + (i & 3)
    order[...] = onehot(wanted == j)
    win[0:48, :] = jnp.zeros_like(win[0:48, :])
    win[(2 * n + 1) * 48 : (2 * n + 2) * 48, :] = jnp.zeros_like(win[0:48, :])
    load_mass.wait()
    for g in range(n):
        mass[g] = mass_in[g].astype(F32)
    group = ((lane + 8) & (BX - 1)) >> 4
    natural = ((lane < 2) & (col == 0)) | ((lane >= BX - 2) & (col == 1))

    def assemble(s):
        @pl.when(s != me)
        def _():
            arrival(density, tiles.at[s], tile_send.at[0], tile_recv.at[s]).wait_recv()
            arrival(codes_out, codes_in.at[s], code_send.at[0], code_recv.at[s]).wait_recv()

        arrival(xedge_out, xedge_in.at[s], x_send.at[0], x_recv.at[s]).wait_recv()
        arrival(yedge_out, yedge_in.at[s], y_send.at[0], y_recv.at[s]).wait_recv()
        arrival(yedge_out, corner_in.at[s], c_send.at[0], c_recv.at[s]).wait_recv()
        xe = xedge_in[s].astype(F32)[0:8]
        ye = yedge_in[s].astype(F32)
        ce = corner_in[s].astype(F32)
        ce = jnp.where(natural, jnp.where(col == 0, ce[0:8], ce[8:16]), jnp.where(col == 0, ye[8:16], ye[0:8]))
        ye = jnp.concatenate([ye[0:8], ye[8:16], ce], axis=1)
        start = pl.multiple_of(s * 96 + 48, 16)
        for zp in range(2):
            windows = []
            for z in (2 * zp, 2 * zp + 1):
                whole = tiles[s, z].astype(F32)
                side = jnp.where(col == 0, whole[:, 128:], whole[:, :128])
                blocks = []
                for i in range(4):
                    p = z * 4 + i
                    edge = pltpu.roll(xe, BX - 2 * p, 1) if p else xe
                    edge = jnp.where(natural, edge, side[i * 8 : i * 8 + 8])
                    blocks.append(jnp.concatenate([whole[i * 8 : i * 8 + 8], edge], axis=1))
                above = jnp.where(gy == 1, pltpu.roll(ye, 8 - 2 * z, 0) if z else ye, 0.0)
                below = jnp.where(gy == 0, pltpu.roll(ye, 6 - 2 * z, 0) if z != 3 else ye, 0.0)
                down = [above] + [pltpu.roll(b, 2, 0) for b in blocks]
                up = [pltpu.roll(b, 6, 0) for b in blocks] + [below]
                held = []
                for i in range(4):
                    held.append(jnp.where(row8 < 2, down[i], down[i + 1]))
                    held.append(jnp.where(row8 < 6, up[i], up[i + 1]))
                windows.append(held)
            strip = None
            for rb in range(8):
                both = jnp.concatenate([windows[0][rb], windows[1][rb]], axis=0)
                w0, w1, ws = both[:, :BX], both[:, BX : 2 * BX], both[:, 2 * BX :]
                r0, r1, rs = pltpu.roll(w0, 1, 1), pltpu.roll(w1, 1, 1), pltpu.roll(ws, 1, 1)
                l0, l1, ls = (pltpu.roll(w, BX - 1, 1) for w in (w0, w1, ws))
                left = jnp.concatenate(
                    [jnp.where(lane == 0, jnp.where(col == 1, rs, 0.0), r0), jnp.where(lane == 0, r0, r1)], axis=1
                )
                right = jnp.concatenate(
                    [jnp.where(lane == BX - 1, l1, l0), jnp.where(lane == BX - 1, jnp.where(col == 0, ls, 0.0), l1)],
                    axis=1,
                )
                for dx, v in enumerate((left, both[:, : 2 * BX], right)):
                    win[pl.ds(start + zp * 48 + dx * 16, 16), rb * 256 : (rb + 1) * 256] = v.astype(BF16)
                strip = ws if rb == 0 else jnp.where(group == rb, pltpu.roll(ws, 16 * rb, 1), strip)
            for dx, v in enumerate((pltpu.roll(strip, 1, 1), strip, pltpu.roll(strip, BX - 1, 1))):
                win[pl.ds(start + zp * 48 + dx * 16, 16), EDGE : EDGE + BX] = v.astype(BF16)

    row16 = iota((16, 1), 0)
    bias2 = jnp.where((iota((32, 1), 0) >> 4) == 0, b2_ref[0], b2_ref[1])

    def process(s):
        code = codes_in[s]
        base = (row16 < 3) | ((row16 == 3) & (s == 0)) | ((row16 == 4) & (s == n - 1))
        start = pl.multiple_of(s * 96, 16)
        at_first, at_last = (row16 == 5) & (gy == 0), (row16 == 6) & (gy == 1)

        def hidden_part(chunk):
            flags = []
            for rb in range(chunk * RBS, (chunk + 1) * RBS):
                flag = base
                if rb == 0:
                    flag = flag | at_first
                if rb == 7:
                    flag = flag | at_last
                flags.append(jnp.broadcast_to(onehot(flag), (16, 256)))
            data = win[pl.ds(start, 192), chunk * RBS * 256 : (chunk + 1) * RBS * 256]
            if chunk == 0:
                flags.append(onehot(base | (at_first & (group == 0)) | (at_last & (group == 7))))
                data = jnp.concatenate([data, win[pl.ds(start, 192), EDGE : EDGE + BX]], axis=1)
            operand = jnp.concatenate([data, jnp.concatenate(flags, axis=1)], axis=0)
            return jnp.maximum(dot(first[...], operand), 0.0).astype(BF16)

        edge = None
        held = hidden_part(0)
        for chunk in range(8 // RBS):
            later = hidden_part(chunk + 1) if chunk + 1 < 8 // RBS else None
            total = dot(second[...], held)
            held = later
            if chunk == 0:
                t = total[:, RBS * 256 :]
                edge = jnp.where(col == 1, pltpu.roll(t[0:32], 1, 1), pltpu.roll(t[64:96], BX - 1, 1))
            for r in range(RBS):
                rb = chunk * RBS + r
                t = total[:, r * 256 : (r + 1) * 256]
                beside = pltpu.roll(edge, BX - 16 * rb, 1) if rb else edge
                a0, a1 = pltpu.roll(t[0:32, :BX], 1, 1), pltpu.roll(t[0:32, BX:], 1, 1)
                c0, c1 = pltpu.roll(t[64:96, :BX], BX - 1, 1), pltpu.roll(t[64:96, BX:], BX - 1, 1)
                v0 = jnp.where(lane == 0, jnp.where(col == 1, beside, 0.0), a0) + t[32:64, :BX]
                v0 = v0 + jnp.where(lane == BX - 1, c1, c0)
                v1 = jnp.where(lane == 0, a0, a1) + t[32:64, BX:]
                v1 = v1 + jnp.where(lane == BX - 1, jnp.where(col == 0, beside, 0.0), c1)
                for cb, value in enumerate((v0, v1)):
                    value = 1.0 / (1.0 + jnp.exp(-(value + bias2)))
                    values_ref[rb * 32 : (rb + 1) * 32, cb * BX : (cb + 1) * BX] = value.astype(BF16)

        @pl.when(s == me)
        def _():
            frac[...] = dot(order[...], values_ref[...]).astype(BF16).reshape(frac.shape)

        placed = jnp.zeros((256, BX), F32)
        for cb in range(2):
            slot = jnp.concatenate([code[2 * cb : 2 * cb + 1], code[2 * cb + 1 : 2 * cb + 2]], axis=1)
            slot = slot - me * 8
            target = jnp.where((slot >= 0) & (slot < 8), (j & 31) * 8 + slot, -1)
            placing = onehot(i == target)
            placed = placed + dot(placing, values_ref[:, cb * BX : (cb + 1) * BX])
        pore = [placed[q * 8 : q * 8 + 8] for q in range(16)]
        organic = [placed[128 + q * 8 : 136 + q * 8] for q in range(16)]
        carbon = [state[s, pl.ds(q, 8, stride=32), :] for q in range(16)]
        oxygen = [state[s, pl.ds(16 + q, 8, stride=32), :] for q in range(16)]
        held = [mass[s, pl.ds(q, 8, stride=16), :] for q in range(16)]
        carbon, oxygen = diffuse(carbon, oxygen, pore, organic, held, iota((8, BX), 1))
        for q in range(16):
            state_new[s, pl.ds(q, 8, stride=32), :] = carbon[q]
            state_new[s, pl.ds(16 + q, 8, stride=32), :] = oxygen[q]

    for k in range(1, n):

        @pl.when(me < k)
        def _():
            pl.semaphore_wait(ready.at[k], 4)
            tile_copy(k).start()
            code_copy(k).start()
            for copy in edge_copies(k):
                copy.start()

    def source(step):
        return jnp.where(me < n // 2, step, n - 1 - step)

    assemble(source(0))
    load_state.wait()

    @pl.loop(0, n)
    def _(step):
        @pl.when(step < n - 1)
        def _():
            assemble(source(step + 1))

        process(source(step))

    for k in range(n):

        @pl.when(k != me)
        def _():
            tile_copy(k).wait_send()
            code_copy(k).wait_send()

        for copy in edge_copies(k):
            copy.wait_send()


def column_call(n, groups, density, operands):
    anywhere = pl.BlockSpec(memory_space=pltpu.HBM)
    inside = pl.BlockSpec(memory_space=pltpu.VMEM)
    remote = [pltpu.SemaphoreType.DMA((n,))] * 10
    return pl.pallas_call(
        functools.partial(column_kernel, n),
        out_shape=(
            pltpu.VMEM((2,) + density.shape, BF16),
            pltpu.VMEM((groups, 256, BX), F32),
        ),
        in_specs=[anywhere] * 8,
        out_specs=(inside, inside),
        scratch_shapes=[
            pltpu.VMEM((8, 27), BF16),
            pltpu.SMEM((8,), F32),
            pltpu.VMEM((16, 27), BF16),
            pltpu.SMEM((2,), F32),
            pltpu.SMEM((16,), jnp.int32),
            pltpu.VMEM((n,) + density.shape, BF16),
            pltpu.VMEM((16, BX), BF16),
            pltpu.VMEM((16, BX), BF16),
            pltpu.VMEM((8, BX), jnp.int32),
            pltpu.VMEM((n, 16, BX), BF16),
            pltpu.VMEM((n, 16, BX), BF16),
            pltpu.VMEM((n, 16, BX), BF16),
            pltpu.VMEM((n, 8, BX), jnp.int32),
            pltpu.VMEM(((2 * n + 2) * 48, EDGE + BX), BF16),
            pltpu.VMEM((288, 208), BF16),
            pltpu.VMEM((96, 288), BF16),
            pltpu.VMEM((256, 256), BF16),
            pltpu.VMEM((256, 256), BF16),
            pltpu.VMEM((groups, 256, BX), F32),
            pltpu.VMEM((groups, 128, BX), BF16),
            pltpu.VMEM((groups, 128, BX), F32),
        ] + remote + [pltpu.SemaphoreType.DMA((8,)), pltpu.SemaphoreType.REGULAR((n,))],
        compiler_params=pltpu.CompilerParams(
            collective_id=1, has_side_effects=True,
            vmem_limit_bytes=(65344 - 128 - groups * 128) * 1024,
        ),
    )(*operands)


def exchange_call(sizes, capacity, groups, density, operands):
    n, slots, per = sizes[0], groups * 8, 8 * capacity
    anywhere = pl.BlockSpec(memory_space=pltpu.HBM)
    inside = pl.BlockSpec(memory_space=pltpu.VMEM)
    return pl.pallas_call(
        functools.partial(kernel, sizes, capacity),
        out_shape=(
            pltpu.VMEM((2,) + density.shape, BF16),
            pltpu.VMEM((groups, 256, BX), F32),
        ),
        in_specs=[anywhere] * 8,
        out_specs=(inside, inside),
        scratch_shapes=[
            pltpu.VMEM((8, 27), BF16),
            pltpu.SMEM((8,), F32),
            pltpu.VMEM((16, 27), BF16),
            pltpu.SMEM((2,), F32),
            pltpu.SMEM((16,), jnp.int32),
            pltpu.VMEM((8, 64, 512), BF16),
            pltpu.VMEM((272, 9 * KR), BF16),
            pltpu.VMEM((3, 192, 272), BF16),
            pltpu.VMEM((8 * 3 * KR, LANES), BF16),
            pltpu.VMEM((6, 272, LANES), BF16),
            pltpu.VMEM((n, 4, per, BX), BF16),
            pltpu.VMEM((n, 4, per, BX), BF16),
            pltpu.VMEM((groups, 256, BX), F32),
            pltpu.VMEM((groups, 128, BX), BF16),
            pltpu.VMEM((groups, 128, BX), F32),
            pltpu.VMEM((32, slots if capacity != 8 else 8, BX), F32),
            pltpu.SemaphoreType.DMA((26,)),
            pltpu.SemaphoreType.DMA((26,)),
            pltpu.SemaphoreType.DMA((n, 4)),
            pltpu.SemaphoreType.DMA((n, 4)),
            pltpu.SemaphoreType.DMA((9,)),
            pltpu.SemaphoreType.DMA((groups,)),
        ],
        compiler_params=pltpu.CompilerParams(
            collective_id=0, has_side_effects=True, vmem_limit_bytes=(65344 - 128 - groups * 128) * 1024
        ),
    )(*operands)


def write_out(frac, state, fractions, solutes_next, sem):
    copies = [
        pltpu.make_async_copy(frac, fractions, sem.at[0]),
        pltpu.make_async_copy(state, solutes_next, sem.at[1]),
    ]
    for copy in copies:
        copy.start()
    for copy in copies:
        copy.wait()


def per_device(
    sizes, density, first_kernel, first_bias, second_kernel, second_bias, owners, solutes, biomass
):
    n = sizes[0]
    slots = solutes.shape[3]
    capacity = slots // n
    anywhere = pl.BlockSpec(memory_space=pltpu.HBM)
    groups = slots // 8
    inside = pl.BlockSpec(memory_space=pltpu.VMEM)
    operands = (
        density,
        first_kernel.transpose(2, 1, 0).reshape(8, 27),
        first_bias,
        second_kernel.transpose(1, 2, 0).reshape(16, 27),
        second_bias,
        owners.reshape(-1),
        solutes.reshape(groups, 256, BX),
        biomass.reshape(groups, 128, BX),
    )
    if sizes == (4, 2, 2) and capacity == 8:
        frac, state_new = column_call(n, groups, density, operands)
    else:
        frac, state_new = exchange_call(sizes, capacity, groups, density, operands)
    fractions, solutes_next = pl.pallas_call(
        write_out,
        out_shape=(
            jax.ShapeDtypeStruct((2,) + density.shape, BF16),
            jax.ShapeDtypeStruct((groups, 256, BX), F32),
        ),
        in_specs=[inside, inside],
        out_specs=(anywhere, anywhere),
        scratch_shapes=[pltpu.SemaphoreType.DMA((2,))],
        compiler_params=pltpu.CompilerParams(vmem_limit_bytes=16 * 1024 * 1024),
    )(frac, state_new)
    return fractions, solutes_next.reshape(solutes.shape)


def solution(mesh):
    sizes = tuple(mesh.shape[axis] for axis in ("gz", "gy", "col"))
    return jax.shard_map(
        functools.partial(per_device, sizes),
        mesh=mesh,
        in_specs=(
            P(("cores", "gz"), "gy", "col"),
            P(),
            P(),
            P(),
            P(),
            P(("cores", "gz"), "gy", "col", None, None),
            P(("cores", "gz"), "gy", "col", None, None, None, None, None),
            P(("cores", "gz"), "gy", "col", None, None, None, None),
        ),
        out_specs=(
            P(None, ("cores", "gz"), "gy", "col"),
            P(("cores", "gz"), "gy", "col", None, None, None, None, None),
        ),
        check_vma=False,
    )
```

```python
import functools
import itertools

import jax
import jax.numpy as jnp
from jax import lax
from jax.experimental import pallas as pl
from jax.experimental.pallas import tpu as pltpu
from jax.sharding import PartitionSpec as P

BY = 4
BX = 128
STEPS = 4
MESH = pl.DeviceIdType.MESH
F32 = jnp.float32
BF16 = jnp.bfloat16
AROUND = [d for d in itertools.product((-1, 0, 1), repeat=3) if d != (0, 0, 0)]
PLACE_Z = {0: (0, 4), 1: (4, 2), -1: (6, 2)}
PLACE_Y = {0: (0, 32), 1: (32, 16), -1: (48, 16)}
PLACE_X = {0: (0, 256), 1: (256, 128), -1: (384, 128)}
TAKE_Z = {0: (0, 4), 1: (0, 2), -1: (2, 2)}
TAKE_Y = {0: (0, 32), 1: (0, 16), -1: (16, 16)}
TAKE_X = {0: (0, 256), 1: (0, 128), -1: (128, 128)}
KR = 48
HR = 34
LANES = 384
OFF = -1e30


def region(ref, tables, offset):
    return ref.at[tuple(pl.ds(*table[o]) for table, o in zip(tables, offset))]


def iota(shape, dim):
    return lax.broadcasted_iota(jnp.int32, shape, dim)


def onehot(condition):
    return jnp.where(condition, 1.0, 0.0).astype(BF16)


def dot(a, b):
    return jnp.dot(a, b, preferred_element_type=F32)


def build_first(w1):
    hidden = w1.shape[0]
    rows, cols = hidden * HR, 9 * KR
    i = iota((rows, 1), 0)
    channel, yi = lax.div(i, HR), lax.rem(i, HR)
    expand = onehot(channel == iota((rows, hidden), 1))
    by_row = dot(expand, w1).astype(BF16)
    j = iota((1, cols), 1)
    tap, r = lax.div(j, KR), lax.rem(j, KR)
    y = jnp.where(r < 40, r, r - KR)
    tap_offset = lax.div(tap, 3) * 9 + lax.rem(tap, 3)
    total = jnp.zeros((rows, cols), F32)
    for dy in range(3):
        pick = onehot(iota((27, cols), 0) == tap_offset + 3 * dy)
        total = total + jnp.where(y == yi + (dy - 2), dot(by_row, pick), 0.0)
    return total.astype(BF16)


def build_second(w2, first_row, last_row):
    hidden = w2.shape[0] // 2
    rows, cols = 192, hidden * HR
    i = iota((rows, 1), 0)
    group, y = lax.div(i, 32), lax.rem(i, 32)
    j = iota((1, cols), 1)
    yi = lax.rem(j, HR)
    inside = jnp.logical_not(((yi == 0) & first_row) | ((yi == HR - 1) & last_row))
    yi = jnp.where(inside, yi, -100)
    pick = onehot(lax.rem(iota((2 * hidden, cols), 0), hidden) == lax.div(j, HR))
    same = lax.rem(group, 2) == lax.div(iota((1, 2 * hidden), 1), hidden)
    blocks = []
    for dz in range(3):
        total = jnp.zeros((rows, cols), F32)
        for dy in range(3):
            select = onehot(iota((rows, 27), 1) == 9 * dz + 3 * dy + lax.div(group, 2))
            values = lax.dot_general(
                select, w2, (((1,), (1,)), ((), ())), preferred_element_type=F32
            )
            values = dot(jnp.where(same, values, 0.0).astype(BF16), pick)
            total = total + jnp.where(yi == y + dy, values, 0.0)
        blocks.append(total.astype(BF16))
    return blocks


def build_placing(owners_ref, slots, capacity):
    count = owners_ref.shape[0]
    target = [owners_ref[b] for b in range(count)]
    j = iota((1, 128), 1)
    brick = ((j & 31) >> 2) * 2 + (j >> 6)
    slot = jnp.zeros((1, 128), jnp.int32)
    for b in range(count):
        rank = jnp.int32(0)
        for other in range(b):
            rank = rank + jnp.where(target[other] == target[b], 1, 0)
        slot = jnp.where(brick == b, target[b] * capacity + rank, slot)
    column = slot * 8 + ((j >> 5) & 1) * 4 + (j & 3)
    i = iota((slots * 8, 1), 0)
    owner = lax.div(i, capacity * 8)
    row = (owner * capacity + lax.rem(i, capacity)) * 8 + lax.rem(lax.div(i, capacity), 8)
    return onehot(row == column)


def diffuse(carbon, oxygen, pore, organic, mass, lane):
    low, high = lane == 0, lane == BX - 1
    pore_c = [0.12 * v for v in pore]
    pore_o = [0.16 * v for v in pore]
    gain = [0.3 * v for v in organic]
    mass = [0.25 * v for v in mass]

    def laplace(field, q):
        z, y = q // 4, q % 4
        v = field[q]
        total = jnp.where(low, v, pltpu.roll(v, 1, 1)) + jnp.where(high, v, pltpu.roll(v, BX - 1, 1))
        near = 2
        for ok, at in ((z > 0, q - 4), (z < 3, q + 4), (y > 0, q - 1), (y < 3, q + 1)):
            if ok:
                total = total + field[at]
                near += 1
        return total - float(near) * v

    for _ in range(STEPS):
        carbon_new, oxygen_new = [], []
        for q in range(16):
            c, o = carbon[q], oxygen[q]
            uptake = mass[q] * c * o / ((0.5 + jnp.abs(c)) * (0.3 + jnp.abs(o)))
            carbon_new.append(c + pore_c[q] * laplace(carbon, q) + gain[q] - uptake)
            oxygen_new.append(o + pore_o[q] * laplace(oxygen, q) - uptake)
        carbon, oxygen = carbon_new, oxygen_new
    return carbon, oxygen


def kernel(
    sizes, capacity,
    density, w1_hbm, b1_hbm, w2_hbm, b2_hbm, owners_hbm, solutes, biomass,
    frac, state_new,
    w1_ref, b1_ref, w2_ref, b2_ref, owners_ref, tile, first, second, shifted, hidden, out, arrived, state, mass_in, mass, gathered,
    halo_send, halo_recv, brick_send, brick_recv, local_sem, group_sem,
):
    n, n_gy, n_col = sizes
    slots = n * capacity
    here = (lax.axis_index("gz"), lax.axis_index("gy"), lax.axis_index("col"))
    me = here[0]

    def exists(offset):
        ok = None
        for position, size, o in zip(here, sizes, offset):
            test = None if o == 0 else (position + o >= 0) & (position + o < size)
            ok = test if ok is None else ok if test is None else ok & test
        return ok

    def device(offset):
        return {"gz": here[0] + offset[0], "gy": here[1] + offset[1], "col": here[2] + offset[2]}

    def halo(offset, index, receiver):
        seen = tuple(-o for o in offset) if not receiver else offset
        return pltpu.make_async_remote_copy(
            src_ref=region(density, (TAKE_Z, TAKE_Y, TAKE_X), seen),
            dst_ref=region(tile, (PLACE_Z, PLACE_Y, PLACE_X), seen),
            send_sem=halo_send.at[index],
            recv_sem=halo_recv.at[AROUND.index(seen)],
            device_id=device(offset),
            device_id_type=MESH,
        )

    small = [
        pltpu.make_async_copy(source, target, local_sem.at[4 + i])
        for i, (source, target) in enumerate(
            (
                (w1_hbm, w1_ref), (w2_hbm, w2_ref), (b1_hbm, b1_ref), (b2_hbm, b2_ref),
                (owners_hbm, owners_ref),
            )
        )
    ]
    for copy in small:
        copy.start()
    tile[...] = jnp.zeros_like(tile)
    barrier = pltpu.get_barrier_semaphore()
    expected = jnp.int32(n - 1)
    for offset in AROUND:
        ok = exists(offset)
        expected = expected + jnp.where(ok, 1, 0)

        @pl.when(ok)
        def _():
            pl.semaphore_signal(barrier, inc=1, device_id=device(offset), device_id_type=MESH)

    for j in range(1, n):
        pl.semaphore_signal(
            barrier, inc=1, device_id={"gz": lax.rem(me + j, n)}, device_id_type=MESH
        )
    own = pltpu.make_async_copy(
        density, region(tile, (PLACE_Z, PLACE_Y, PLACE_X), (0, 0, 0)), local_sem.at[0]
    )
    own.start()
    load_state = pltpu.make_async_copy(solutes, state, local_sem.at[1])
    load_mass = pltpu.make_async_copy(biomass, mass_in, local_sem.at[2])
    pl.semaphore_wait(barrier, expected)

    for index, offset in enumerate(AROUND):

        @pl.when(exists(offset))
        def _():
            halo(offset, index, False).start()

    load_state.start()
    load_mass.start()

    for copy in small:
        copy.wait()
    first[...] = build_first(w1_ref[...])
    for dz, block in enumerate(build_second(w2_ref[...], here[1] == 0, here[1] == n_gy - 1)):
        second[dz] = block
    placing = build_placing(owners_ref, slots, capacity)
    channel = lax.div(iota((272, 1), 0), HR)
    bias1 = jnp.zeros((272, 1), F32)
    for o in range(8):
        bias1 = jnp.where(channel == o, b1_ref[o], bias1)
    bias2 = jnp.where(iota((64, 1), 0) < 32, b2_ref[0], b2_ref[1])
    lane = iota((1, BX), 1)
    keep = jnp.where(
        ((lane == 0) & (here[2] < n_col - 1)) | ((lane == BX - 1) & (here[2] > 0)), 1.0, 0.0
    )
    load_mass.wait()
    for g in range(slots // 8):
        mass[g] = mass_in[g].astype(F32)

    own.wait()
    for index, offset in enumerate(AROUND):

        @pl.when(exists(offset))
        def _():
            halo(offset, index, True).wait_recv()

    half_row = iota((16, 512), 0) < 8
    half_lane = iota((KR, BX), 1) < 64
    for zz in range(8):
        z = (zz + 6) % 8
        side = jnp.where(half_row, tile[z, 32:48, :].astype(F32), tile[z, 48:64, :].astype(F32))
        whole = jnp.concatenate([tile[z, 0:32, :].astype(F32), side], axis=0)
        edge = jnp.where(half_lane, whole[:, 256:384], whole[:, 384:512])
        whole = jnp.concatenate([whole[:, :256], edge], axis=1)
        base = zz * 3 * KR
        shifted[base : base + KR, :] = pltpu.roll(whole, 1, 1).astype(BF16)
        shifted[base + KR : base + 2 * KR, :] = whole.astype(BF16)
        shifted[base + 2 * KR : base + 3 * KR, :] = pltpu.roll(whole, LANES - 1, 1).astype(BF16)

    def hidden_slice(zi):
        value = dot(first[...], shifted[zi * 3 * KR : (zi + 3) * 3 * KR, :])
        value = jnp.maximum(value + bias1, 0.0)
        hidden[zi, :, 0:256] = value[:, :256].astype(BF16)
        hidden[zi, :, 256:384] = (value[:, 256:] * keep).astype(BF16)

    def brick_copy(j, z):
        to = lax.rem(me + j, n)
        return pltpu.make_async_remote_copy(
            src_ref=out.at[to, z],
            dst_ref=arrived.at[me, z],
            send_sem=brick_send.at[j, z],
            recv_sem=brick_recv.at[j, z],
            device_id={"gz": to},
            device_id_type=MESH,
        )

    hidden_slice(0)

    @pl.when(me == 0)
    def _():
        hidden[0] = jnp.zeros_like(hidden[0])

    hidden_slice(1)
    per = 8 * capacity
    for z in range(4):
        hidden_slice(z + 2)
        if z == 3:

            @pl.when(me == n - 1)
            def _():
                hidden[5] = jnp.zeros_like(hidden[5])

        total = jnp.zeros((192, LANES), F32)
        for dz in range(3):
            total = total + dot(second[dz], hidden[z + dz])
        value = (
            pltpu.roll(total[0:64], 1, 1) + total[64:128] + pltpu.roll(total[128:192], LANES - 1, 1)
        )[:, :256]
        value = (1.0 / (1.0 + jnp.exp(-(value + bias2)))).astype(BF16)
        frac[0, z] = value[:32]
        frac[1, z] = value[32:]
        placed = dot(placing, jnp.concatenate([value[:, :128], value[:, 128:]], axis=0)).astype(BF16)
        for d in range(n):
            out[d, z] = placed[d * per : (d + 1) * per]
        for j in range(1, n):
            brick_copy(j, z).start()

    load_state.wait()

    def received(j, z):
        source = lax.rem(me - j + n, n)
        pltpu.make_async_remote_copy(
            src_ref=out.at[source, z],
            dst_ref=arrived.at[source, z],
            send_sem=brick_send.at[j, z],
            recv_sem=brick_recv.at[j, z],
            device_id={"gz": source},
            device_id_type=MESH,
        ).wait_recv()


    def group(g, pore, organic):
        carbon = [state[g, pl.ds(q, 8, stride=32), :] for q in range(16)]
        oxygen = [state[g, pl.ds(16 + q, 8, stride=32), :] for q in range(16)]
        held = [mass[g, pl.ds(q, 8, stride=16), :] for q in range(16)]
        carbon, oxygen = diffuse(carbon, oxygen, pore, organic, held, iota((8, BX), 1))
        for q in range(16):
            state_new[g, pl.ds(q, 8, stride=32), :] = carbon[q]
            state_new[g, pl.ds(16 + q, 8, stride=32), :] = oxygen[q]

    if capacity == 8:
        for j in range(n):
            source = lax.rem(me - j + n, n)
            values = [[None] * 16, [None] * 16]
            for z in range(4):
                if j:
                    received(j, z)
                ref = arrived if j else out
                for o in range(2):
                    for pair in range(2):
                        at = o * 32 + pair * 16
                        both = ref[source, z, at : at + 16, :].astype(F32)
                        values[o][z * 4 + pair * 2] = both[:8]
                        values[o][z * 4 + pair * 2 + 1] = both[8:]
            group(source, *values)
    else:
        for z in range(4):
            arrived[me, z] = out[me, z]
        for j in range(1, n):
            for z in range(4):
                received(j, z)
        for s in range(n):
            for z in range(4):
                block = arrived[s, z].astype(F32)
                for o in range(2):
                    for y in range(4):
                        at = (o * 4 + y) * capacity
                        gathered[o * 16 + z * 4 + y, s * capacity : (s + 1) * capacity, :] = block[
                            at : at + capacity
                        ]

        @pl.loop(0, slots // 8)
        def _(g):
            start = pl.multiple_of(g * 8, 8)
            group(
                g,
                [gathered[q, pl.ds(start, 8), :] for q in range(16)],
                [gathered[16 + q, pl.ds(start, 8), :] for q in range(16)],
            )

    for index, offset in enumerate(AROUND):

        @pl.when(exists(offset))
        def _():
            halo(offset, index, False).wait_send()

    for j in range(1, n):
        for z in range(4):
            brick_copy(j, z).wait_send()


def build_first_block(w1, b1_ref):
    rows, cols = 288, 192
    m = iota((rows, 1), 0)
    zh, yh, channel = lax.div(m, 48), lax.rem(lax.div(m, 8), 6), m & 7
    by_row = dot(onehot(channel == iota((rows, 8), 1)), w1).astype(BF16)
    k = iota((1, cols), 1)
    pair, dx, part = lax.div(k, 48), lax.rem(lax.div(k, 16), 3), k & 15
    z, y = pair * 2 + (part >> 3), part & 7
    total = jnp.zeros((rows, cols), F32)
    for dz in range(3):
        for dy in range(3):
            pick = onehot(iota((27, cols), 0) == 9 * dz + 3 * dy + dx)
            total = total + jnp.where((z == zh + dz) & (y == yh + dy), dot(by_row, pick), 0.0)
    bias = jnp.zeros((rows, 1), F32)
    for o in range(8):
        bias = jnp.where(channel == o, b1_ref[o], bias)
    high = bias.astype(BF16).astype(F32)
    middle = (bias - high).astype(BF16).astype(F32)
    low = bias - high - middle
    c = iota((1, 16), 1)
    extra = jnp.where(c == 0, high, jnp.where(c == 1, middle, jnp.where(c == 2, low, 0.0)))
    off = (
        ((c == 3) & (zh == 0)) | ((c == 4) & (zh == 5)) | ((c == 5) & (yh == 0))
        | ((c == 6) & (yh == 5)) | (c == 7)
    )
    extra = jnp.where(off, OFF, extra)
    return total.astype(BF16), extra.astype(BF16)


def build_second_block(w2):
    rows, cols = 96, 288
    m = iota((rows, 1), 0)
    dx, o, z, y = lax.div(m, 32), (m >> 4) & 1, (m >> 2) & 3, m & 3
    k = iota((1, cols), 1)
    zh, yh, channel = lax.div(k, 48), lax.rem(lax.div(k, 8), 6), k & 7
    pick = onehot((iota((16, cols), 0) & 7) == channel)
    same = o == (iota((1, 16), 1) >> 3)
    total = jnp.zeros((rows, cols), F32)
    for dz in range(3):
        for dy in range(3):
            select = onehot(iota((rows, 27), 1) == 9 * dz + 3 * dy + dx)
            values = lax.dot_general(
                select, w2, (((1,), (1,)), ((), ())), preferred_element_type=F32
            )
            values = dot(jnp.where(same, values, 0.0).astype(BF16), pick)
            total = total + jnp.where((zh == z + dz) & (yh == y + dy), values, 0.0)
    return total.astype(BF16)


def build_codes(owners_ref, capacity):
    target = [owners_ref[b] for b in range(16)]
    lane = iota((1, 128), 1)
    bricks = jnp.full((1, 128), -1, jnp.int32)
    for b in range(16):
        rank = jnp.int32(0)
        for other in range(b):
            rank = rank + jnp.where(target[other] == target[b], 1, 0)
        bricks = jnp.where(lane == target[b] * capacity + rank, (b % 2) * 8 + b // 2, bricks)
    return bricks


def column_kernel(
    n,
    density, w1_hbm, b1_hbm, w2_hbm, b2_hbm, owners_hbm, solutes, biomass,
    frac, state_new,
    w1_ref, b1_ref, w2_ref, b2_ref, owners_ref, tiles, yedge_out, xedge_out, codes_out,
    yedge_in, xedge_in, corner_in, codes_in, win, first, second, order, values_ref,
    state, mass_in, mass,
    tile_send, tile_recv, code_send, code_recv, y_send, y_recv, x_send, x_recv, c_send, c_recv,
    local_sem, ready, beside, strips, beside_ref, placed_ref, slots_ref, slots_sem,
):
    me, gy, col = lax.axis_index("gz"), lax.axis_index("gy"), lax.axis_index("col")
    small = [
        pltpu.make_async_copy(source, target, local_sem.at[3 + i])
        for i, (source, target) in enumerate(
            (
                (w1_hbm, w1_ref), (w2_hbm, w2_ref), (b1_hbm, b1_ref), (b2_hbm, b2_ref),
                (owners_hbm, owners_ref),
            )
        )
    ]
    own = pltpu.make_async_copy(density, tiles.at[me], local_sem.at[0])
    own.start()
    for copy in small:
        copy.start()
    barrier = pltpu.get_barrier_semaphore()

    across = ({"gy": 1 - gy}, {"col": 1 - col}, {"gy": 1 - gy, "col": 1 - col})
    @pl.when(me == 0)
    def _():
        for where in across:
            pl.semaphore_signal(barrier, inc=1, device_id=where, device_id_type=MESH)

    for k in range(1, n):

        @pl.when(me < k)
        def _():
            for where in ({},) + across:
                pl.semaphore_signal(barrier, inc=1, device_id={"gz": k, **where}, device_id_type=MESH)

    load_state = pltpu.make_async_copy(solutes, state, local_sem.at[1])
    load_mass = pltpu.make_async_copy(biomass, mass_in, local_sem.at[2])

    def tile_copy(k):
        return pltpu.make_async_remote_copy(
            src_ref=density, dst_ref=tiles.at[me], send_sem=tile_send.at[k], recv_sem=tile_recv.at[me],
            device_id={"gz": k}, device_id_type=MESH,
        )

    def code_copy(k):
        return pltpu.make_async_remote_copy(
            src_ref=codes_out, dst_ref=codes_in.at[me], send_sem=code_send.at[k],
            recv_sem=code_recv.at[me], device_id={"gz": k}, device_id_type=MESH,
        )

    def edge_copy(k, source, target, send, recv, across):
        return pltpu.make_async_remote_copy(
            src_ref=source, dst_ref=target.at[me], send_sem=send.at[k], recv_sem=recv.at[me],
            device_id={"gz": k, **across}, device_id_type=MESH,
        )

    def edge_copies(k):
        return (
            edge_copy(k, xedge_out, xedge_in, x_send, x_recv, {"col": 1 - col}),
            edge_copy(k, yedge_out, yedge_in, y_send, y_recv, {"gy": 1 - gy}),
            edge_copy(k, yedge_out, corner_in, c_send, c_recv, {"gy": 1 - gy, "col": 1 - col}),
        )

    def arrival(source, target, send, recv):
        return pltpu.make_async_remote_copy(
            src_ref=source, dst_ref=target, send_sem=send, recv_sem=recv,
            device_id={"col": 1 - col}, device_id_type=MESH,
        )

    pl.semaphore_wait(barrier, jnp.where(me == 0, 3, 4 * me))
    for k in range(n - 1):

        @pl.when(k < me)
        def _():
            if k == 0:
                tile_copy(k).start()
            for where in ({},) + across:
                pl.semaphore_signal(ready.at[me], inc=1, device_id={"gz": k, **where}, device_id_type=MESH)

    row8 = iota((8, 1), 0)
    lane = iota((1, BX), 1)

    own.wait()
    packed = jnp.zeros((8, 256), F32)
    for z in range(4):
        top = tiles[me, z, 0:16, :].astype(F32)[0:8]
        bottom = tiles[me, z, 16:32, :].astype(F32)[8:16]
        pair = jnp.where(gy == 0, pltpu.roll(bottom, 2, 0), top)
        packed = jnp.where((row8 >> 1) == z, pltpu.roll(pair, 2 * z, 0) if z else pair, packed)
    yedge_out[...] = jnp.concatenate([packed[:, :128], packed[:, 128:]], axis=0).astype(BF16)
    packed = jnp.zeros((8, BX), F32)
    place = ((lane + jnp.where(col == 0, 2, 0)) & (BX - 1)) >> 1
    for z in range(4):
        whole = tiles[me, z].astype(F32)
        side = jnp.where(col == 0, whole[:, 128:], whole[:, :128])
        for i in range(4):
            p = z * 4 + i
            block = side[i * 8 : i * 8 + 8]
            packed = jnp.where(place == p, pltpu.roll(block, 2 * p, 1) if p else block, packed)
    xedge_out[...] = jnp.concatenate([packed, packed], axis=0).astype(BF16)
    for k in range(n):

        @pl.when((k < me) | (me + k == 0))
        def _():
            for copy in edge_copies(k):
                copy.start()

    for copy in small:
        copy.wait()
    codes_out[...] = build_codes(owners_ref, 8)
    codes_in[me] = codes_out[...]
    for k in range(n - 1):

        @pl.when(k < me)
        def _():
            code_copy(k).start()

    load_state.start()
    load_mass.start()

    banded, extra = build_first_block(w1_ref[...], b1_ref)
    first[:, 0:192] = banded
    first[:, 192:208] = extra

    @pl.when(me < n - 1)
    def _():
        pl.semaphore_wait(ready.at[me + 1], 4)
        pl.semaphore_signal(beside, inc=1, device_id={"gz": me + 1}, device_id_type=MESH)
        tile_copy(me + 1).start()
        code_copy(me + 1).start()
        for copy in edge_copies(me + 1):
            copy.start()

    second[...] = build_second_block(w2_ref[...])
    i = iota((256, 1), 0)
    j = iota((1, 256), 1)
    wanted = (lax.rem(i, 32) >> 2) * 32 + (i >> 5) * 4 + (i & 3)
    order[...] = onehot(wanted == j)
    for first_row in (0, (2 * n + 1) * 48):
        win[:, first_row : first_row + 48, :] = jnp.zeros((16, 48, BX), BF16)
        strips[first_row : first_row + 48, :] = jnp.zeros((48, BX), BF16)
    load_mass.wait()
    for g in range(n):
        mass[g] = mass_in[g].astype(F32)
    group = ((lane + 8) & (BX - 1)) >> 4
    natural = ((lane < 2) & (col == 0)) | ((lane >= BX - 2) & (col == 1))

    def slots_copy(s):
        return pltpu.make_async_copy(codes_in.at[s], slots_ref.at[s], slots_sem.at[s])

    def assemble(s):
        @pl.when(s != me)
        def _():
            arrival(density, tiles.at[s], tile_send.at[0], tile_recv.at[s]).wait_recv()
            arrival(codes_out, codes_in.at[s], code_send.at[0], code_recv.at[s]).wait_recv()

        slots_copy(s).start()
        arrival(xedge_out, xedge_in.at[s], x_send.at[0], x_recv.at[s]).wait_recv()
        arrival(yedge_out, yedge_in.at[s], y_send.at[0], y_recv.at[s]).wait_recv()
        arrival(yedge_out, corner_in.at[s], c_send.at[0], c_recv.at[s]).wait_recv()
        xe = xedge_in[s].astype(F32)[0:8]
        ye = yedge_in[s].astype(F32)
        ce = corner_in[s].astype(F32)
        ce = jnp.where(natural, jnp.where(col == 0, ce[0:8], ce[8:16]), jnp.where(col == 0, ye[8:16], ye[0:8]))
        inner = pltpu.roll(jnp.where(lane < 64, ye[8:16], ye[0:8]), 4, 1)
        ce = jnp.where((lane >= 2) & (lane < 6), inner, ce)
        ye = jnp.concatenate([ye[0:8], ye[8:16], ce], axis=1)
        start = pl.multiple_of(s * 96 + 48, 16)
        for zp in range(2):
            windows = []
            for z in (2 * zp, 2 * zp + 1):
                whole = tiles[s, z].astype(F32)
                side = jnp.where(col == 0, whole[:, 128:], whole[:, :128])
                inner = pltpu.roll(jnp.where(lane < 64, whole[:, 128:], whole[:, :128]), 4, 1)
                blocks = []
                for i in range(4):
                    p = z * 4 + i
                    edge = pltpu.roll(xe, BX - 2 * p, 1) if p else xe
                    edge = jnp.where(natural, edge, side[i * 8 : i * 8 + 8])
                    edge = jnp.where((lane >= 2) & (lane < 6), inner[i * 8 : i * 8 + 8], edge)
                    blocks.append(jnp.concatenate([whole[i * 8 : i * 8 + 8], edge], axis=1))
                above = jnp.where(gy == 1, pltpu.roll(ye, 8 - 2 * z, 0) if z else ye, 0.0)
                below = jnp.where(gy == 0, pltpu.roll(ye, 6 - 2 * z, 0) if z != 3 else ye, 0.0)
                down = [above] + [pltpu.roll(b, 2, 0) for b in blocks]
                up = [pltpu.roll(b, 6, 0) for b in blocks] + [below]
                held = []
                for i in range(4):
                    held.append(jnp.where(row8 < 2, down[i], down[i + 1]))
                    held.append(jnp.where(row8 < 6, up[i], up[i + 1]))
                windows.append(held)
            strip = None
            for rb in range(8):
                both = jnp.concatenate([windows[0][rb], windows[1][rb]], axis=0)
                w0, w1, ws = both[:, :BX], both[:, BX : 2 * BX], both[:, 2 * BX :]
                r0, r1, rs = pltpu.roll(w0, 1, 1), pltpu.roll(w1, 1, 1), pltpu.roll(ws, 1, 1)
                l0, l1, ls = (pltpu.roll(w, BX - 1, 1) for w in (w0, w1, ws))
                left = jnp.concatenate(
                    [jnp.where(lane == 0, jnp.where(col == 1, rs, 0.0), r0), jnp.where(lane == 0, r0, r1)], axis=1
                )
                right = jnp.concatenate(
                    [jnp.where(lane == BX - 1, l1, l0), jnp.where(lane == BX - 1, jnp.where(col == 0, ls, 0.0), l1)],
                    axis=1,
                )
                for dx, v in enumerate((left, both[:, : 2 * BX], right)):
                    win[rb, pl.ds(start + zp * 48 + dx * 16, 16), :] = v[:, :BX].astype(BF16)
                    win[8 + rb, pl.ds(start + zp * 48 + dx * 16, 16), :] = v[:, BX:].astype(BF16)
                strip = ws if rb == 0 else jnp.where(group == rb, pltpu.roll(ws, 16 * rb, 1), strip)
            for dx, v in enumerate((pltpu.roll(strip, 1, 1), strip, pltpu.roll(strip, BX - 1, 1))):
                strips[pl.ds(start + zp * 48 + dx * 16, 16), :] = v.astype(BF16)

    row16 = iota((16, 1), 0)
    bias2 = jnp.where((iota((32, 1), 0) >> 4) == 0, b2_ref[0], b2_ref[1])

    def convolve(s, bricks, put):
        base = (row16 < 3) | ((row16 == 3) & (s == 0)) | ((row16 == 4) & (s == n - 1))
        start = pl.multiple_of(s * 96, 16)
        at_first, at_last = (row16 == 5) & (gy == 0), (row16 == 6) & (gy == 1)
        chunks = [bricks[i : i + 4] for i in range(0, len(bricks), 4)]

        def hidden_part(chunk):
            data, flags = [], []
            for b in chunks[chunk]:
                flag = base | (at_first & ((b == 0) | (b == 8))) | (at_last & ((b == 7) | (b == 15)))
                flags.append(jnp.broadcast_to(onehot(flag), (16, BX)))
                data.append(win[b, pl.ds(start, 192), :])
            if chunk == 0:
                flags.append(onehot(base | (at_first & (group == 0)) | (at_last & (group == 7))))
                data.append(strips[pl.ds(start, 192), :])
            operand = jnp.concatenate(
                [jnp.concatenate(data, axis=1), jnp.concatenate(flags, axis=1)], axis=0
            )
            return jnp.maximum(dot(first[...], operand), 0.0).astype(BF16)

        held = hidden_part(0)
        for chunk in range(len(chunks)):
            later = hidden_part(chunk + 1) if chunk + 1 < len(chunks) else None
            total = dot(second[...], held)
            held = later
            if chunk == 0:
                t = total[:, 4 * BX :]
                for b in range(16):
                    rb, cb = b % 8, b // 8
                    before = pltpu.roll(t[0:32], (BX + 1 - 4 * cb - 16 * rb) % BX, 1)
                    after = pltpu.roll(t[64:96], (BX - 1 - 4 * (1 - cb) - 16 * rb) % BX, 1)
                    at_left = (lane == 0) if cb else (lane == 0) & (col == 1)
                    at_right = (lane == BX - 1) & (col == 0) if cb else lane == BX - 1
                    beside_ref[b] = jnp.where(at_left, before, jnp.where(at_right, after, 0.0))
            for r, b in enumerate(chunks[chunk]):
                t = total[:, r * BX : (r + 1) * BX]
                value = jnp.where(lane == 0, 0.0, pltpu.roll(t[0:32], 1, 1)) + t[32:64]
                value = value + jnp.where(lane == BX - 1, 0.0, pltpu.roll(t[64:96], BX - 1, 1))
                value = value + beside_ref[b]
                value = (1.0 / (1.0 + jnp.exp(-(value + bias2)))).astype(BF16)
                put(chunk * 4 + r, value)

    def process(s):
        held = [slots_ref[s, 0, me * 8 + k] for k in range(8)]
        bricks = [jnp.maximum(b, 0) for b in held]
        kept = [jnp.where(b >= 0, 1.0, 0.0) for b in held]

        def put_slot(k, value):
            placed_ref[pl.ds(k, 32, stride=8), :] = value.astype(F32) * kept[k]

        @pl.when(s != me)
        def _():
            convolve(s, bricks, put_slot)

        @pl.when(s == me)
        def _():
            def put_own(b, value):
                values_ref[b] = value

            convolve(s, list(range(16)), put_own)
            both = [values_ref[8 * cb : 8 * cb + 8].reshape(256, BX) for cb in range(2)]
            whole = dot(order[...], jnp.concatenate(both, axis=1))
            frac[...] = whole.astype(BF16).reshape(frac.shape)
            for k in range(8):
                put_slot(k, values_ref[bricks[k]])

        placed = placed_ref[...]
        pore = [placed[q * 8 : q * 8 + 8] for q in range(16)]
        organic = [placed[128 + q * 8 : 136 + q * 8] for q in range(16)]
        carbon = [state[s, pl.ds(q, 8, stride=32), :] for q in range(16)]
        oxygen = [state[s, pl.ds(16 + q, 8, stride=32), :] for q in range(16)]
        weight = [mass[s, pl.ds(q, 8, stride=16), :] for q in range(16)]
        carbon, oxygen = diffuse(carbon, oxygen, pore, organic, weight, iota((8, BX), 1))
        for q in range(16):
            state_new[s, pl.ds(q, 8, stride=32), :] = carbon[q]
            state_new[s, pl.ds(16 + q, 8, stride=32), :] = oxygen[q]

    for k in range(1, n - 1):

        @pl.when(k < me)
        def _():
            tile_copy(k).start()

    @pl.when(me > 0)
    def _():
        pl.semaphore_wait(beside, 1)
        for copy in edge_copies(me):
            copy.start()

    for k in range(2, n):

        @pl.when(me < k - 1)
        def _():
            pl.semaphore_wait(ready.at[k], 4)
            tile_copy(k).start()
            code_copy(k).start()
            for copy in edge_copies(k):
                copy.start()

    def source(step):
        return jnp.where(me < n // 2, step, n - 1 - step)

    assemble(source(0))
    load_state.wait()

    @pl.loop(0, n)
    def _(step):
        @pl.when(step < n - 1)
        def _():
            assemble(source(step + 1))

        slots_copy(source(step)).wait()
        process(source(step))

    for k in range(n):

        @pl.when(k != me)
        def _():
            tile_copy(k).wait_send()
            code_copy(k).wait_send()

        for copy in edge_copies(k):
            copy.wait_send()


def column_call(n, groups, density, operands):
    anywhere = pl.BlockSpec(memory_space=pltpu.HBM)
    inside = pl.BlockSpec(memory_space=pltpu.VMEM)
    remote = [pltpu.SemaphoreType.DMA((n,))] * 10
    return pl.pallas_call(
        functools.partial(column_kernel, n),
        out_shape=(
            pltpu.VMEM((2,) + density.shape, BF16),
            pltpu.VMEM((groups, 256, BX), F32),
        ),
        in_specs=[anywhere] * 8,
        out_specs=(inside, inside),
        scratch_shapes=[
            pltpu.VMEM((8, 27), BF16),
            pltpu.SMEM((8,), F32),
            pltpu.VMEM((16, 27), BF16),
            pltpu.SMEM((2,), F32),
            pltpu.SMEM((16,), jnp.int32),
            pltpu.VMEM((n,) + density.shape, BF16),
            pltpu.VMEM((16, BX), BF16),
            pltpu.VMEM((16, BX), BF16),
            pltpu.VMEM((1, BX), jnp.int32),
            pltpu.VMEM((n, 16, BX), BF16),
            pltpu.VMEM((n, 16, BX), BF16),
            pltpu.VMEM((n, 16, BX), BF16),
            pltpu.VMEM((n, 1, BX), jnp.int32),
            pltpu.VMEM((16, (2 * n + 2) * 48, BX), BF16),
            pltpu.VMEM((288, 208), BF16),
            pltpu.VMEM((96, 288), BF16),
            pltpu.VMEM((256, 256), BF16),
            pltpu.VMEM((16, 32, BX), BF16),
            pltpu.VMEM((groups, 256, BX), F32),
            pltpu.VMEM((groups, 128, BX), BF16),
            pltpu.VMEM((groups, 128, BX), F32),
        ] + remote + [pltpu.SemaphoreType.DMA((8,)), pltpu.SemaphoreType.REGULAR((n,)), pltpu.SemaphoreType.REGULAR,
            pltpu.VMEM(((2 * n + 2) * 48, BX), BF16),
            pltpu.VMEM((16, 32, BX), F32),
            pltpu.VMEM((256, BX), F32),
            pltpu.SMEM((n, 1, BX), jnp.int32),
            pltpu.SemaphoreType.DMA((n,)),
        ],
        compiler_params=pltpu.CompilerParams(
            collective_id=1, has_side_effects=True,
            vmem_limit_bytes=(65344 - 128 - groups * 128) * 1024,
        ),
    )(*operands)


def exchange_call(sizes, capacity, groups, density, operands):
    n, slots, per = sizes[0], groups * 8, 8 * capacity
    anywhere = pl.BlockSpec(memory_space=pltpu.HBM)
    inside = pl.BlockSpec(memory_space=pltpu.VMEM)
    return pl.pallas_call(
        functools.partial(kernel, sizes, capacity),
        out_shape=(
            pltpu.VMEM((2,) + density.shape, BF16),
            pltpu.VMEM((groups, 256, BX), F32),
        ),
        in_specs=[anywhere] * 8,
        out_specs=(inside, inside),
        scratch_shapes=[
            pltpu.VMEM((8, 27), BF16),
            pltpu.SMEM((8,), F32),
            pltpu.VMEM((16, 27), BF16),
            pltpu.SMEM((2,), F32),
            pltpu.SMEM((16,), jnp.int32),
            pltpu.VMEM((8, 64, 512), BF16),
            pltpu.VMEM((272, 9 * KR), BF16),
            pltpu.VMEM((3, 192, 272), BF16),
            pltpu.VMEM((8 * 3 * KR, LANES), BF16),
            pltpu.VMEM((6, 272, LANES), BF16),
            pltpu.VMEM((n, 4, per, BX), BF16),
            pltpu.VMEM((n, 4, per, BX), BF16),
            pltpu.VMEM((groups, 256, BX), F32),
            pltpu.VMEM((groups, 128, BX), BF16),
            pltpu.VMEM((groups, 128, BX), F32),
            pltpu.VMEM((32, slots if capacity != 8 else 8, BX), F32),
            pltpu.SemaphoreType.DMA((26,)),
            pltpu.SemaphoreType.DMA((26,)),
            pltpu.SemaphoreType.DMA((n, 4)),
            pltpu.SemaphoreType.DMA((n, 4)),
            pltpu.SemaphoreType.DMA((9,)),
            pltpu.SemaphoreType.DMA((groups,)),
        ],
        compiler_params=pltpu.CompilerParams(
            collective_id=0, has_side_effects=True, vmem_limit_bytes=(65344 - 128 - groups * 128) * 1024
        ),
    )(*operands)


def write_out(frac, state, fractions, solutes_next, sem):
    copies = [
        pltpu.make_async_copy(frac, fractions, sem.at[0]),
        pltpu.make_async_copy(state, solutes_next, sem.at[1]),
    ]
    for copy in copies:
        copy.start()
    for copy in copies:
        copy.wait()


def per_device(
    sizes, density, first_kernel, first_bias, second_kernel, second_bias, owners, solutes, biomass
):
    n = sizes[0]
    slots = solutes.shape[3]
    capacity = slots // n
    anywhere = pl.BlockSpec(memory_space=pltpu.HBM)
    groups = slots // 8
    inside = pl.BlockSpec(memory_space=pltpu.VMEM)
    operands = (
        density,
        first_kernel.transpose(2, 1, 0).reshape(8, 27),
        first_bias,
        second_kernel.transpose(1, 2, 0).reshape(16, 27),
        second_bias,
        owners.reshape(-1),
        solutes.reshape(groups, 256, BX),
        biomass.reshape(groups, 128, BX),
    )
    if sizes == (4, 2, 2) and capacity == 8:
        frac, state_new = column_call(n, groups, density, operands)
    else:
        frac, state_new = exchange_call(sizes, capacity, groups, density, operands)
    fractions, solutes_next = pl.pallas_call(
        write_out,
        out_shape=(
            jax.ShapeDtypeStruct((2,) + density.shape, BF16),
            jax.ShapeDtypeStruct((groups, 256, BX), F32),
        ),
        in_specs=[inside, inside],
        out_specs=(anywhere, anywhere),
        scratch_shapes=[pltpu.SemaphoreType.DMA((2,))],
        compiler_params=pltpu.CompilerParams(vmem_limit_bytes=16 * 1024 * 1024),
    )(frac, state_new)
    return fractions, solutes_next.reshape(solutes.shape)


def solution(mesh):
    sizes = tuple(mesh.shape[axis] for axis in ("gz", "gy", "col"))
    return jax.shard_map(
        functools.partial(per_device, sizes),
        mesh=mesh,
        in_specs=(
            P(("cores", "gz"), "gy", "col"),
            P(),
            P(),
            P(),
            P(),
            P(("cores", "gz"), "gy", "col", None, None),
            P(("cores", "gz"), "gy", "col", None, None, None, None, None),
            P(("cores", "gz"), "gy", "col", None, None, None, None),
        ),
        out_specs=(
            P(None, ("cores", "gz"), "gy", "col"),
            P(("cores", "gz"), "gy", "col", None, None, None, None, None),
        ),
        check_vma=False,
    )
```

```python
import functools
import itertools

import jax
import jax.numpy as jnp
from jax import lax
from jax.experimental import pallas as pl
from jax.experimental.pallas import tpu as pltpu
from jax.sharding import PartitionSpec as P

BY = 4
BX = 128
STEPS = 4
MESH = pl.DeviceIdType.MESH
F32 = jnp.float32
BF16 = jnp.bfloat16
AROUND = [d for d in itertools.product((-1, 0, 1), repeat=3) if d != (0, 0, 0)]
PLACE_Z = {0: (0, 4), 1: (4, 2), -1: (6, 2)}
PLACE_Y = {0: (0, 32), 1: (32, 16), -1: (48, 16)}
PLACE_X = {0: (0, 256), 1: (256, 128), -1: (384, 128)}
TAKE_Z = {0: (0, 4), 1: (0, 2), -1: (2, 2)}
TAKE_Y = {0: (0, 32), 1: (0, 16), -1: (16, 16)}
TAKE_X = {0: (0, 256), 1: (0, 128), -1: (128, 128)}
KR = 48
HR = 34
LANES = 384
CHUNK = 4
OFF = -1e30


def region(ref, tables, offset):
    return ref.at[tuple(pl.ds(*table[o]) for table, o in zip(tables, offset))]


def iota(shape, dim):
    return lax.broadcasted_iota(jnp.int32, shape, dim)


def onehot(condition):
    return jnp.where(condition, 1.0, 0.0).astype(BF16)


def dot(a, b):
    return jnp.dot(a, b, preferred_element_type=F32)


def build_first(w1):
    hidden = w1.shape[0]
    rows, cols = hidden * HR, 9 * KR
    i = iota((rows, 1), 0)
    channel, yi = lax.div(i, HR), lax.rem(i, HR)
    expand = onehot(channel == iota((rows, hidden), 1))
    by_row = dot(expand, w1).astype(BF16)
    j = iota((1, cols), 1)
    tap, r = lax.div(j, KR), lax.rem(j, KR)
    y = jnp.where(r < 40, r, r - KR)
    tap_offset = lax.div(tap, 3) * 9 + lax.rem(tap, 3)
    total = jnp.zeros((rows, cols), F32)
    for dy in range(3):
        pick = onehot(iota((27, cols), 0) == tap_offset + 3 * dy)
        total = total + jnp.where(y == yi + (dy - 2), dot(by_row, pick), 0.0)
    return total.astype(BF16)


def build_second(w2, first_row, last_row):
    hidden = w2.shape[0] // 2
    rows, cols = 192, hidden * HR
    i = iota((rows, 1), 0)
    group, y = lax.div(i, 32), lax.rem(i, 32)
    j = iota((1, cols), 1)
    yi = lax.rem(j, HR)
    inside = jnp.logical_not(((yi == 0) & first_row) | ((yi == HR - 1) & last_row))
    yi = jnp.where(inside, yi, -100)
    pick = onehot(lax.rem(iota((2 * hidden, cols), 0), hidden) == lax.div(j, HR))
    same = lax.rem(group, 2) == lax.div(iota((1, 2 * hidden), 1), hidden)
    blocks = []
    for dz in range(3):
        total = jnp.zeros((rows, cols), F32)
        for dy in range(3):
            select = onehot(iota((rows, 27), 1) == 9 * dz + 3 * dy + lax.div(group, 2))
            values = lax.dot_general(
                select, w2, (((1,), (1,)), ((), ())), preferred_element_type=F32
            )
            values = dot(jnp.where(same, values, 0.0).astype(BF16), pick)
            total = total + jnp.where(yi == y + dy, values, 0.0)
        blocks.append(total.astype(BF16))
    return blocks


def build_placing(owners_ref, slots, capacity):
    count = owners_ref.shape[0]
    target = [owners_ref[b] for b in range(count)]
    j = iota((1, 128), 1)
    brick = ((j & 31) >> 2) * 2 + (j >> 6)
    slot = jnp.zeros((1, 128), jnp.int32)
    for b in range(count):
        rank = jnp.int32(0)
        for other in range(b):
            rank = rank + jnp.where(target[other] == target[b], 1, 0)
        slot = jnp.where(brick == b, target[b] * capacity + rank, slot)
    column = slot * 8 + ((j >> 5) & 1) * 4 + (j & 3)
    i = iota((slots * 8, 1), 0)
    owner = lax.div(i, capacity * 8)
    row = (owner * capacity + lax.rem(i, capacity)) * 8 + lax.rem(lax.div(i, capacity), 8)
    return onehot(row == column)


def diffuse_steps(carbon, oxygen, pore, organic, mass, lane):
    low, high = lane == 0, lane == BX - 1
    pore_c = [0.12 * v for v in pore]
    pore_o = [0.16 * v for v in pore]
    gain = [0.3 * v for v in organic]
    mass = [0.25 * v for v in mass]

    def laplace(field, q):
        z, y = q // 4, q % 4
        v = field[q]
        total = jnp.where(low, v, pltpu.roll(v, 1, 1)) + jnp.where(high, v, pltpu.roll(v, BX - 1, 1))
        near = 2
        for ok, at in ((z > 0, q - 4), (z < 3, q + 4), (y > 0, q - 1), (y < 3, q + 1)):
            if ok:
                total = total + field[at]
                near += 1
        return total - float(near) * v

    for _ in range(STEPS):
        carbon_new, oxygen_new = [], []
        for q in range(16):
            c, o = carbon[q], oxygen[q]
            uptake = mass[q] * c * o / ((0.5 + jnp.abs(c)) * (0.3 + jnp.abs(o)))
            carbon_new.append(c + pore_c[q] * laplace(carbon, q) + gain[q] - uptake)
            oxygen_new.append(o + pore_o[q] * laplace(oxygen, q) - uptake)
        carbon, oxygen = carbon_new, oxygen_new
        yield carbon, oxygen


def diffuse(*fields):
    *_, last = diffuse_steps(*fields)
    return last


def kernel(
    sizes, capacity,
    density, w1_hbm, b1_hbm, w2_hbm, b2_hbm, owners_hbm, solutes, biomass,
    frac, state_new,
    w1_ref, b1_ref, w2_ref, b2_ref, owners_ref, tile, first, second, shifted, hidden, out, arrived, state, mass_in, mass, gathered,
    halo_send, halo_recv, brick_send, brick_recv, local_sem, group_sem,
):
    n, n_gy, n_col = sizes
    slots = n * capacity
    here = (lax.axis_index("gz"), lax.axis_index("gy"), lax.axis_index("col"))
    me = here[0]

    def exists(offset):
        ok = None
        for position, size, o in zip(here, sizes, offset):
            test = None if o == 0 else (position + o >= 0) & (position + o < size)
            ok = test if ok is None else ok if test is None else ok & test
        return ok

    def device(offset):
        return {"gz": here[0] + offset[0], "gy": here[1] + offset[1], "col": here[2] + offset[2]}

    def halo(offset, index, receiver):
        seen = tuple(-o for o in offset) if not receiver else offset
        return pltpu.make_async_remote_copy(
            src_ref=region(density, (TAKE_Z, TAKE_Y, TAKE_X), seen),
            dst_ref=region(tile, (PLACE_Z, PLACE_Y, PLACE_X), seen),
            send_sem=halo_send.at[index],
            recv_sem=halo_recv.at[AROUND.index(seen)],
            device_id=device(offset),
            device_id_type=MESH,
        )

    small = [
        pltpu.make_async_copy(source, target, local_sem.at[4 + i])
        for i, (source, target) in enumerate(
            (
                (w1_hbm, w1_ref), (w2_hbm, w2_ref), (b1_hbm, b1_ref), (b2_hbm, b2_ref),
                (owners_hbm, owners_ref),
            )
        )
    ]
    for copy in small:
        copy.start()
    tile[...] = jnp.zeros_like(tile)
    barrier = pltpu.get_barrier_semaphore()
    expected = jnp.int32(n - 1)
    for offset in AROUND:
        ok = exists(offset)
        expected = expected + jnp.where(ok, 1, 0)

        @pl.when(ok)
        def _():
            pl.semaphore_signal(barrier, inc=1, device_id=device(offset), device_id_type=MESH)

    for j in range(1, n):
        pl.semaphore_signal(
            barrier, inc=1, device_id={"gz": lax.rem(me + j, n)}, device_id_type=MESH
        )
    own = pltpu.make_async_copy(
        density, region(tile, (PLACE_Z, PLACE_Y, PLACE_X), (0, 0, 0)), local_sem.at[0]
    )
    own.start()
    load_state = pltpu.make_async_copy(solutes, state, local_sem.at[1])
    load_mass = pltpu.make_async_copy(biomass, mass_in, local_sem.at[2])
    pl.semaphore_wait(barrier, expected)

    for index, offset in enumerate(AROUND):

        @pl.when(exists(offset))
        def _():
            halo(offset, index, False).start()

    load_state.start()
    load_mass.start()

    for copy in small:
        copy.wait()
    first[...] = build_first(w1_ref[...])
    for dz, block in enumerate(build_second(w2_ref[...], here[1] == 0, here[1] == n_gy - 1)):
        second[dz] = block
    placing = build_placing(owners_ref, slots, capacity)
    channel = lax.div(iota((272, 1), 0), HR)
    bias1 = jnp.zeros((272, 1), F32)
    for o in range(8):
        bias1 = jnp.where(channel == o, b1_ref[o], bias1)
    bias2 = jnp.where(iota((64, 1), 0) < 32, b2_ref[0], b2_ref[1])
    lane = iota((1, BX), 1)
    keep = jnp.where(
        ((lane == 0) & (here[2] < n_col - 1)) | ((lane == BX - 1) & (here[2] > 0)), 1.0, 0.0
    )
    load_mass.wait()
    for g in range(slots // 8):
        mass[g] = mass_in[g].astype(F32)

    own.wait()
    for index, offset in enumerate(AROUND):

        @pl.when(exists(offset))
        def _():
            halo(offset, index, True).wait_recv()

    half_row = iota((16, 512), 0) < 8
    half_lane = iota((KR, BX), 1) < 64
    for zz in range(8):
        z = (zz + 6) % 8
        side = jnp.where(half_row, tile[z, 32:48, :].astype(F32), tile[z, 48:64, :].astype(F32))
        whole = jnp.concatenate([tile[z, 0:32, :].astype(F32), side], axis=0)
        edge = jnp.where(half_lane, whole[:, 256:384], whole[:, 384:512])
        whole = jnp.concatenate([whole[:, :256], edge], axis=1)
        base = zz * 3 * KR
        shifted[base : base + KR, :] = pltpu.roll(whole, 1, 1).astype(BF16)
        shifted[base + KR : base + 2 * KR, :] = whole.astype(BF16)
        shifted[base + 2 * KR : base + 3 * KR, :] = pltpu.roll(whole, LANES - 1, 1).astype(BF16)

    def hidden_slice(zi):
        value = dot(first[...], shifted[zi * 3 * KR : (zi + 3) * 3 * KR, :])
        value = jnp.maximum(value + bias1, 0.0)
        hidden[zi, :, 0:256] = value[:, :256].astype(BF16)
        hidden[zi, :, 256:384] = (value[:, 256:] * keep).astype(BF16)

    def brick_copy(j, z):
        to = lax.rem(me + j, n)
        return pltpu.make_async_remote_copy(
            src_ref=out.at[to, z],
            dst_ref=arrived.at[me, z],
            send_sem=brick_send.at[j, z],
            recv_sem=brick_recv.at[j, z],
            device_id={"gz": to},
            device_id_type=MESH,
        )

    hidden_slice(0)

    @pl.when(me == 0)
    def _():
        hidden[0] = jnp.zeros_like(hidden[0])

    hidden_slice(1)
    per = 8 * capacity
    for z in range(4):
        hidden_slice(z + 2)
        if z == 3:

            @pl.when(me == n - 1)
            def _():
                hidden[5] = jnp.zeros_like(hidden[5])

        total = jnp.zeros((192, LANES), F32)
        for dz in range(3):
            total = total + dot(second[dz], hidden[z + dz])
        value = (
            pltpu.roll(total[0:64], 1, 1) + total[64:128] + pltpu.roll(total[128:192], LANES - 1, 1)
        )[:, :256]
        value = (1.0 / (1.0 + jnp.exp(-(value + bias2)))).astype(BF16)
        frac[0, z] = value[:32]
        frac[1, z] = value[32:]
        placed = dot(placing, jnp.concatenate([value[:, :128], value[:, 128:]], axis=0)).astype(BF16)
        for d in range(n):
            out[d, z] = placed[d * per : (d + 1) * per]
        for j in range(1, n):
            brick_copy(j, z).start()

    load_state.wait()

    def received(j, z):
        source = lax.rem(me - j + n, n)
        pltpu.make_async_remote_copy(
            src_ref=out.at[source, z],
            dst_ref=arrived.at[source, z],
            send_sem=brick_send.at[j, z],
            recv_sem=brick_recv.at[j, z],
            device_id={"gz": source},
            device_id_type=MESH,
        ).wait_recv()


    def group(g, pore, organic):
        carbon = [state[g, pl.ds(q, 8, stride=32), :] for q in range(16)]
        oxygen = [state[g, pl.ds(16 + q, 8, stride=32), :] for q in range(16)]
        held = [mass[g, pl.ds(q, 8, stride=16), :] for q in range(16)]
        carbon, oxygen = diffuse(carbon, oxygen, pore, organic, held, iota((8, BX), 1))
        for q in range(16):
            state_new[g, pl.ds(q, 8, stride=32), :] = carbon[q]
            state_new[g, pl.ds(16 + q, 8, stride=32), :] = oxygen[q]

    if capacity == 8:
        for j in range(n):
            source = lax.rem(me - j + n, n)
            values = [[None] * 16, [None] * 16]
            for z in range(4):
                if j:
                    received(j, z)
                ref = arrived if j else out
                for o in range(2):
                    for pair in range(2):
                        at = o * 32 + pair * 16
                        both = ref[source, z, at : at + 16, :].astype(F32)
                        values[o][z * 4 + pair * 2] = both[:8]
                        values[o][z * 4 + pair * 2 + 1] = both[8:]
            group(source, *values)
    else:
        for z in range(4):
            arrived[me, z] = out[me, z]
        for j in range(1, n):
            for z in range(4):
                received(j, z)
        for s in range(n):
            for z in range(4):
                block = arrived[s, z].astype(F32)
                for o in range(2):
                    for y in range(4):
                        at = (o * 4 + y) * capacity
                        gathered[o * 16 + z * 4 + y, s * capacity : (s + 1) * capacity, :] = block[
                            at : at + capacity
                        ]

        @pl.loop(0, slots // 8)
        def _(g):
            start = pl.multiple_of(g * 8, 8)
            group(
                g,
                [gathered[q, pl.ds(start, 8), :] for q in range(16)],
                [gathered[16 + q, pl.ds(start, 8), :] for q in range(16)],
            )

    for index, offset in enumerate(AROUND):

        @pl.when(exists(offset))
        def _():
            halo(offset, index, False).wait_send()

    for j in range(1, n):
        for z in range(4):
            brick_copy(j, z).wait_send()


def build_first_block(w1, b1_ref):
    rows, cols = 288, 192
    m = iota((rows, 1), 0)
    zh, yh, channel = lax.div(m, 48), lax.rem(lax.div(m, 8), 6), m & 7
    by_row = dot(onehot(channel == iota((rows, 8), 1)), w1).astype(BF16)
    k = iota((1, cols), 1)
    pair, dx, part = lax.div(k, 48), lax.rem(lax.div(k, 16), 3), k & 15
    z, y = pair * 2 + (part >> 3), part & 7
    total = jnp.zeros((rows, cols), F32)
    for dz in range(3):
        for dy in range(3):
            pick = onehot(iota((27, cols), 0) == 9 * dz + 3 * dy + dx)
            total = total + jnp.where((z == zh + dz) & (y == yh + dy), dot(by_row, pick), 0.0)
    bias = jnp.zeros((rows, 1), F32)
    for o in range(8):
        bias = jnp.where(channel == o, b1_ref[o], bias)
    high = bias.astype(BF16).astype(F32)
    middle = (bias - high).astype(BF16).astype(F32)
    low = bias - high - middle
    c = iota((1, 16), 1)
    extra = jnp.where(c == 0, high, jnp.where(c == 1, middle, jnp.where(c == 2, low, 0.0)))
    off = (
        ((c == 3) & (zh == 0)) | ((c == 4) & (zh == 5)) | ((c == 5) & (yh == 0))
        | ((c == 6) & (yh == 5)) | (c == 7)
    )
    extra = jnp.where(off, OFF, extra)
    return total.astype(BF16), extra.astype(BF16)


def build_second_block(w2):
    rows, cols = 96, 288
    m = iota((rows, 1), 0)
    dx, o, z, y = lax.div(m, 32), (m >> 4) & 1, (m >> 2) & 3, m & 3
    k = iota((1, cols), 1)
    zh, yh, channel = lax.div(k, 48), lax.rem(lax.div(k, 8), 6), k & 7
    pick = onehot((iota((16, cols), 0) & 7) == channel)
    same = o == (iota((1, 16), 1) >> 3)
    total = jnp.zeros((rows, cols), F32)
    for dz in range(3):
        for dy in range(3):
            select = onehot(iota((rows, 27), 1) == 9 * dz + 3 * dy + dx)
            values = lax.dot_general(
                select, w2, (((1,), (1,)), ((), ())), preferred_element_type=F32
            )
            values = dot(jnp.where(same, values, 0.0).astype(BF16), pick)
            total = total + jnp.where((zh == z + dz) & (yh == y + dy), values, 0.0)
    return total.astype(BF16)


def build_codes(owners_ref, capacity):
    target = [owners_ref[b] for b in range(16)]
    lane = iota((1, 128), 1)
    bricks = jnp.full((1, 128), -1, jnp.int32)
    for b in range(16):
        rank = jnp.int32(0)
        for other in range(b):
            rank = rank + jnp.where(target[other] == target[b], 1, 0)
        bricks = jnp.where(lane == target[b] * capacity + rank, (b % 2) * 8 + b // 2, bricks)
    return bricks


def column_kernel(
    n,
    density, w1_hbm, b1_hbm, w2_hbm, b2_hbm, owners_hbm, solutes, biomass,
    frac, state_new,
    w1_ref, b1_ref, w2_ref, b2_ref, owners_ref, tiles, yedge_out, xedge_out, codes_out,
    yedge_in, xedge_in, corner_in, codes_in, win, first, second, order, values_ref,
    state, mass_in, mass,
    tile_send, tile_recv, code_send, code_recv, y_send, y_recv, x_send, x_recv, c_send, c_recv,
    local_sem, ready, beside, strips, beside_ref, placed_ref, slots_ref, slots_sem,
):
    me, gy, col = lax.axis_index("gz"), lax.axis_index("gy"), lax.axis_index("col")
    small = [
        pltpu.make_async_copy(source, target, local_sem.at[3 + i])
        for i, (source, target) in enumerate(
            (
                (w1_hbm, w1_ref), (w2_hbm, w2_ref), (b1_hbm, b1_ref), (b2_hbm, b2_ref),
                (owners_hbm, owners_ref),
            )
        )
    ]
    own = pltpu.make_async_copy(density, tiles.at[me], local_sem.at[0])
    own.start()
    for copy in small:
        copy.start()
    barrier = pltpu.get_barrier_semaphore()

    across = ({"gy": 1 - gy}, {"col": 1 - col}, {"gy": 1 - gy, "col": 1 - col})
    @pl.when(me == 0)
    def _():
        for where in across:
            pl.semaphore_signal(barrier, inc=1, device_id=where, device_id_type=MESH)

    for k in range(1, n):

        @pl.when(me < k)
        def _():
            for where in ({},) + across:
                pl.semaphore_signal(barrier, inc=1, device_id={"gz": k, **where}, device_id_type=MESH)

    load_state = pltpu.make_async_copy(solutes, state, local_sem.at[1])
    load_mass = pltpu.make_async_copy(biomass, mass_in, local_sem.at[2])

    def tile_copy(k):
        return pltpu.make_async_remote_copy(
            src_ref=density, dst_ref=tiles.at[me], send_sem=tile_send.at[k], recv_sem=tile_recv.at[me],
            device_id={"gz": k}, device_id_type=MESH,
        )

    def code_copy(k):
        return pltpu.make_async_remote_copy(
            src_ref=codes_out, dst_ref=codes_in.at[me], send_sem=code_send.at[k],
            recv_sem=code_recv.at[me], device_id={"gz": k}, device_id_type=MESH,
        )

    def edge_copy(k, source, target, send, recv, across):
        return pltpu.make_async_remote_copy(
            src_ref=source, dst_ref=target.at[me], send_sem=send.at[k], recv_sem=recv.at[me],
            device_id={"gz": k, **across}, device_id_type=MESH,
        )

    def edge_copies(k):
        return (
            edge_copy(k, xedge_out, xedge_in, x_send, x_recv, {"col": 1 - col}),
            edge_copy(k, yedge_out, yedge_in, y_send, y_recv, {"gy": 1 - gy}),
            edge_copy(k, yedge_out, corner_in, c_send, c_recv, {"gy": 1 - gy, "col": 1 - col}),
        )

    def arrival(source, target, send, recv):
        return pltpu.make_async_remote_copy(
            src_ref=source, dst_ref=target, send_sem=send, recv_sem=recv,
            device_id={"col": 1 - col}, device_id_type=MESH,
        )

    pl.semaphore_wait(barrier, jnp.where(me == 0, 3, 4 * me))
    for k in range(n - 1):

        @pl.when(k < me)
        def _():
            if k == 0:
                tile_copy(k).start()
            for where in ({},) + across:
                pl.semaphore_signal(ready.at[me], inc=1, device_id={"gz": k, **where}, device_id_type=MESH)

    row8 = iota((8, 1), 0)
    lane = iota((1, BX), 1)

    own.wait()
    packed = jnp.zeros((8, 256), F32)
    for z in range(4):
        top = tiles[me, z, 0:16, :].astype(F32)[0:8]
        bottom = tiles[me, z, 16:32, :].astype(F32)[8:16]
        pair = jnp.where(gy == 0, pltpu.roll(bottom, 2, 0), top)
        packed = jnp.where((row8 >> 1) == z, pltpu.roll(pair, 2 * z, 0) if z else pair, packed)
    yedge_out[...] = jnp.concatenate([packed[:, :128], packed[:, 128:]], axis=0).astype(BF16)
    packed = jnp.zeros((8, BX), F32)
    place = ((lane + jnp.where(col == 0, 2, 0)) & (BX - 1)) >> 1
    for z in range(4):
        whole = tiles[me, z].astype(F32)
        side = jnp.where(col == 0, whole[:, 128:], whole[:, :128])
        for i in range(4):
            p = z * 4 + i
            block = side[i * 8 : i * 8 + 8]
            packed = jnp.where(place == p, pltpu.roll(block, 2 * p, 1) if p else block, packed)
    xedge_out[...] = jnp.concatenate([packed, packed], axis=0).astype(BF16)
    for k in range(n):

        @pl.when((k < me) | (me + k == 0))
        def _():
            for copy in edge_copies(k):
                copy.start()

    for copy in small:
        copy.wait()
    codes_out[...] = build_codes(owners_ref, 8)
    codes_in[me] = codes_out[...]
    for k in range(n - 1):

        @pl.when(k < me)
        def _():
            code_copy(k).start()

    load_state.start()
    load_mass.start()

    banded, extra = build_first_block(w1_ref[...], b1_ref)
    first[:, 0:192] = banded
    first[:, 192:208] = extra

    @pl.when(me < n - 1)
    def _():
        pl.semaphore_wait(ready.at[me + 1], 4)
        pl.semaphore_signal(beside, inc=1, device_id={"gz": me + 1}, device_id_type=MESH)
        tile_copy(me + 1).start()
        code_copy(me + 1).start()
        for copy in edge_copies(me + 1):
            copy.start()

    second[...] = build_second_block(w2_ref[...])
    i = iota((256, 1), 0)
    j = iota((1, 256), 1)
    wanted = (lax.rem(i, 32) >> 2) * 32 + (i >> 5) * 4 + (i & 3)
    order[...] = onehot(wanted == j)
    for first_row in (0, (2 * n + 1) * 48):
        win[:, first_row : first_row + 48, :] = jnp.zeros((16, 48, BX), BF16)
        strips[first_row : first_row + 48, :] = jnp.zeros((48, BX), BF16)
    load_mass.wait()
    for g in range(n):
        mass[g] = mass_in[g].astype(F32)
    group = ((lane + 8) & (BX - 1)) >> 4
    natural = ((lane < 2) & (col == 0)) | ((lane >= BX - 2) & (col == 1))

    def slots_copy(s):
        return pltpu.make_async_copy(codes_in.at[s], slots_ref.at[s], slots_sem.at[s])

    def assemble(s):
        @pl.when(s != me)
        def _():
            arrival(density, tiles.at[s], tile_send.at[0], tile_recv.at[s]).wait_recv()
            arrival(codes_out, codes_in.at[s], code_send.at[0], code_recv.at[s]).wait_recv()

        slots_copy(s).start()
        arrival(xedge_out, xedge_in.at[s], x_send.at[0], x_recv.at[s]).wait_recv()
        arrival(yedge_out, yedge_in.at[s], y_send.at[0], y_recv.at[s]).wait_recv()
        arrival(yedge_out, corner_in.at[s], c_send.at[0], c_recv.at[s]).wait_recv()
        xe = xedge_in[s].astype(F32)[0:8]
        ye = yedge_in[s].astype(F32)
        ce = corner_in[s].astype(F32)
        ce = jnp.where(natural, jnp.where(col == 0, ce[0:8], ce[8:16]), jnp.where(col == 0, ye[8:16], ye[0:8]))
        inner = pltpu.roll(jnp.where(lane < 64, ye[8:16], ye[0:8]), 4, 1)
        ce = jnp.where((lane >= 2) & (lane < 6), inner, ce)
        ye = jnp.concatenate([ye[0:8], ye[8:16], ce], axis=1)
        start = pl.multiple_of(s * 96 + 48, 16)
        for zp in range(2):
            windows = []
            for z in (2 * zp, 2 * zp + 1):
                whole = tiles[s, z].astype(F32)
                side = jnp.where(col == 0, whole[:, 128:], whole[:, :128])
                inner = pltpu.roll(jnp.where(lane < 64, whole[:, 128:], whole[:, :128]), 4, 1)
                blocks = []
                for i in range(4):
                    p = z * 4 + i
                    edge = pltpu.roll(xe, BX - 2 * p, 1) if p else xe
                    edge = jnp.where(natural, edge, side[i * 8 : i * 8 + 8])
                    edge = jnp.where((lane >= 2) & (lane < 6), inner[i * 8 : i * 8 + 8], edge)
                    blocks.append(jnp.concatenate([whole[i * 8 : i * 8 + 8], edge], axis=1))
                above = jnp.where(gy == 1, pltpu.roll(ye, 8 - 2 * z, 0) if z else ye, 0.0)
                below = jnp.where(gy == 0, pltpu.roll(ye, 6 - 2 * z, 0) if z != 3 else ye, 0.0)
                down = [above] + [pltpu.roll(b, 2, 0) for b in blocks]
                up = [pltpu.roll(b, 6, 0) for b in blocks] + [below]
                held = []
                for i in range(4):
                    held.append(jnp.where(row8 < 2, down[i], down[i + 1]))
                    held.append(jnp.where(row8 < 6, up[i], up[i + 1]))
                windows.append(held)
            strip = None
            for rb in range(8):
                both = jnp.concatenate([windows[0][rb], windows[1][rb]], axis=0)
                w0, w1, ws = both[:, :BX], both[:, BX : 2 * BX], both[:, 2 * BX :]
                r0, r1, rs = pltpu.roll(w0, 1, 1), pltpu.roll(w1, 1, 1), pltpu.roll(ws, 1, 1)
                l0, l1, ls = (pltpu.roll(w, BX - 1, 1) for w in (w0, w1, ws))
                left = jnp.concatenate(
                    [jnp.where(lane == 0, jnp.where(col == 1, rs, 0.0), r0), jnp.where(lane == 0, r0, r1)], axis=1
                )
                right = jnp.concatenate(
                    [jnp.where(lane == BX - 1, l1, l0), jnp.where(lane == BX - 1, jnp.where(col == 0, ls, 0.0), l1)],
                    axis=1,
                )
                for dx, v in enumerate((left, both[:, : 2 * BX], right)):
                    win[rb, pl.ds(start + zp * 48 + dx * 16, 16), :] = v[:, :BX].astype(BF16)
                    win[8 + rb, pl.ds(start + zp * 48 + dx * 16, 16), :] = v[:, BX:].astype(BF16)
                strip = ws if rb == 0 else jnp.where(group == rb, pltpu.roll(ws, 16 * rb, 1), strip)
            for dx, v in enumerate((pltpu.roll(strip, 1, 1), strip, pltpu.roll(strip, BX - 1, 1))):
                strips[pl.ds(start + zp * 48 + dx * 16, 16), :] = v.astype(BF16)

    row16 = iota((16, 1), 0)
    bias2 = jnp.where((iota((32, 1), 0) >> 4) == 0, b2_ref[0], b2_ref[1])

    def convolution(s, bricks, put, at):
        base = (row16 < 3) | ((row16 == 3) & (s == 0)) | ((row16 == 4) & (s == n - 1))
        start = pl.multiple_of(s * 96, 16)
        at_first, at_last = (row16 == 5) & (gy == 0), (row16 == 6) & (gy == 1)

        def hidden_part(first_brick):
            data, flags = [], []
            for b in bricks[first_brick : first_brick + CHUNK]:
                flag = base | (at_first & ((b == 0) | (b == 8))) | (at_last & ((b == 7) | (b == 15)))
                flags.append(jnp.broadcast_to(onehot(flag), (16, BX)))
                data.append(win[b, pl.ds(start, 192), :])
            if first_brick == 0:
                flags.append(onehot(base | (at_first & (group == 0)) | (at_last & (group == 7))))
                data.append(strips[pl.ds(start, 192), :])
            operand = jnp.concatenate(
                [jnp.concatenate(data, axis=1), jnp.concatenate(flags, axis=1)], axis=0
            )
            return jnp.maximum(dot(first[...], operand), 0.0).astype(BF16)

        def fraction_part(first_brick, held):
            total = dot(second[...], held)
            if first_brick == 0:
                t = total[:, CHUNK * BX :]
                for b in range(16):
                    rb, cb = b % 8, b // 8
                    before = pltpu.roll(t[0:32], (BX + 1 - 4 * cb - 16 * rb) % BX, 1)
                    after = pltpu.roll(t[64:96], (BX - 1 - 4 * (1 - cb) - 16 * rb) % BX, 1)
                    at_left = (lane == 0) if cb else (lane == 0) & (col == 1)
                    at_right = (lane == BX - 1) & (col == 0) if cb else lane == BX - 1
                    beside_ref[at * 16 + b] = jnp.where(at_left, before, jnp.where(at_right, after, 0.0))
            for r, b in enumerate(bricks[first_brick : first_brick + CHUNK]):
                t = total[:, r * BX : (r + 1) * BX]
                value = jnp.where(lane == 0, 0.0, pltpu.roll(t[0:32], 1, 1)) + t[32:64]
                value = value + jnp.where(lane == BX - 1, 0.0, pltpu.roll(t[64:96], BX - 1, 1))
                value = value + beside_ref[b + at * 16]
                value = (1.0 / (1.0 + jnp.exp(-(value + bias2)))).astype(BF16)
                put(first_brick + r, value)

        return [
            (functools.partial(hidden_part, i), functools.partial(fraction_part, i))
            for i in range(0, len(bricks), CHUNK)
        ]

    def diffusion(s, at):
        placed = placed_ref[at]
        pore = [placed[q * 8 : q * 8 + 8] for q in range(16)]
        organic = [placed[128 + q * 8 : 136 + q * 8] for q in range(16)]
        carbon = [state[s, pl.ds(q, 8, stride=32), :] for q in range(16)]
        oxygen = [state[s, pl.ds(16 + q, 8, stride=32), :] for q in range(16)]
        weight = [mass[s, pl.ds(q, 8, stride=16), :] for q in range(16)]
        for carbon, oxygen in diffuse_steps(
            carbon, oxygen, pore, organic, weight, iota((8, BX), 1)
        ):
            yield
        for q in range(16):
            state_new[s, pl.ds(q, 8, stride=32), :] = carbon[q]
            state_new[s, pl.ds(16 + q, 8, stride=32), :] = oxygen[q]

    def fractions_of_slots(s, at):
        held = [slots_ref[s, 0, me * 8 + k] for k in range(8)]
        bricks = [jnp.maximum(b, 0) for b in held]
        kept = [jnp.where(b >= 0, 1.0, 0.0) for b in held]

        def put_slot(k, value):
            placed_ref[at, pl.ds(k, 32, stride=8), :] = value.astype(F32) * kept[k]

        return bricks, put_slot

    def received_tile(s, at):
        bricks, put_slot = fractions_of_slots(s, at)
        return convolution(s, bricks, put_slot, at), lambda: None

    def own_tile(s, at):
        def put_own(b, value):
            values_ref[b] = value

        def finish():
            both = [values_ref[8 * cb : 8 * cb + 8].reshape(256, BX) for cb in range(2)]
            whole = dot(order[...], jnp.concatenate(both, axis=1))
            frac[...] = whole.astype(BF16).reshape(frac.shape)
            bricks, put_slot = fractions_of_slots(s, at)
            for k in range(8):
                put_slot(k, values_ref[bricks[k]])

        return convolution(s, list(range(16)), put_own, at), finish

    def process(tiles_and_kinds):
        parts, behind = [], []
        for at, (s, kind) in enumerate(tiles_and_kinds):
            chunks, finish = kind(s, at)
            parts += [(c, None) for c in chunks[:-1]] + [(chunks[-1], (finish, s, at))]
        held = parts[0][0][0]()
        for index, ((_, fraction_part), end) in enumerate(parts):
            later = parts[index + 1][0][0]() if index + 1 < len(parts) else None
            fraction_part(held)
            held = later
            for steps in behind:
                for _ in range(2):
                    next(steps, None)
            if end is not None:
                finish, s, at = end
                finish()
                behind.append(diffusion(s, at))
        for steps in behind:
            for _ in steps:
                pass

    for k in range(1, n - 1):

        @pl.when(k < me)
        def _():
            tile_copy(k).start()

    @pl.when(me > 0)
    def _():
        pl.semaphore_wait(beside, 1)
        for copy in edge_copies(me):
            copy.start()

    for k in range(2, n):

        @pl.when(me < k - 1)
        def _():
            pl.semaphore_wait(ready.at[k], 4)
            tile_copy(k).start()
            code_copy(k).start()
            for copy in edge_copies(k):
                copy.start()

    def source(step):
        return jnp.where(me < n // 2, step, n - 1 - step)

    assemble(source(0))
    load_state.wait()

    s0, s1, s2, s3 = (source(step) for step in range(n))
    assemble(s1)
    slots_copy(s0).wait()

    @pl.when(s0 == me)
    def _():
        process([(s0, own_tile)])

    @pl.when(s0 != me)
    def _():
        process([(s0, received_tile)])

    assemble(s2)
    slots_copy(s1).wait()
    assemble(s3)
    slots_copy(s2).wait()
    slots_copy(s3).wait()

    @pl.when(s1 == me)
    def _():
        process([(s1, own_tile), (s2, received_tile), (s3, received_tile)])

    @pl.when(s1 != me)
    def _():
        process([(s1, received_tile), (s2, received_tile), (s3, received_tile)])


    for k in range(n):

        @pl.when(k != me)
        def _():
            tile_copy(k).wait_send()
            code_copy(k).wait_send()

        for copy in edge_copies(k):
            copy.wait_send()


def column_call(n, groups, density, operands):
    anywhere = pl.BlockSpec(memory_space=pltpu.HBM)
    inside = pl.BlockSpec(memory_space=pltpu.VMEM)
    remote = [pltpu.SemaphoreType.DMA((n,))] * 10
    return pl.pallas_call(
        functools.partial(column_kernel, n),
        out_shape=(
            pltpu.VMEM((2,) + density.shape, BF16),
            pltpu.VMEM((groups, 256, BX), F32),
        ),
        in_specs=[anywhere] * 8,
        out_specs=(inside, inside),
        scratch_shapes=[
            pltpu.VMEM((8, 27), BF16),
            pltpu.SMEM((8,), F32),
            pltpu.VMEM((16, 27), BF16),
            pltpu.SMEM((2,), F32),
            pltpu.SMEM((16,), jnp.int32),
            pltpu.VMEM((n,) + density.shape, BF16),
            pltpu.VMEM((16, BX), BF16),
            pltpu.VMEM((16, BX), BF16),
            pltpu.VMEM((1, BX), jnp.int32),
            pltpu.VMEM((n, 16, BX), BF16),
            pltpu.VMEM((n, 16, BX), BF16),
            pltpu.VMEM((n, 16, BX), BF16),
            pltpu.VMEM((n, 1, BX), jnp.int32),
            pltpu.VMEM((16, (2 * n + 2) * 48, BX), BF16),
            pltpu.VMEM((288, 208), BF16),
            pltpu.VMEM((96, 288), BF16),
            pltpu.VMEM((256, 256), BF16),
            pltpu.VMEM((16, 32, BX), BF16),
            pltpu.VMEM((groups, 256, BX), F32),
            pltpu.VMEM((groups, 128, BX), BF16),
            pltpu.VMEM((groups, 128, BX), F32),
        ] + remote + [pltpu.SemaphoreType.DMA((8,)), pltpu.SemaphoreType.REGULAR((n,)), pltpu.SemaphoreType.REGULAR,
            pltpu.VMEM(((2 * n + 2) * 48, BX), BF16),
            pltpu.VMEM((48, 32, BX), F32),
            pltpu.VMEM((3, 256, BX), F32),
            pltpu.SMEM((n, 1, BX), jnp.int32),
            pltpu.SemaphoreType.DMA((n,)),
        ],
        compiler_params=pltpu.CompilerParams(
            collective_id=1, has_side_effects=True,
            vmem_limit_bytes=(65344 - 128 - groups * 128) * 1024,
        ),
    )(*operands)


def exchange_call(sizes, capacity, groups, density, operands):
    n, slots, per = sizes[0], groups * 8, 8 * capacity
    anywhere = pl.BlockSpec(memory_space=pltpu.HBM)
    inside = pl.BlockSpec(memory_space=pltpu.VMEM)
    return pl.pallas_call(
        functools.partial(kernel, sizes, capacity),
        out_shape=(
            pltpu.VMEM((2,) + density.shape, BF16),
            pltpu.VMEM((groups, 256, BX), F32),
        ),
        in_specs=[anywhere] * 8,
        out_specs=(inside, inside),
        scratch_shapes=[
            pltpu.VMEM((8, 27), BF16),
            pltpu.SMEM((8,), F32),
            pltpu.VMEM((16, 27), BF16),
            pltpu.SMEM((2,), F32),
            pltpu.SMEM((16,), jnp.int32),
            pltpu.VMEM((8, 64, 512), BF16),
            pltpu.VMEM((272, 9 * KR), BF16),
            pltpu.VMEM((3, 192, 272), BF16),
            pltpu.VMEM((8 * 3 * KR, LANES), BF16),
            pltpu.VMEM((6, 272, LANES), BF16),
            pltpu.VMEM((n, 4, per, BX), BF16),
            pltpu.VMEM((n, 4, per, BX), BF16),
            pltpu.VMEM((groups, 256, BX), F32),
            pltpu.VMEM((groups, 128, BX), BF16),
            pltpu.VMEM((groups, 128, BX), F32),
            pltpu.VMEM((32, slots if capacity != 8 else 8, BX), F32),
            pltpu.SemaphoreType.DMA((26,)),
            pltpu.SemaphoreType.DMA((26,)),
            pltpu.SemaphoreType.DMA((n, 4)),
            pltpu.SemaphoreType.DMA((n, 4)),
            pltpu.SemaphoreType.DMA((9,)),
            pltpu.SemaphoreType.DMA((groups,)),
        ],
        compiler_params=pltpu.CompilerParams(
            collective_id=0, has_side_effects=True, vmem_limit_bytes=(65344 - 128 - groups * 128) * 1024
        ),
    )(*operands)


def write_out(frac, state, fractions, solutes_next, sem):
    copies = [
        pltpu.make_async_copy(frac, fractions, sem.at[0]),
        pltpu.make_async_copy(state, solutes_next, sem.at[1]),
    ]
    for copy in copies:
        copy.start()
    for copy in copies:
        copy.wait()


def per_device(
    sizes, density, first_kernel, first_bias, second_kernel, second_bias, owners, solutes, biomass
):
    n = sizes[0]
    slots = solutes.shape[3]
    capacity = slots // n
    anywhere = pl.BlockSpec(memory_space=pltpu.HBM)
    groups = slots // 8
    inside = pl.BlockSpec(memory_space=pltpu.VMEM)
    operands = (
        density,
        first_kernel.transpose(2, 1, 0).reshape(8, 27),
        first_bias,
        second_kernel.transpose(1, 2, 0).reshape(16, 27),
        second_bias,
        owners.reshape(-1),
        solutes.reshape(groups, 256, BX),
        biomass.reshape(groups, 128, BX),
    )
    if sizes == (4, 2, 2) and capacity == 8:
        frac, state_new = column_call(n, groups, density, operands)
    else:
        frac, state_new = exchange_call(sizes, capacity, groups, density, operands)
    fractions, solutes_next = pl.pallas_call(
        write_out,
        out_shape=(
            jax.ShapeDtypeStruct((2,) + density.shape, BF16),
            jax.ShapeDtypeStruct((groups, 256, BX), F32),
        ),
        in_specs=[inside, inside],
        out_specs=(anywhere, anywhere),
        scratch_shapes=[pltpu.SemaphoreType.DMA((2,))],
        compiler_params=pltpu.CompilerParams(vmem_limit_bytes=16 * 1024 * 1024),
    )(frac, state_new)
    return fractions, solutes_next.reshape(solutes.shape)


def solution(mesh):
    sizes = tuple(mesh.shape[axis] for axis in ("gz", "gy", "col"))
    return jax.shard_map(
        functools.partial(per_device, sizes),
        mesh=mesh,
        in_specs=(
            P(("cores", "gz"), "gy", "col"),
            P(),
            P(),
            P(),
            P(),
            P(("cores", "gz"), "gy", "col", None, None),
            P(("cores", "gz"), "gy", "col", None, None, None, None, None),
            P(("cores", "gz"), "gy", "col", None, None, None, None),
        ),
        out_specs=(
            P(None, ("cores", "gz"), "gy", "col"),
            P(("cores", "gz"), "gy", "col", None, None, None, None, None),
        ),
        check_vma=False,
    )
```

```python
import functools
import itertools

import jax
import jax.numpy as jnp
from jax import lax
from jax.experimental import pallas as pl
from jax.experimental.pallas import tpu as pltpu
from jax.sharding import PartitionSpec as P

BY = 4
BX = 128
STEPS = 4
MESH = pl.DeviceIdType.MESH
F32 = jnp.float32
BF16 = jnp.bfloat16
AROUND = [d for d in itertools.product((-1, 0, 1), repeat=3) if d != (0, 0, 0)]
PLACE_Z = {0: (0, 4), 1: (4, 2), -1: (6, 2)}
PLACE_Y = {0: (0, 32), 1: (32, 16), -1: (48, 16)}
PLACE_X = {0: (0, 256), 1: (256, 128), -1: (384, 128)}
TAKE_Z = {0: (0, 4), 1: (0, 2), -1: (2, 2)}
TAKE_Y = {0: (0, 32), 1: (0, 16), -1: (16, 16)}
TAKE_X = {0: (0, 256), 1: (0, 128), -1: (128, 128)}
KR = 48
HR = 34
LANES = 384
CHUNK = 4
OFF = -1e30


def region(ref, tables, offset):
    return ref.at[tuple(pl.ds(*table[o]) for table, o in zip(tables, offset))]


def iota(shape, dim):
    return lax.broadcasted_iota(jnp.int32, shape, dim)


def onehot(condition):
    return jnp.where(condition, 1.0, 0.0).astype(BF16)


def dot(a, b):
    return jnp.dot(a, b, preferred_element_type=F32)


def build_first(w1):
    hidden = w1.shape[0]
    rows, cols = hidden * HR, 9 * KR
    i = iota((rows, 1), 0)
    channel, yi = lax.div(i, HR), lax.rem(i, HR)
    expand = onehot(channel == iota((rows, hidden), 1))
    by_row = dot(expand, w1).astype(BF16)
    j = iota((1, cols), 1)
    tap, r = lax.div(j, KR), lax.rem(j, KR)
    y = jnp.where(r < 40, r, r - KR)
    tap_offset = lax.div(tap, 3) * 9 + lax.rem(tap, 3)
    total = jnp.zeros((rows, cols), F32)
    for dy in range(3):
        pick = onehot(iota((27, cols), 0) == tap_offset + 3 * dy)
        total = total + jnp.where(y == yi + (dy - 2), dot(by_row, pick), 0.0)
    return total.astype(BF16)


def build_second(w2, first_row, last_row):
    hidden = w2.shape[0] // 2
    rows, cols = 192, hidden * HR
    i = iota((rows, 1), 0)
    group, y = lax.div(i, 32), lax.rem(i, 32)
    j = iota((1, cols), 1)
    yi = lax.rem(j, HR)
    inside = jnp.logical_not(((yi == 0) & first_row) | ((yi == HR - 1) & last_row))
    yi = jnp.where(inside, yi, -100)
    pick = onehot(lax.rem(iota((2 * hidden, cols), 0), hidden) == lax.div(j, HR))
    same = lax.rem(group, 2) == lax.div(iota((1, 2 * hidden), 1), hidden)
    blocks = []
    for dz in range(3):
        total = jnp.zeros((rows, cols), F32)
        for dy in range(3):
            select = onehot(iota((rows, 27), 1) == 9 * dz + 3 * dy + lax.div(group, 2))
            values = lax.dot_general(
                select, w2, (((1,), (1,)), ((), ())), preferred_element_type=F32
            )
            values = dot(jnp.where(same, values, 0.0).astype(BF16), pick)
            total = total + jnp.where(yi == y + dy, values, 0.0)
        blocks.append(total.astype(BF16))
    return blocks


def build_placing(owners_ref, slots, capacity):
    count = owners_ref.shape[0]
    target = [owners_ref[b] for b in range(count)]
    j = iota((1, 128), 1)
    brick = ((j & 31) >> 2) * 2 + (j >> 6)
    slot = jnp.zeros((1, 128), jnp.int32)
    for b in range(count):
        rank = jnp.int32(0)
        for other in range(b):
            rank = rank + jnp.where(target[other] == target[b], 1, 0)
        slot = jnp.where(brick == b, target[b] * capacity + rank, slot)
    column = slot * 8 + ((j >> 5) & 1) * 4 + (j & 3)
    i = iota((slots * 8, 1), 0)
    owner = lax.div(i, capacity * 8)
    row = (owner * capacity + lax.rem(i, capacity)) * 8 + lax.rem(lax.div(i, capacity), 8)
    return onehot(row == column)


def diffuse_steps(carbon, oxygen, pore, organic, mass, lane):
    low, high = lane == 0, lane == BX - 1
    pore_c = [0.12 * v for v in pore]
    pore_o = [0.16 * v for v in pore]
    gain = [0.3 * v for v in organic]
    mass = [0.25 * v for v in mass]

    def laplace(field, q):
        z, y = q // 4, q % 4
        v = field[q]
        total = jnp.where(low, v, pltpu.roll(v, 1, 1)) + jnp.where(high, v, pltpu.roll(v, BX - 1, 1))
        near = 2
        for ok, at in ((z > 0, q - 4), (z < 3, q + 4), (y > 0, q - 1), (y < 3, q + 1)):
            if ok:
                total = total + field[at]
                near += 1
        return total - float(near) * v

    for _ in range(STEPS):
        carbon_new, oxygen_new = [], []
        for q in range(16):
            c, o = carbon[q], oxygen[q]
            uptake = mass[q] * c * o / ((0.5 + jnp.abs(c)) * (0.3 + jnp.abs(o)))
            carbon_new.append(c + pore_c[q] * laplace(carbon, q) + gain[q] - uptake)
            oxygen_new.append(o + pore_o[q] * laplace(oxygen, q) - uptake)
        carbon, oxygen = carbon_new, oxygen_new
        yield carbon, oxygen


def diffuse(*fields):
    *_, last = diffuse_steps(*fields)
    return last


def kernel(
    sizes, capacity,
    density, w1_hbm, b1_hbm, w2_hbm, b2_hbm, owners_hbm, solutes, biomass,
    frac, state_new,
    w1_ref, b1_ref, w2_ref, b2_ref, owners_ref, tile, first, second, shifted, hidden, out, arrived, state, mass_in, mass, gathered,
    halo_send, halo_recv, brick_send, brick_recv, local_sem, group_sem,
):
    n, n_gy, n_col = sizes
    slots = n * capacity
    here = (lax.axis_index("gz"), lax.axis_index("gy"), lax.axis_index("col"))
    me = here[0]

    def exists(offset):
        ok = None
        for position, size, o in zip(here, sizes, offset):
            test = None if o == 0 else (position + o >= 0) & (position + o < size)
            ok = test if ok is None else ok if test is None else ok & test
        return ok

    def device(offset):
        return {"gz": here[0] + offset[0], "gy": here[1] + offset[1], "col": here[2] + offset[2]}

    def halo(offset, index, receiver):
        seen = tuple(-o for o in offset) if not receiver else offset
        return pltpu.make_async_remote_copy(
            src_ref=region(density, (TAKE_Z, TAKE_Y, TAKE_X), seen),
            dst_ref=region(tile, (PLACE_Z, PLACE_Y, PLACE_X), seen),
            send_sem=halo_send.at[index],
            recv_sem=halo_recv.at[AROUND.index(seen)],
            device_id=device(offset),
            device_id_type=MESH,
        )

    small = [
        pltpu.make_async_copy(source, target, local_sem.at[4 + i])
        for i, (source, target) in enumerate(
            (
                (w1_hbm, w1_ref), (w2_hbm, w2_ref), (b1_hbm, b1_ref), (b2_hbm, b2_ref),
                (owners_hbm, owners_ref),
            )
        )
    ]
    for copy in small:
        copy.start()
    tile[...] = jnp.zeros_like(tile)
    barrier = pltpu.get_barrier_semaphore()
    expected = jnp.int32(n - 1)
    for offset in AROUND:
        ok = exists(offset)
        expected = expected + jnp.where(ok, 1, 0)

        @pl.when(ok)
        def _():
            pl.semaphore_signal(barrier, inc=1, device_id=device(offset), device_id_type=MESH)

    for j in range(1, n):
        pl.semaphore_signal(
            barrier, inc=1, device_id={"gz": lax.rem(me + j, n)}, device_id_type=MESH
        )
    own = pltpu.make_async_copy(
        density, region(tile, (PLACE_Z, PLACE_Y, PLACE_X), (0, 0, 0)), local_sem.at[0]
    )
    own.start()
    load_state = pltpu.make_async_copy(solutes, state, local_sem.at[1])
    load_mass = pltpu.make_async_copy(biomass, mass_in, local_sem.at[2])
    pl.semaphore_wait(barrier, expected)

    for index, offset in enumerate(AROUND):

        @pl.when(exists(offset))
        def _():
            halo(offset, index, False).start()

    load_state.start()
    load_mass.start()

    for copy in small:
        copy.wait()
    first[...] = build_first(w1_ref[...])
    for dz, block in enumerate(build_second(w2_ref[...], here[1] == 0, here[1] == n_gy - 1)):
        second[dz] = block
    placing = build_placing(owners_ref, slots, capacity)
    channel = lax.div(iota((272, 1), 0), HR)
    bias1 = jnp.zeros((272, 1), F32)
    for o in range(8):
        bias1 = jnp.where(channel == o, b1_ref[o], bias1)
    bias2 = jnp.where(iota((64, 1), 0) < 32, b2_ref[0], b2_ref[1])
    lane = iota((1, BX), 1)
    keep = jnp.where(
        ((lane == 0) & (here[2] < n_col - 1)) | ((lane == BX - 1) & (here[2] > 0)), 1.0, 0.0
    )
    load_mass.wait()
    for g in range(slots // 8):
        mass[g] = mass_in[g].astype(F32)

    own.wait()
    for index, offset in enumerate(AROUND):

        @pl.when(exists(offset))
        def _():
            halo(offset, index, True).wait_recv()

    half_row = iota((16, 512), 0) < 8
    half_lane = iota((KR, BX), 1) < 64
    for zz in range(8):
        z = (zz + 6) % 8
        side = jnp.where(half_row, tile[z, 32:48, :].astype(F32), tile[z, 48:64, :].astype(F32))
        whole = jnp.concatenate([tile[z, 0:32, :].astype(F32), side], axis=0)
        edge = jnp.where(half_lane, whole[:, 256:384], whole[:, 384:512])
        whole = jnp.concatenate([whole[:, :256], edge], axis=1)
        base = zz * 3 * KR
        shifted[base : base + KR, :] = pltpu.roll(whole, 1, 1).astype(BF16)
        shifted[base + KR : base + 2 * KR, :] = whole.astype(BF16)
        shifted[base + 2 * KR : base + 3 * KR, :] = pltpu.roll(whole, LANES - 1, 1).astype(BF16)

    def hidden_slice(zi):
        value = dot(first[...], shifted[zi * 3 * KR : (zi + 3) * 3 * KR, :])
        value = jnp.maximum(value + bias1, 0.0)
        hidden[zi, :, 0:256] = value[:, :256].astype(BF16)
        hidden[zi, :, 256:384] = (value[:, 256:] * keep).astype(BF16)

    def brick_copy(j, z):
        to = lax.rem(me + j, n)
        return pltpu.make_async_remote_copy(
            src_ref=out.at[to, z],
            dst_ref=arrived.at[me, z],
            send_sem=brick_send.at[j, z],
            recv_sem=brick_recv.at[j, z],
            device_id={"gz": to},
            device_id_type=MESH,
        )

    hidden_slice(0)

    @pl.when(me == 0)
    def _():
        hidden[0] = jnp.zeros_like(hidden[0])

    hidden_slice(1)
    per = 8 * capacity
    for z in range(4):
        hidden_slice(z + 2)
        if z == 3:

            @pl.when(me == n - 1)
            def _():
                hidden[5] = jnp.zeros_like(hidden[5])

        total = jnp.zeros((192, LANES), F32)
        for dz in range(3):
            total = total + dot(second[dz], hidden[z + dz])
        value = (
            pltpu.roll(total[0:64], 1, 1) + total[64:128] + pltpu.roll(total[128:192], LANES - 1, 1)
        )[:, :256]
        value = (1.0 / (1.0 + jnp.exp(-(value + bias2)))).astype(BF16)
        frac[0, z] = value[:32]
        frac[1, z] = value[32:]
        placed = dot(placing, jnp.concatenate([value[:, :128], value[:, 128:]], axis=0)).astype(BF16)
        for d in range(n):
            out[d, z] = placed[d * per : (d + 1) * per]
        for j in range(1, n):
            brick_copy(j, z).start()

    load_state.wait()

    def received(j, z):
        source = lax.rem(me - j + n, n)
        pltpu.make_async_remote_copy(
            src_ref=out.at[source, z],
            dst_ref=arrived.at[source, z],
            send_sem=brick_send.at[j, z],
            recv_sem=brick_recv.at[j, z],
            device_id={"gz": source},
            device_id_type=MESH,
        ).wait_recv()


    def group(g, pore, organic):
        carbon = [state[g, pl.ds(q, 8, stride=32), :] for q in range(16)]
        oxygen = [state[g, pl.ds(16 + q, 8, stride=32), :] for q in range(16)]
        held = [mass[g, pl.ds(q, 8, stride=16), :] for q in range(16)]
        carbon, oxygen = diffuse(carbon, oxygen, pore, organic, held, iota((8, BX), 1))
        for q in range(16):
            state_new[g, pl.ds(q, 8, stride=32), :] = carbon[q]
            state_new[g, pl.ds(16 + q, 8, stride=32), :] = oxygen[q]

    if capacity == 8:
        for j in range(n):
            source = lax.rem(me - j + n, n)
            values = [[None] * 16, [None] * 16]
            for z in range(4):
                if j:
                    received(j, z)
                ref = arrived if j else out
                for o in range(2):
                    for pair in range(2):
                        at = o * 32 + pair * 16
                        both = ref[source, z, at : at + 16, :].astype(F32)
                        values[o][z * 4 + pair * 2] = both[:8]
                        values[o][z * 4 + pair * 2 + 1] = both[8:]
            group(source, *values)
    else:
        for z in range(4):
            arrived[me, z] = out[me, z]
        for j in range(1, n):
            for z in range(4):
                received(j, z)
        for s in range(n):
            for z in range(4):
                block = arrived[s, z].astype(F32)
                for o in range(2):
                    for y in range(4):
                        at = (o * 4 + y) * capacity
                        gathered[o * 16 + z * 4 + y, s * capacity : (s + 1) * capacity, :] = block[
                            at : at + capacity
                        ]

        @pl.loop(0, slots // 8)
        def _(g):
            start = pl.multiple_of(g * 8, 8)
            group(
                g,
                [gathered[q, pl.ds(start, 8), :] for q in range(16)],
                [gathered[16 + q, pl.ds(start, 8), :] for q in range(16)],
            )

    for index, offset in enumerate(AROUND):

        @pl.when(exists(offset))
        def _():
            halo(offset, index, False).wait_send()

    for j in range(1, n):
        for z in range(4):
            brick_copy(j, z).wait_send()


def build_first_block(w1, b1_ref):
    rows, cols = 288, 192
    m = iota((rows, 1), 0)
    zh, yh, channel = lax.div(m, 48), lax.rem(lax.div(m, 8), 6), m & 7
    by_row = dot(onehot(channel == iota((rows, 8), 1)), w1).astype(BF16)
    k = iota((1, cols), 1)
    pair, dx, part = lax.div(k, 48), lax.rem(lax.div(k, 16), 3), k & 15
    z, y = pair * 2 + (part >> 3), part & 7
    total = jnp.zeros((rows, cols), F32)
    for dz in range(3):
        for dy in range(3):
            pick = onehot(iota((27, cols), 0) == 9 * dz + 3 * dy + dx)
            total = total + jnp.where((z == zh + dz) & (y == yh + dy), dot(by_row, pick), 0.0)
    bias = jnp.zeros((rows, 1), F32)
    for o in range(8):
        bias = jnp.where(channel == o, b1_ref[o], bias)
    high = bias.astype(BF16).astype(F32)
    middle = (bias - high).astype(BF16).astype(F32)
    low = bias - high - middle
    c = iota((1, 16), 1)
    extra = jnp.where(c == 0, high, jnp.where(c == 1, middle, jnp.where(c == 2, low, 0.0)))
    off = (
        ((c == 3) & (zh == 0)) | ((c == 4) & (zh == 5)) | ((c == 5) & (yh == 0))
        | ((c == 6) & (yh == 5)) | (c == 7)
    )
    extra = jnp.where(off, OFF, extra)
    return total.astype(BF16), extra.astype(BF16)


def build_second_block(w2):
    rows, cols = 96, 288
    m = iota((rows, 1), 0)
    dx, o, z, y = lax.div(m, 32), (m >> 4) & 1, (m >> 2) & 3, m & 3
    k = iota((1, cols), 1)
    zh, yh, channel = lax.div(k, 48), lax.rem(lax.div(k, 8), 6), k & 7
    pick = onehot((iota((16, cols), 0) & 7) == channel)
    same = o == (iota((1, 16), 1) >> 3)
    total = jnp.zeros((rows, cols), F32)
    for dz in range(3):
        for dy in range(3):
            select = onehot(iota((rows, 27), 1) == 9 * dz + 3 * dy + dx)
            values = lax.dot_general(
                select, w2, (((1,), (1,)), ((), ())), preferred_element_type=F32
            )
            values = dot(jnp.where(same, values, 0.0).astype(BF16), pick)
            total = total + jnp.where((zh == z + dz) & (yh == y + dy), values, 0.0)
    return total.astype(BF16)


def build_codes(owners_ref, capacity):
    target = [owners_ref[b] for b in range(16)]
    lane = iota((1, 128), 1)
    bricks = jnp.full((1, 128), -1, jnp.int32)
    for b in range(16):
        rank = jnp.int32(0)
        for other in range(b):
            rank = rank + jnp.where(target[other] == target[b], 1, 0)
        bricks = jnp.where(lane == target[b] * capacity + rank, (b % 2) * 8 + b // 2, bricks)
    return bricks


def column_kernel(
    n,
    density, w1_hbm, b1_hbm, w2_hbm, b2_hbm, owners_hbm, solutes, biomass,
    frac, state_new,
    w1_ref, b1_ref, w2_ref, b2_ref, owners_ref, tiles, yedge_out, xedge_out, codes_out,
    yedge_in, xedge_in, corner_in, codes_in, win, first, second, order, values_ref,
    state, mass_in, mass,
    tile_send, tile_recv, code_send, code_recv, y_send, y_recv, x_send, x_recv, c_send, c_recv,
    local_sem, ready, beside, strips, beside_ref, placed_ref, slots_ref, slots_sem,
):
    me, gy, col = lax.axis_index("gz"), lax.axis_index("gy"), lax.axis_index("col")
    small = [
        pltpu.make_async_copy(source, target, local_sem.at[3 + i])
        for i, (source, target) in enumerate(
            (
                (w1_hbm, w1_ref), (w2_hbm, w2_ref), (b1_hbm, b1_ref), (b2_hbm, b2_ref),
                (owners_hbm, owners_ref),
            )
        )
    ]
    own = pltpu.make_async_copy(density, tiles.at[me], local_sem.at[0])
    own.start()
    for copy in small:
        copy.start()
    barrier = pltpu.get_barrier_semaphore()

    across = ({"gy": 1 - gy}, {"col": 1 - col}, {"gy": 1 - gy, "col": 1 - col})
    @pl.when(me == 0)
    def _():
        for where in across:
            pl.semaphore_signal(barrier, inc=1, device_id=where, device_id_type=MESH)

    for k in range(1, n):

        @pl.when(me < k)
        def _():
            for where in ({},) + across:
                pl.semaphore_signal(barrier, inc=1, device_id={"gz": k, **where}, device_id_type=MESH)

    load_state = pltpu.make_async_copy(solutes, state, local_sem.at[1])
    load_mass = pltpu.make_async_copy(biomass, mass_in, local_sem.at[2])

    def tile_copy(k):
        return pltpu.make_async_remote_copy(
            src_ref=density, dst_ref=tiles.at[me], send_sem=tile_send.at[k], recv_sem=tile_recv.at[me],
            device_id={"gz": k}, device_id_type=MESH,
        )

    def code_copy(k):
        return pltpu.make_async_remote_copy(
            src_ref=codes_out, dst_ref=codes_in.at[me], send_sem=code_send.at[k],
            recv_sem=code_recv.at[me], device_id={"gz": k}, device_id_type=MESH,
        )

    def edge_copy(k, source, target, send, recv, across):
        return pltpu.make_async_remote_copy(
            src_ref=source, dst_ref=target.at[me], send_sem=send.at[k], recv_sem=recv.at[me],
            device_id={"gz": k, **across}, device_id_type=MESH,
        )

    def edge_copies(k):
        return (
            edge_copy(k, xedge_out, xedge_in, x_send, x_recv, {"col": 1 - col}),
            edge_copy(k, yedge_out, yedge_in, y_send, y_recv, {"gy": 1 - gy}),
            edge_copy(k, yedge_out, corner_in, c_send, c_recv, {"gy": 1 - gy, "col": 1 - col}),
        )

    def arrival(source, target, send, recv):
        return pltpu.make_async_remote_copy(
            src_ref=source, dst_ref=target, send_sem=send, recv_sem=recv,
            device_id={"col": 1 - col}, device_id_type=MESH,
        )

    pl.semaphore_wait(barrier, jnp.where(me == 0, 3, 4 * me))
    for k in range(n - 1):

        @pl.when(k < me)
        def _():
            if k == 0:
                tile_copy(k).start()
            for where in ({},) + across:
                pl.semaphore_signal(ready.at[me], inc=1, device_id={"gz": k, **where}, device_id_type=MESH)

    row8 = iota((8, 1), 0)
    lane = iota((1, BX), 1)

    own.wait()
    packed = jnp.zeros((8, 256), F32)
    for z in range(4):
        top = tiles[me, z, 0:16, :].astype(F32)[0:8]
        bottom = tiles[me, z, 16:32, :].astype(F32)[8:16]
        pair = jnp.where(gy == 0, pltpu.roll(bottom, 2, 0), top)
        packed = jnp.where((row8 >> 1) == z, pltpu.roll(pair, 2 * z, 0) if z else pair, packed)
    yedge_out[...] = jnp.concatenate([packed[:, :128], packed[:, 128:]], axis=0).astype(BF16)
    packed = jnp.zeros((8, BX), F32)
    place = ((lane + jnp.where(col == 0, 2, 0)) & (BX - 1)) >> 1
    for z in range(4):
        whole = tiles[me, z].astype(F32)
        side = jnp.where(col == 0, whole[:, 128:], whole[:, :128])
        for i in range(4):
            p = z * 4 + i
            block = side[i * 8 : i * 8 + 8]
            packed = jnp.where(place == p, pltpu.roll(block, 2 * p, 1) if p else block, packed)
    xedge_out[...] = jnp.concatenate([packed, packed], axis=0).astype(BF16)
    for k in range(n):

        @pl.when((k < me) | (me + k == 0))
        def _():
            for copy in edge_copies(k):
                copy.start()

    for copy in small:
        copy.wait()
    codes_out[...] = build_codes(owners_ref, 8)
    codes_in[me] = codes_out[...]
    for k in range(n - 1):

        @pl.when(k < me)
        def _():
            code_copy(k).start()

    load_state.start()
    load_mass.start()

    banded, extra = build_first_block(w1_ref[...], b1_ref)
    first[:, 0:192] = banded
    first[:, 192:208] = extra

    @pl.when(me < n - 1)
    def _():
        pl.semaphore_wait(ready.at[me + 1], 4)
        pl.semaphore_signal(beside, inc=1, device_id={"gz": me + 1}, device_id_type=MESH)
        tile_copy(me + 1).start()
        code_copy(me + 1).start()
        for copy in edge_copies(me + 1):
            copy.start()

    second[...] = build_second_block(w2_ref[...])
    i = iota((256, 1), 0)
    j = iota((1, 256), 1)
    wanted = (lax.rem(i, 32) >> 2) * 32 + (i >> 5) * 4 + (i & 3)
    order[...] = onehot(wanted == j)
    for first_row in (0, (2 * n + 1) * 48):
        win[:, first_row : first_row + 48, :] = jnp.zeros((16, 48, BX), BF16)
        strips[first_row : first_row + 48, :] = jnp.zeros((48, BX), BF16)
    load_mass.wait()
    for g in range(n):
        mass[g] = mass_in[g].astype(F32)
    group = ((lane + 8) & (BX - 1)) >> 4
    natural = ((lane < 2) & (col == 0)) | ((lane >= BX - 2) & (col == 1))

    def slots_copy(s):
        return pltpu.make_async_copy(codes_in.at[s], slots_ref.at[s], slots_sem.at[s])

    def assemble(s):
        @pl.when(s != me)
        def _():
            arrival(density, tiles.at[s], tile_send.at[0], tile_recv.at[s]).wait_recv()
            arrival(codes_out, codes_in.at[s], code_send.at[0], code_recv.at[s]).wait_recv()

        slots_copy(s).start()
        arrival(xedge_out, xedge_in.at[s], x_send.at[0], x_recv.at[s]).wait_recv()
        arrival(yedge_out, yedge_in.at[s], y_send.at[0], y_recv.at[s]).wait_recv()
        arrival(yedge_out, corner_in.at[s], c_send.at[0], c_recv.at[s]).wait_recv()
        xe = xedge_in[s].astype(F32)[0:8]
        ye = yedge_in[s].astype(F32)
        ce = corner_in[s].astype(F32)
        ce = jnp.where(natural, jnp.where(col == 0, ce[0:8], ce[8:16]), jnp.where(col == 0, ye[8:16], ye[0:8]))
        inner = pltpu.roll(jnp.where(lane < 64, ye[8:16], ye[0:8]), 4, 1)
        ce = jnp.where((lane >= 2) & (lane < 6), inner, ce)
        ye = jnp.concatenate([ye[0:8], ye[8:16], ce], axis=1)
        start = pl.multiple_of(s * 96 + 48, 16)
        for zp in range(2):
            windows = []
            for z in (2 * zp, 2 * zp + 1):
                whole = tiles[s, z].astype(F32)
                side = jnp.where(col == 0, whole[:, 128:], whole[:, :128])
                inner = pltpu.roll(jnp.where(lane < 64, whole[:, 128:], whole[:, :128]), 4, 1)
                blocks = []
                for i in range(4):
                    p = z * 4 + i
                    edge = pltpu.roll(xe, BX - 2 * p, 1) if p else xe
                    edge = jnp.where(natural, edge, side[i * 8 : i * 8 + 8])
                    edge = jnp.where((lane >= 2) & (lane < 6), inner[i * 8 : i * 8 + 8], edge)
                    blocks.append(jnp.concatenate([whole[i * 8 : i * 8 + 8], edge], axis=1))
                above = jnp.where(gy == 1, pltpu.roll(ye, 8 - 2 * z, 0) if z else ye, 0.0)
                below = jnp.where(gy == 0, pltpu.roll(ye, 6 - 2 * z, 0) if z != 3 else ye, 0.0)
                down = [above] + [pltpu.roll(b, 2, 0) for b in blocks]
                up = [pltpu.roll(b, 6, 0) for b in blocks] + [below]
                held = []
                for i in range(4):
                    held.append(jnp.where(row8 < 2, down[i], down[i + 1]))
                    held.append(jnp.where(row8 < 6, up[i], up[i + 1]))
                windows.append(held)
            strip = None
            for rb in range(8):
                both = jnp.concatenate([windows[0][rb], windows[1][rb]], axis=0)
                w0, w1, ws = both[:, :BX], both[:, BX : 2 * BX], both[:, 2 * BX :]
                r0, r1, rs = pltpu.roll(w0, 1, 1), pltpu.roll(w1, 1, 1), pltpu.roll(ws, 1, 1)
                l0, l1, ls = (pltpu.roll(w, BX - 1, 1) for w in (w0, w1, ws))
                left = jnp.concatenate(
                    [jnp.where(lane == 0, jnp.where(col == 1, rs, 0.0), r0), jnp.where(lane == 0, r0, r1)], axis=1
                )
                right = jnp.concatenate(
                    [jnp.where(lane == BX - 1, l1, l0), jnp.where(lane == BX - 1, jnp.where(col == 0, ls, 0.0), l1)],
                    axis=1,
                )
                for dx, v in enumerate((left, both[:, : 2 * BX], right)):
                    win[rb, pl.ds(start + zp * 48 + dx * 16, 16), :] = v[:, :BX].astype(BF16)
                    win[8 + rb, pl.ds(start + zp * 48 + dx * 16, 16), :] = v[:, BX:].astype(BF16)
                strip = ws if rb == 0 else jnp.where(group == rb, pltpu.roll(ws, 16 * rb, 1), strip)
            for dx, v in enumerate((pltpu.roll(strip, 1, 1), strip, pltpu.roll(strip, BX - 1, 1))):
                strips[pl.ds(start + zp * 48 + dx * 16, 16), :] = v.astype(BF16)

    row16 = iota((16, 1), 0)
    bias2 = jnp.where((iota((32, 1), 0) >> 4) == 0, b2_ref[0], b2_ref[1])

    def convolution(s, bricks, put, at):
        base = (row16 < 3) | ((row16 == 3) & (s == 0)) | ((row16 == 4) & (s == n - 1))
        start = pl.multiple_of(s * 96, 16)
        at_first, at_last = (row16 == 5) & (gy == 0), (row16 == 6) & (gy == 1)

        def hidden_part(first_brick):
            data, flags = [], []
            for b in bricks[first_brick : first_brick + CHUNK]:
                flag = base | (at_first & ((b == 0) | (b == 8))) | (at_last & ((b == 7) | (b == 15)))
                flags.append(jnp.broadcast_to(onehot(flag), (16, BX)))
                data.append(win[b, pl.ds(start, 192), :])
            if first_brick == 0:
                flags.append(onehot(base | (at_first & (group == 0)) | (at_last & (group == 7))))
                data.append(strips[pl.ds(start, 192), :])
            operand = jnp.concatenate(
                [jnp.concatenate(data, axis=1), jnp.concatenate(flags, axis=1)], axis=0
            )
            return jnp.maximum(dot(first[...], operand), 0.0).astype(BF16)

        def fraction_part(first_brick, held):
            total = dot(second[...], held)
            if first_brick == 0:
                t = total[:, CHUNK * BX :]
                for b in range(16):
                    rb, cb = b % 8, b // 8
                    before = pltpu.roll(t[0:32], (BX + 1 - 4 * cb - 16 * rb) % BX, 1)
                    after = pltpu.roll(t[64:96], (BX - 1 - 4 * (1 - cb) - 16 * rb) % BX, 1)
                    at_left = (lane == 0) if cb else (lane == 0) & (col == 1)
                    at_right = (lane == BX - 1) & (col == 0) if cb else lane == BX - 1
                    beside_ref[at * 16 + b] = jnp.where(at_left, before, jnp.where(at_right, after, 0.0))
            for r, b in enumerate(bricks[first_brick : first_brick + CHUNK]):
                t = total[:, r * BX : (r + 1) * BX]
                value = jnp.where(lane == 0, 0.0, pltpu.roll(t[0:32], 1, 1)) + t[32:64]
                value = value + jnp.where(lane == BX - 1, 0.0, pltpu.roll(t[64:96], BX - 1, 1))
                value = value + beside_ref[b + at * 16]
                value = (1.0 / (1.0 + jnp.exp(-(value + bias2)))).astype(BF16)
                put(first_brick + r, value)

        return [
            (functools.partial(hidden_part, i), functools.partial(fraction_part, i))
            for i in range(0, len(bricks), CHUNK)
        ]

    def diffusion(s, at):
        placed = placed_ref[at]
        pore = [placed[q * 8 : q * 8 + 8] for q in range(16)]
        organic = [placed[128 + q * 8 : 136 + q * 8] for q in range(16)]
        carbon = [state[s, pl.ds(q, 8, stride=32), :] for q in range(16)]
        oxygen = [state[s, pl.ds(16 + q, 8, stride=32), :] for q in range(16)]
        weight = [mass[s, pl.ds(q, 8, stride=16), :] for q in range(16)]
        for carbon, oxygen in diffuse_steps(
            carbon, oxygen, pore, organic, weight, iota((8, BX), 1)
        ):
            yield
        for q in range(16):
            state_new[s, pl.ds(q, 8, stride=32), :] = carbon[q]
            state_new[s, pl.ds(16 + q, 8, stride=32), :] = oxygen[q]

    def fractions_of_slots(s, at):
        held = [slots_ref[s, 0, me * 8 + k] for k in range(8)]
        bricks = [jnp.maximum(b, 0) for b in held]
        kept = [jnp.where(b >= 0, 1.0, 0.0) for b in held]

        def put_slot(k, value):
            placed_ref[at, pl.ds(k, 32, stride=8), :] = value.astype(F32) * kept[k]

        return bricks, put_slot

    def received_tile(s, at):
        bricks, put_slot = fractions_of_slots(s, at)
        return convolution(s, bricks, put_slot, at), lambda: None

    def own_tile(s, at):
        def put_own(b, value):
            values_ref[b] = value

        def finish():
            both = [values_ref[8 * cb : 8 * cb + 8].reshape(256, BX) for cb in range(2)]
            whole = dot(order[...], jnp.concatenate(both, axis=1))
            frac[...] = whole.astype(BF16).reshape(frac.shape)
            bricks, put_slot = fractions_of_slots(s, at)
            for k in range(8):
                put_slot(k, values_ref[bricks[k]])

        return convolution(s, list(range(16)), put_own, at), finish

    def process(tiles_and_kinds):
        parts, behind = [], []
        for at, (s, kind) in enumerate(tiles_and_kinds):
            chunks, finish = kind(s, at)
            parts += [(c, None) for c in chunks[:-1]] + [(chunks[-1], (finish, s, at))]
        held = parts[0][0][0]()
        for index, ((_, fraction_part), end) in enumerate(parts):
            later = parts[index + 1][0][0]() if index + 1 < len(parts) else None
            fraction_part(held)
            held = later
            for steps in behind:
                for _ in range(2):
                    next(steps, None)
            if end is not None:
                finish, s, at = end
                finish()
                behind.append(diffusion(s, at))
        for steps in behind:
            for _ in steps:
                pass

    for k in range(1, n - 1):

        @pl.when(k < me)
        def _():
            tile_copy(k).start()

    @pl.when(me > 0)
    def _():
        pl.semaphore_wait(beside, 1)
        for copy in edge_copies(me):
            copy.start()

    for k in range(2, n):

        @pl.when(me < k - 1)
        def _():
            pl.semaphore_wait(ready.at[k], 4)
            tile_copy(k).start()
            code_copy(k).start()
            for copy in edge_copies(k):
                copy.start()

    def source(step):
        return jnp.where(me < n // 2, step, n - 1 - step)

    assemble(source(0))
    load_state.wait()

    s0, s1, s2, s3 = (source(step) for step in range(n))
    assemble(s1)
    slots_copy(s0).wait()

    @pl.when(s0 == me)
    def _():
        process([(s0, own_tile)])

    @pl.when(s0 != me)
    def _():
        process([(s0, received_tile)])

    slots_copy(s1).wait()
    assemble(s3)
    assemble(s2)
    slots_copy(s2).wait()
    slots_copy(s3).wait()

    @pl.when(s1 == me)
    def _():
        process([(s1, own_tile), (s2, received_tile), (s3, received_tile)])

    @pl.when(s1 != me)
    def _():
        process([(s1, received_tile), (s2, received_tile), (s3, received_tile)])


    for k in range(n):

        @pl.when(k != me)
        def _():
            tile_copy(k).wait_send()
            code_copy(k).wait_send()

        for copy in edge_copies(k):
            copy.wait_send()


def column_call(n, groups, density, operands):
    anywhere = pl.BlockSpec(memory_space=pltpu.HBM)
    inside = pl.BlockSpec(memory_space=pltpu.VMEM)
    remote = [pltpu.SemaphoreType.DMA((n,))] * 10
    return pl.pallas_call(
        functools.partial(column_kernel, n),
        out_shape=(
            pltpu.VMEM((2,) + density.shape, BF16),
            pltpu.VMEM((groups, 256, BX), F32),
        ),
        in_specs=[anywhere] * 8,
        out_specs=(inside, inside),
        scratch_shapes=[
            pltpu.VMEM((8, 27), BF16),
            pltpu.SMEM((8,), F32),
            pltpu.VMEM((16, 27), BF16),
            pltpu.SMEM((2,), F32),
            pltpu.SMEM((16,), jnp.int32),
            pltpu.VMEM((n,) + density.shape, BF16),
            pltpu.VMEM((16, BX), BF16),
            pltpu.VMEM((16, BX), BF16),
            pltpu.VMEM((1, BX), jnp.int32),
            pltpu.VMEM((n, 16, BX), BF16),
            pltpu.VMEM((n, 16, BX), BF16),
            pltpu.VMEM((n, 16, BX), BF16),
            pltpu.VMEM((n, 1, BX), jnp.int32),
            pltpu.VMEM((16, (2 * n + 2) * 48, BX), BF16),
            pltpu.VMEM((288, 208), BF16),
            pltpu.VMEM((96, 288), BF16),
            pltpu.VMEM((256, 256), BF16),
            pltpu.VMEM((16, 32, BX), BF16),
            pltpu.VMEM((groups, 256, BX), F32),
            pltpu.VMEM((groups, 128, BX), BF16),
            pltpu.VMEM((groups, 128, BX), F32),
        ] + remote + [pltpu.SemaphoreType.DMA((8,)), pltpu.SemaphoreType.REGULAR((n,)), pltpu.SemaphoreType.REGULAR,
            pltpu.VMEM(((2 * n + 2) * 48, BX), BF16),
            pltpu.VMEM((48, 32, BX), F32),
            pltpu.VMEM((3, 256, BX), F32),
            pltpu.SMEM((n, 1, BX), jnp.int32),
            pltpu.SemaphoreType.DMA((n,)),
        ],
        compiler_params=pltpu.CompilerParams(
            collective_id=1, has_side_effects=True,
            vmem_limit_bytes=(65344 - 128 - groups * 128) * 1024,
        ),
    )(*operands)


def exchange_call(sizes, capacity, groups, density, operands):
    n, slots, per = sizes[0], groups * 8, 8 * capacity
    anywhere = pl.BlockSpec(memory_space=pltpu.HBM)
    inside = pl.BlockSpec(memory_space=pltpu.VMEM)
    return pl.pallas_call(
        functools.partial(kernel, sizes, capacity),
        out_shape=(
            pltpu.VMEM((2,) + density.shape, BF16),
            pltpu.VMEM((groups, 256, BX), F32),
        ),
        in_specs=[anywhere] * 8,
        out_specs=(inside, inside),
        scratch_shapes=[
            pltpu.VMEM((8, 27), BF16),
            pltpu.SMEM((8,), F32),
            pltpu.VMEM((16, 27), BF16),
            pltpu.SMEM((2,), F32),
            pltpu.SMEM((16,), jnp.int32),
            pltpu.VMEM((8, 64, 512), BF16),
            pltpu.VMEM((272, 9 * KR), BF16),
            pltpu.VMEM((3, 192, 272), BF16),
            pltpu.VMEM((8 * 3 * KR, LANES), BF16),
            pltpu.VMEM((6, 272, LANES), BF16),
            pltpu.VMEM((n, 4, per, BX), BF16),
            pltpu.VMEM((n, 4, per, BX), BF16),
            pltpu.VMEM((groups, 256, BX), F32),
            pltpu.VMEM((groups, 128, BX), BF16),
            pltpu.VMEM((groups, 128, BX), F32),
            pltpu.VMEM((32, slots if capacity != 8 else 8, BX), F32),
            pltpu.SemaphoreType.DMA((26,)),
            pltpu.SemaphoreType.DMA((26,)),
            pltpu.SemaphoreType.DMA((n, 4)),
            pltpu.SemaphoreType.DMA((n, 4)),
            pltpu.SemaphoreType.DMA((9,)),
            pltpu.SemaphoreType.DMA((groups,)),
        ],
        compiler_params=pltpu.CompilerParams(
            collective_id=0, has_side_effects=True, vmem_limit_bytes=(65344 - 128 - groups * 128) * 1024
        ),
    )(*operands)


def write_out(frac, state, fractions, solutes_next, sem):
    copies = [
        pltpu.make_async_copy(frac, fractions, sem.at[0]),
        pltpu.make_async_copy(state, solutes_next, sem.at[1]),
    ]
    for copy in copies:
        copy.start()
    for copy in copies:
        copy.wait()


def per_device(
    sizes, density, first_kernel, first_bias, second_kernel, second_bias, owners, solutes, biomass
):
    n = sizes[0]
    slots = solutes.shape[3]
    capacity = slots // n
    anywhere = pl.BlockSpec(memory_space=pltpu.HBM)
    groups = slots // 8
    inside = pl.BlockSpec(memory_space=pltpu.VMEM)
    operands = (
        density,
        first_kernel.transpose(2, 1, 0).reshape(8, 27),
        first_bias,
        second_kernel.transpose(1, 2, 0).reshape(16, 27),
        second_bias,
        owners.reshape(-1),
        solutes.reshape(groups, 256, BX),
        biomass.reshape(groups, 128, BX),
    )
    if sizes == (4, 2, 2) and capacity == 8:
        frac, state_new = column_call(n, groups, density, operands)
    else:
        frac, state_new = exchange_call(sizes, capacity, groups, density, operands)
    fractions, solutes_next = pl.pallas_call(
        write_out,
        out_shape=(
            jax.ShapeDtypeStruct((2,) + density.shape, BF16),
            jax.ShapeDtypeStruct((groups, 256, BX), F32),
        ),
        in_specs=[inside, inside],
        out_specs=(anywhere, anywhere),
        scratch_shapes=[pltpu.SemaphoreType.DMA((2,))],
        compiler_params=pltpu.CompilerParams(vmem_limit_bytes=16 * 1024 * 1024),
    )(frac, state_new)
    return fractions, solutes_next.reshape(solutes.shape)


def solution(mesh):
    sizes = tuple(mesh.shape[axis] for axis in ("gz", "gy", "col"))
    return jax.shard_map(
        functools.partial(per_device, sizes),
        mesh=mesh,
        in_specs=(
            P(("cores", "gz"), "gy", "col"),
            P(),
            P(),
            P(),
            P(),
            P(("cores", "gz"), "gy", "col", None, None),
            P(("cores", "gz"), "gy", "col", None, None, None, None, None),
            P(("cores", "gz"), "gy", "col", None, None, None, None),
        ),
        out_specs=(
            P(None, ("cores", "gz"), "gy", "col"),
            P(("cores", "gz"), "gy", "col", None, None, None, None, None),
        ),
        check_vma=False,
    )
```

```python
import functools
import itertools

import jax
import jax.numpy as jnp
from jax import lax
from jax.experimental import pallas as pl
from jax.experimental.pallas import tpu as pltpu
from jax.sharding import PartitionSpec as P

BY = 4
BX = 128
STEPS = 4
MESH = pl.DeviceIdType.MESH
F32 = jnp.float32
BF16 = jnp.bfloat16
AROUND = [d for d in itertools.product((-1, 0, 1), repeat=3) if d != (0, 0, 0)]
PLACE_Z = {0: (0, 4), 1: (4, 2), -1: (6, 2)}
PLACE_Y = {0: (0, 32), 1: (32, 16), -1: (48, 16)}
PLACE_X = {0: (0, 256), 1: (256, 128), -1: (384, 128)}
TAKE_Z = {0: (0, 4), 1: (0, 2), -1: (2, 2)}
TAKE_Y = {0: (0, 32), 1: (0, 16), -1: (16, 16)}
TAKE_X = {0: (0, 256), 1: (0, 128), -1: (128, 128)}
KR = 48
HR = 34
LANES = 384
CHUNK = 4
OFF = -1e30


def region(ref, tables, offset):
    return ref.at[tuple(pl.ds(*table[o]) for table, o in zip(tables, offset))]


def iota(shape, dim):
    return lax.broadcasted_iota(jnp.int32, shape, dim)


def onehot(condition):
    return jnp.where(condition, 1.0, 0.0).astype(BF16)


def dot(a, b):
    return jnp.dot(a, b, preferred_element_type=F32)


def build_first(w1):
    hidden = w1.shape[0]
    rows, cols = hidden * HR, 9 * KR
    i = iota((rows, 1), 0)
    channel, yi = lax.div(i, HR), lax.rem(i, HR)
    expand = onehot(channel == iota((rows, hidden), 1))
    by_row = dot(expand, w1).astype(BF16)
    j = iota((1, cols), 1)
    tap, r = lax.div(j, KR), lax.rem(j, KR)
    y = jnp.where(r < 40, r, r - KR)
    tap_offset = lax.div(tap, 3) * 9 + lax.rem(tap, 3)
    total = jnp.zeros((rows, cols), F32)
    for dy in range(3):
        pick = onehot(iota((27, cols), 0) == tap_offset + 3 * dy)
        total = total + jnp.where(y == yi + (dy - 2), dot(by_row, pick), 0.0)
    return total.astype(BF16)


def build_second(w2, first_row, last_row):
    hidden = w2.shape[0] // 2
    rows, cols = 192, hidden * HR
    i = iota((rows, 1), 0)
    group, y = lax.div(i, 32), lax.rem(i, 32)
    j = iota((1, cols), 1)
    yi = lax.rem(j, HR)
    inside = jnp.logical_not(((yi == 0) & first_row) | ((yi == HR - 1) & last_row))
    yi = jnp.where(inside, yi, -100)
    pick = onehot(lax.rem(iota((2 * hidden, cols), 0), hidden) == lax.div(j, HR))
    same = lax.rem(group, 2) == lax.div(iota((1, 2 * hidden), 1), hidden)
    blocks = []
    for dz in range(3):
        total = jnp.zeros((rows, cols), F32)
        for dy in range(3):
            select = onehot(iota((rows, 27), 1) == 9 * dz + 3 * dy + lax.div(group, 2))
            values = lax.dot_general(
                select, w2, (((1,), (1,)), ((), ())), preferred_element_type=F32
            )
            values = dot(jnp.where(same, values, 0.0).astype(BF16), pick)
            total = total + jnp.where(yi == y + dy, values, 0.0)
        blocks.append(total.astype(BF16))
    return blocks


def build_placing(owners_ref, slots, capacity):
    count = owners_ref.shape[0]
    target = [owners_ref[b] for b in range(count)]
    j = iota((1, 128), 1)
    brick = ((j & 31) >> 2) * 2 + (j >> 6)
    slot = jnp.zeros((1, 128), jnp.int32)
    for b in range(count):
        rank = jnp.int32(0)
        for other in range(b):
            rank = rank + jnp.where(target[other] == target[b], 1, 0)
        slot = jnp.where(brick == b, target[b] * capacity + rank, slot)
    column = slot * 8 + ((j >> 5) & 1) * 4 + (j & 3)
    i = iota((slots * 8, 1), 0)
    owner = lax.div(i, capacity * 8)
    row = (owner * capacity + lax.rem(i, capacity)) * 8 + lax.rem(lax.div(i, capacity), 8)
    return onehot(row == column)


def diffuse_steps(carbon, oxygen, pore, organic, mass, lane):
    low, high = lane == 0, lane == BX - 1
    pore_c = [0.12 * v for v in pore]
    pore_o = [0.16 * v for v in pore]
    gain = [0.3 * v for v in organic]
    mass = [0.25 * v for v in mass]

    def laplace(field, q):
        z, y = q // 4, q % 4
        v = field[q]
        total = jnp.where(low, v, pltpu.roll(v, 1, 1)) + jnp.where(high, v, pltpu.roll(v, BX - 1, 1))
        near = 2
        for ok, at in ((z > 0, q - 4), (z < 3, q + 4), (y > 0, q - 1), (y < 3, q + 1)):
            if ok:
                total = total + field[at]
                near += 1
        return total - float(near) * v

    for _ in range(STEPS):
        carbon_new, oxygen_new = [], []
        for q in range(16):
            c, o = carbon[q], oxygen[q]
            uptake = mass[q] * c * o / ((0.5 + jnp.abs(c)) * (0.3 + jnp.abs(o)))
            carbon_new.append(c + pore_c[q] * laplace(carbon, q) + gain[q] - uptake)
            oxygen_new.append(o + pore_o[q] * laplace(oxygen, q) - uptake)
        carbon, oxygen = carbon_new, oxygen_new
        yield carbon, oxygen


def diffuse(*fields):
    *_, last = diffuse_steps(*fields)
    return last


def kernel(
    sizes, capacity,
    density, w1_hbm, b1_hbm, w2_hbm, b2_hbm, owners_hbm, solutes, biomass,
    frac, state_new,
    w1_ref, b1_ref, w2_ref, b2_ref, owners_ref, tile, first, second, shifted, hidden, out, arrived, state, mass_in, mass, gathered,
    halo_send, halo_recv, brick_send, brick_recv, local_sem, group_sem,
):
    n, n_gy, n_col = sizes
    slots = n * capacity
    here = (lax.axis_index("gz"), lax.axis_index("gy"), lax.axis_index("col"))
    me = here[0]

    def exists(offset):
        ok = None
        for position, size, o in zip(here, sizes, offset):
            test = None if o == 0 else (position + o >= 0) & (position + o < size)
            ok = test if ok is None else ok if test is None else ok & test
        return ok

    def device(offset):
        return {"gz": here[0] + offset[0], "gy": here[1] + offset[1], "col": here[2] + offset[2]}

    def halo(offset, index, receiver):
        seen = tuple(-o for o in offset) if not receiver else offset
        return pltpu.make_async_remote_copy(
            src_ref=region(density, (TAKE_Z, TAKE_Y, TAKE_X), seen),
            dst_ref=region(tile, (PLACE_Z, PLACE_Y, PLACE_X), seen),
            send_sem=halo_send.at[index],
            recv_sem=halo_recv.at[AROUND.index(seen)],
            device_id=device(offset),
            device_id_type=MESH,
        )

    small = [
        pltpu.make_async_copy(source, target, local_sem.at[4 + i])
        for i, (source, target) in enumerate(
            (
                (w1_hbm, w1_ref), (w2_hbm, w2_ref), (b1_hbm, b1_ref), (b2_hbm, b2_ref),
                (owners_hbm, owners_ref),
            )
        )
    ]
    for copy in small:
        copy.start()
    tile[...] = jnp.zeros_like(tile)
    barrier = pltpu.get_barrier_semaphore()
    expected = jnp.int32(n - 1)
    for offset in AROUND:
        ok = exists(offset)
        expected = expected + jnp.where(ok, 1, 0)

        @pl.when(ok)
        def _():
            pl.semaphore_signal(barrier, inc=1, device_id=device(offset), device_id_type=MESH)

    for j in range(1, n):
        pl.semaphore_signal(
            barrier, inc=1, device_id={"gz": lax.rem(me + j, n)}, device_id_type=MESH
        )
    own = pltpu.make_async_copy(
        density, region(tile, (PLACE_Z, PLACE_Y, PLACE_X), (0, 0, 0)), local_sem.at[0]
    )
    own.start()
    load_state = pltpu.make_async_copy(solutes, state, local_sem.at[1])
    load_mass = pltpu.make_async_copy(biomass, mass_in, local_sem.at[2])
    pl.semaphore_wait(barrier, expected)

    for index, offset in enumerate(AROUND):

        @pl.when(exists(offset))
        def _():
            halo(offset, index, False).start()

    load_state.start()
    load_mass.start()

    for copy in small:
        copy.wait()
    first[...] = build_first(w1_ref[...])
    for dz, block in enumerate(build_second(w2_ref[...], here[1] == 0, here[1] == n_gy - 1)):
        second[dz] = block
    placing = build_placing(owners_ref, slots, capacity)
    channel = lax.div(iota((272, 1), 0), HR)
    bias1 = jnp.zeros((272, 1), F32)
    for o in range(8):
        bias1 = jnp.where(channel == o, b1_ref[o], bias1)
    bias2 = jnp.where(iota((64, 1), 0) < 32, b2_ref[0], b2_ref[1])
    lane = iota((1, BX), 1)
    keep = jnp.where(
        ((lane == 0) & (here[2] < n_col - 1)) | ((lane == BX - 1) & (here[2] > 0)), 1.0, 0.0
    )
    load_mass.wait()
    for g in range(slots // 8):
        mass[g] = mass_in[g].astype(F32)

    own.wait()
    for index, offset in enumerate(AROUND):

        @pl.when(exists(offset))
        def _():
            halo(offset, index, True).wait_recv()

    half_row = iota((16, 512), 0) < 8
    half_lane = iota((KR, BX), 1) < 64
    for zz in range(8):
        z = (zz + 6) % 8
        side = jnp.where(half_row, tile[z, 32:48, :].astype(F32), tile[z, 48:64, :].astype(F32))
        whole = jnp.concatenate([tile[z, 0:32, :].astype(F32), side], axis=0)
        edge = jnp.where(half_lane, whole[:, 256:384], whole[:, 384:512])
        whole = jnp.concatenate([whole[:, :256], edge], axis=1)
        base = zz * 3 * KR
        shifted[base : base + KR, :] = pltpu.roll(whole, 1, 1).astype(BF16)
        shifted[base + KR : base + 2 * KR, :] = whole.astype(BF16)
        shifted[base + 2 * KR : base + 3 * KR, :] = pltpu.roll(whole, LANES - 1, 1).astype(BF16)

    def hidden_slice(zi):
        value = dot(first[...], shifted[zi * 3 * KR : (zi + 3) * 3 * KR, :])
        value = jnp.maximum(value + bias1, 0.0)
        hidden[zi, :, 0:256] = value[:, :256].astype(BF16)
        hidden[zi, :, 256:384] = (value[:, 256:] * keep).astype(BF16)

    def brick_copy(j, z):
        to = lax.rem(me + j, n)
        return pltpu.make_async_remote_copy(
            src_ref=out.at[to, z],
            dst_ref=arrived.at[me, z],
            send_sem=brick_send.at[j, z],
            recv_sem=brick_recv.at[j, z],
            device_id={"gz": to},
            device_id_type=MESH,
        )

    hidden_slice(0)

    @pl.when(me == 0)
    def _():
        hidden[0] = jnp.zeros_like(hidden[0])

    hidden_slice(1)
    per = 8 * capacity
    for z in range(4):
        hidden_slice(z + 2)
        if z == 3:

            @pl.when(me == n - 1)
            def _():
                hidden[5] = jnp.zeros_like(hidden[5])

        total = jnp.zeros((192, LANES), F32)
        for dz in range(3):
            total = total + dot(second[dz], hidden[z + dz])
        value = (
            pltpu.roll(total[0:64], 1, 1) + total[64:128] + pltpu.roll(total[128:192], LANES - 1, 1)
        )[:, :256]
        value = (1.0 / (1.0 + jnp.exp(-(value + bias2)))).astype(BF16)
        frac[0, z] = value[:32]
        frac[1, z] = value[32:]
        placed = dot(placing, jnp.concatenate([value[:, :128], value[:, 128:]], axis=0)).astype(BF16)
        for d in range(n):
            out[d, z] = placed[d * per : (d + 1) * per]
        for j in range(1, n):
            brick_copy(j, z).start()

    load_state.wait()

    def received(j, z):
        source = lax.rem(me - j + n, n)
        pltpu.make_async_remote_copy(
            src_ref=out.at[source, z],
            dst_ref=arrived.at[source, z],
            send_sem=brick_send.at[j, z],
            recv_sem=brick_recv.at[j, z],
            device_id={"gz": source},
            device_id_type=MESH,
        ).wait_recv()


    def group(g, pore, organic):
        carbon = [state[g, pl.ds(q, 8, stride=32), :] for q in range(16)]
        oxygen = [state[g, pl.ds(16 + q, 8, stride=32), :] for q in range(16)]
        held = [mass[g, pl.ds(q, 8, stride=16), :] for q in range(16)]
        carbon, oxygen = diffuse(carbon, oxygen, pore, organic, held, iota((8, BX), 1))
        for q in range(16):
            state_new[g, pl.ds(q, 8, stride=32), :] = carbon[q]
            state_new[g, pl.ds(16 + q, 8, stride=32), :] = oxygen[q]

    if capacity == 8:
        for j in range(n):
            source = lax.rem(me - j + n, n)
            values = [[None] * 16, [None] * 16]
            for z in range(4):
                if j:
                    received(j, z)
                ref = arrived if j else out
                for o in range(2):
                    for pair in range(2):
                        at = o * 32 + pair * 16
                        both = ref[source, z, at : at + 16, :].astype(F32)
                        values[o][z * 4 + pair * 2] = both[:8]
                        values[o][z * 4 + pair * 2 + 1] = both[8:]
            group(source, *values)
    else:
        for z in range(4):
            arrived[me, z] = out[me, z]
        for j in range(1, n):
            for z in range(4):
                received(j, z)
        for s in range(n):
            for z in range(4):
                block = arrived[s, z].astype(F32)
                for o in range(2):
                    for y in range(4):
                        at = (o * 4 + y) * capacity
                        gathered[o * 16 + z * 4 + y, s * capacity : (s + 1) * capacity, :] = block[
                            at : at + capacity
                        ]

        @pl.loop(0, slots // 8)
        def _(g):
            start = pl.multiple_of(g * 8, 8)
            group(
                g,
                [gathered[q, pl.ds(start, 8), :] for q in range(16)],
                [gathered[16 + q, pl.ds(start, 8), :] for q in range(16)],
            )

    for index, offset in enumerate(AROUND):

        @pl.when(exists(offset))
        def _():
            halo(offset, index, False).wait_send()

    for j in range(1, n):
        for z in range(4):
            brick_copy(j, z).wait_send()


def build_first_block(w1, b1_ref):
    rows, cols = 288, 192
    m = iota((rows, 1), 0)
    zh, yh, channel = lax.div(m, 48), lax.rem(lax.div(m, 8), 6), m & 7
    by_row = dot(onehot(channel == iota((rows, 8), 1)), w1).astype(BF16)
    k = iota((1, cols), 1)
    pair, dx, part = lax.div(k, 48), lax.rem(lax.div(k, 16), 3), k & 15
    z, y = pair * 2 + (part >> 3), part & 7
    total = jnp.zeros((rows, cols), F32)
    for dz in range(3):
        for dy in range(3):
            pick = onehot(iota((27, cols), 0) == 9 * dz + 3 * dy + dx)
            total = total + jnp.where((z == zh + dz) & (y == yh + dy), dot(by_row, pick), 0.0)
    bias = jnp.zeros((rows, 1), F32)
    for o in range(8):
        bias = jnp.where(channel == o, b1_ref[o], bias)
    high = bias.astype(BF16).astype(F32)
    middle = (bias - high).astype(BF16).astype(F32)
    low = bias - high - middle
    c = iota((1, 16), 1)
    extra = jnp.where(c == 0, high, jnp.where(c == 1, middle, jnp.where(c == 2, low, 0.0)))
    off = (
        ((c == 3) & (zh == 0)) | ((c == 4) & (zh == 5)) | ((c == 5) & (yh == 0))
        | ((c == 6) & (yh == 5)) | (c == 7)
    )
    extra = jnp.where(off, OFF, extra)
    return total.astype(BF16), extra.astype(BF16)


def build_second_block(w2):
    rows, cols = 96, 288
    m = iota((rows, 1), 0)
    dx, o, z, y = lax.div(m, 32), (m >> 4) & 1, (m >> 2) & 3, m & 3
    k = iota((1, cols), 1)
    zh, yh, channel = lax.div(k, 48), lax.rem(lax.div(k, 8), 6), k & 7
    pick = onehot((iota((16, cols), 0) & 7) == channel)
    same = o == (iota((1, 16), 1) >> 3)
    total = jnp.zeros((rows, cols), F32)
    for dz in range(3):
        for dy in range(3):
            select = onehot(iota((rows, 27), 1) == 9 * dz + 3 * dy + dx)
            values = lax.dot_general(
                select, w2, (((1,), (1,)), ((), ())), preferred_element_type=F32
            )
            values = dot(jnp.where(same, values, 0.0).astype(BF16), pick)
            total = total + jnp.where((zh == z + dz) & (yh == y + dy), values, 0.0)
    return total.astype(BF16)


def build_codes(owners_ref, capacity):
    target = [owners_ref[b] for b in range(16)]
    lane = iota((1, 128), 1)
    bricks = jnp.full((1, 128), -1, jnp.int32)
    for b in range(16):
        rank = jnp.int32(0)
        for other in range(b):
            rank = rank + jnp.where(target[other] == target[b], 1, 0)
        bricks = jnp.where(lane == target[b] * capacity + rank, (b % 2) * 8 + b // 2, bricks)
    return bricks


def column_kernel(
    n,
    density, w1_hbm, b1_hbm, w2_hbm, b2_hbm, owners_hbm, solutes, biomass,
    frac, state_new,
    w1_ref, b1_ref, w2_ref, b2_ref, owners_ref, tiles, yedge_out, xedge_out, codes_out,
    yedge_in, xedge_in, corner_in, codes_in, win, first, second, order, values_ref,
    state, mass_in, mass,
    tile_send, tile_recv, code_send, code_recv, y_send, y_recv, x_send, x_recv, c_send, c_recv,
    local_sem, ready, beside, strips, beside_ref, placed_ref, slots_ref, slots_sem,
):
    me, gy, col = lax.axis_index("gz"), lax.axis_index("gy"), lax.axis_index("col")
    small = [
        pltpu.make_async_copy(source, target, local_sem.at[3 + i])
        for i, (source, target) in enumerate(
            (
                (w1_hbm, w1_ref), (w2_hbm, w2_ref), (b1_hbm, b1_ref), (b2_hbm, b2_ref),
                (owners_hbm, owners_ref),
            )
        )
    ]
    own = pltpu.make_async_copy(density, tiles.at[me], local_sem.at[0])
    own.start()
    for copy in small:
        copy.start()
    barrier = pltpu.get_barrier_semaphore()

    across = ({"gy": 1 - gy}, {"col": 1 - col}, {"gy": 1 - gy, "col": 1 - col})
    @pl.when(me == 0)
    def _():
        for where in across:
            pl.semaphore_signal(barrier, inc=1, device_id=where, device_id_type=MESH)

    for k in range(1, n):

        @pl.when(me < k)
        def _():
            for where in ({},) + across:
                pl.semaphore_signal(barrier, inc=1, device_id={"gz": k, **where}, device_id_type=MESH)

    load_state = pltpu.make_async_copy(solutes, state, local_sem.at[1])
    load_mass = pltpu.make_async_copy(biomass, mass_in, local_sem.at[2])

    def tile_copy(k):
        return pltpu.make_async_remote_copy(
            src_ref=density, dst_ref=tiles.at[me], send_sem=tile_send.at[k], recv_sem=tile_recv.at[me],
            device_id={"gz": k}, device_id_type=MESH,
        )

    def code_copy(k):
        return pltpu.make_async_remote_copy(
            src_ref=codes_out, dst_ref=codes_in.at[me], send_sem=code_send.at[k],
            recv_sem=code_recv.at[me], device_id={"gz": k}, device_id_type=MESH,
        )

    def edge_copy(k, source, target, send, recv, across):
        return pltpu.make_async_remote_copy(
            src_ref=source, dst_ref=target.at[me], send_sem=send.at[k], recv_sem=recv.at[me],
            device_id={"gz": k, **across}, device_id_type=MESH,
        )

    def edge_copies(k):
        return (
            edge_copy(k, xedge_out, xedge_in, x_send, x_recv, {"col": 1 - col}),
            edge_copy(k, yedge_out, yedge_in, y_send, y_recv, {"gy": 1 - gy}),
            edge_copy(k, yedge_out, corner_in, c_send, c_recv, {"gy": 1 - gy, "col": 1 - col}),
        )

    def arrival(source, target, send, recv):
        return pltpu.make_async_remote_copy(
            src_ref=source, dst_ref=target, send_sem=send, recv_sem=recv,
            device_id={"col": 1 - col}, device_id_type=MESH,
        )

    pl.semaphore_wait(barrier, jnp.where(me == 0, 3, 4 * me))
    for k in range(n - 1):

        @pl.when(k < me)
        def _():
            if k == 0:
                tile_copy(k).start()
            for where in ({},) + across:
                pl.semaphore_signal(ready.at[me], inc=1, device_id={"gz": k, **where}, device_id_type=MESH)

    row8 = iota((8, 1), 0)
    lane = iota((1, BX), 1)

    own.wait()
    packed = jnp.zeros((8, 256), F32)
    for z in range(4):
        top = tiles[me, z, 0:16, :].astype(F32)[0:8]
        bottom = tiles[me, z, 16:32, :].astype(F32)[8:16]
        pair = jnp.where(gy == 0, pltpu.roll(bottom, 2, 0), top)
        packed = jnp.where((row8 >> 1) == z, pltpu.roll(pair, 2 * z, 0) if z else pair, packed)
    yedge_out[...] = jnp.concatenate([packed[:, :128], packed[:, 128:]], axis=0).astype(BF16)
    packed = jnp.zeros((8, BX), F32)
    place = ((lane + jnp.where(col == 0, 2, 0)) & (BX - 1)) >> 1
    for z in range(4):
        whole = tiles[me, z].astype(F32)
        side = jnp.where(col == 0, whole[:, 128:], whole[:, :128])
        for i in range(4):
            p = z * 4 + i
            block = side[i * 8 : i * 8 + 8]
            packed = jnp.where(place == p, pltpu.roll(block, 2 * p, 1) if p else block, packed)
    xedge_out[...] = jnp.concatenate([packed, packed], axis=0).astype(BF16)
    for k in range(n):

        @pl.when((k < me) | (me + k == 0))
        def _():
            for copy in edge_copies(k):
                copy.start()

    for copy in small:
        copy.wait()
    codes_out[...] = build_codes(owners_ref, 8)
    codes_in[me] = codes_out[...]
    for k in range(n - 1):

        @pl.when(k < me)
        def _():
            code_copy(k).start()

    load_state.start()
    load_mass.start()

    banded, extra = build_first_block(w1_ref[...], b1_ref)
    first[:, 0:192] = banded
    first[:, 192:208] = extra

    @pl.when(me < n - 1)
    def _():
        pl.semaphore_wait(ready.at[me + 1], 4)
        pl.semaphore_signal(beside, inc=1, device_id={"gz": me + 1}, device_id_type=MESH)
        tile_copy(me + 1).start()
        code_copy(me + 1).start()
        for copy in edge_copies(me + 1):
            copy.start()

    second[...] = build_second_block(w2_ref[...])
    i = iota((256, 1), 0)
    j = iota((1, 256), 1)
    wanted = (lax.rem(i, 32) >> 2) * 32 + (i >> 5) * 4 + (i & 3)
    order[...] = onehot(wanted == j)
    for first_row in (0, (2 * n + 1) * 48):
        win[:, first_row : first_row + 48, :] = jnp.zeros((16, 48, BX), BF16)
        strips[first_row : first_row + 48, :] = jnp.zeros((48, BX), BF16)
    load_mass.wait()
    for g in range(n):
        mass[g] = mass_in[g].astype(F32)
    group = ((lane + 8) & (BX - 1)) >> 4
    natural = ((lane < 2) & (col == 0)) | ((lane >= BX - 2) & (col == 1))

    def slots_copy(s):
        return pltpu.make_async_copy(codes_in.at[s], slots_ref.at[s], slots_sem.at[s])

    def assemble(s):
        @pl.when(s != me)
        def _():
            arrival(density, tiles.at[s], tile_send.at[0], tile_recv.at[s]).wait_recv()
            arrival(codes_out, codes_in.at[s], code_send.at[0], code_recv.at[s]).wait_recv()

        slots_copy(s).start()
        arrival(xedge_out, xedge_in.at[s], x_send.at[0], x_recv.at[s]).wait_recv()
        arrival(yedge_out, yedge_in.at[s], y_send.at[0], y_recv.at[s]).wait_recv()
        arrival(yedge_out, corner_in.at[s], c_send.at[0], c_recv.at[s]).wait_recv()
        xe = xedge_in[s].astype(F32)[0:8]
        ye = yedge_in[s].astype(F32)
        ce = corner_in[s].astype(F32)
        ce = jnp.where(natural, jnp.where(col == 0, ce[0:8], ce[8:16]), jnp.where(col == 0, ye[8:16], ye[0:8]))
        inner = pltpu.roll(jnp.where(lane < 64, ye[8:16], ye[0:8]), 4, 1)
        ce = jnp.where((lane >= 2) & (lane < 6), inner, ce)
        ye = jnp.concatenate([ye[0:8], ye[8:16], ce], axis=1)
        start = pl.multiple_of(s * 96 + 48, 16)
        for zp in range(2):
            windows = []
            for z in (2 * zp, 2 * zp + 1):
                whole = tiles[s, z].astype(F32)
                side = jnp.where(col == 0, whole[:, 128:], whole[:, :128])
                inner = pltpu.roll(jnp.where(lane < 64, whole[:, 128:], whole[:, :128]), 4, 1)
                blocks = []
                for i in range(4):
                    p = z * 4 + i
                    edge = pltpu.roll(xe, BX - 2 * p, 1) if p else xe
                    edge = jnp.where(natural, edge, side[i * 8 : i * 8 + 8])
                    edge = jnp.where((lane >= 2) & (lane < 6), inner[i * 8 : i * 8 + 8], edge)
                    blocks.append(jnp.concatenate([whole[i * 8 : i * 8 + 8], edge], axis=1))
                above = jnp.where(gy == 1, pltpu.roll(ye, 8 - 2 * z, 0) if z else ye, 0.0)
                below = jnp.where(gy == 0, pltpu.roll(ye, 6 - 2 * z, 0) if z != 3 else ye, 0.0)
                down = [above] + [pltpu.roll(b, 2, 0) for b in blocks]
                up = [pltpu.roll(b, 6, 0) for b in blocks] + [below]
                held = []
                for i in range(4):
                    held.append(jnp.where(row8 < 2, down[i], down[i + 1]))
                    held.append(jnp.where(row8 < 6, up[i], up[i + 1]))
                windows.append(held)
            strip = None
            for rb in range(8):
                both = jnp.concatenate([windows[0][rb], windows[1][rb]], axis=0)
                w0, w1, ws = both[:, :BX], both[:, BX : 2 * BX], both[:, 2 * BX :]
                r0, r1, rs = pltpu.roll(w0, 1, 1), pltpu.roll(w1, 1, 1), pltpu.roll(ws, 1, 1)
                l0, l1, ls = (pltpu.roll(w, BX - 1, 1) for w in (w0, w1, ws))
                left = jnp.concatenate(
                    [jnp.where(lane == 0, jnp.where(col == 1, rs, 0.0), r0), jnp.where(lane == 0, r0, r1)], axis=1
                )
                right = jnp.concatenate(
                    [jnp.where(lane == BX - 1, l1, l0), jnp.where(lane == BX - 1, jnp.where(col == 0, ls, 0.0), l1)],
                    axis=1,
                )
                for dx, v in enumerate((left, both[:, : 2 * BX], right)):
                    win[rb, pl.ds(start + zp * 48 + dx * 16, 16), :] = v[:, :BX].astype(BF16)
                    win[8 + rb, pl.ds(start + zp * 48 + dx * 16, 16), :] = v[:, BX:].astype(BF16)
                strip = ws if rb == 0 else jnp.where(group == rb, pltpu.roll(ws, 16 * rb, 1), strip)
            for dx, v in enumerate((pltpu.roll(strip, 1, 1), strip, pltpu.roll(strip, BX - 1, 1))):
                strips[pl.ds(start + zp * 48 + dx * 16, 16), :] = v.astype(BF16)

    row16 = iota((16, 1), 0)
    bias2 = jnp.where((iota((32, 1), 0) >> 4) == 0, b2_ref[0], b2_ref[1])

    def convolution(s, bricks, put, at):
        base = (row16 < 3) | ((row16 == 3) & (s == 0)) | ((row16 == 4) & (s == n - 1))
        start = pl.multiple_of(s * 96, 16)
        at_first, at_last = (row16 == 5) & (gy == 0), (row16 == 6) & (gy == 1)

        def hidden_part(first_brick):
            data, flags = [], []
            for b in bricks[first_brick : first_brick + CHUNK]:
                flag = base | (at_first & ((b == 0) | (b == 8))) | (at_last & ((b == 7) | (b == 15)))
                flags.append(jnp.broadcast_to(onehot(flag), (16, BX)))
                data.append(win[b, pl.ds(start, 192), :])
            if first_brick == 0:
                flags.append(onehot(base | (at_first & (group == 0)) | (at_last & (group == 7))))
                data.append(strips[pl.ds(start, 192), :])
            operand = jnp.concatenate(
                [jnp.concatenate(data, axis=1), jnp.concatenate(flags, axis=1)], axis=0
            )
            return jnp.maximum(dot(first[...], operand), 0.0).astype(BF16)

        def fraction_part(first_brick, held):
            total = dot(second[...], held)
            if first_brick == 0:
                t = total[:, CHUNK * BX :]
                for b in range(16):
                    rb, cb = b % 8, b // 8
                    before = pltpu.roll(t[0:32], (BX + 1 - 4 * cb - 16 * rb) % BX, 1)
                    after = pltpu.roll(t[64:96], (BX - 1 - 4 * (1 - cb) - 16 * rb) % BX, 1)
                    at_left = (lane == 0) if cb else (lane == 0) & (col == 1)
                    at_right = (lane == BX - 1) & (col == 0) if cb else lane == BX - 1
                    beside_ref[at * 16 + b] = jnp.where(at_left, before, jnp.where(at_right, after, 0.0))
            for r, b in enumerate(bricks[first_brick : first_brick + CHUNK]):
                t = total[:, r * BX : (r + 1) * BX]
                value = jnp.where(lane == 0, 0.0, pltpu.roll(t[0:32], 1, 1)) + t[32:64]
                value = value + jnp.where(lane == BX - 1, 0.0, pltpu.roll(t[64:96], BX - 1, 1))
                value = value + beside_ref[b + at * 16]
                value = (1.0 / (1.0 + jnp.exp(-(value + bias2)))).astype(BF16)
                put(first_brick + r, value)

        return [
            (functools.partial(hidden_part, i), functools.partial(fraction_part, i))
            for i in range(0, len(bricks), CHUNK)
        ]

    def diffusion(s, at):
        placed = placed_ref[at]
        pore = [placed[q * 8 : q * 8 + 8] for q in range(16)]
        organic = [placed[128 + q * 8 : 136 + q * 8] for q in range(16)]
        carbon = [state[s, pl.ds(q, 8, stride=32), :] for q in range(16)]
        oxygen = [state[s, pl.ds(16 + q, 8, stride=32), :] for q in range(16)]
        weight = [mass[s, pl.ds(q, 8, stride=16), :] for q in range(16)]
        for carbon, oxygen in diffuse_steps(
            carbon, oxygen, pore, organic, weight, iota((8, BX), 1)
        ):
            yield
        for q in range(16):
            state_new[s, pl.ds(q, 8, stride=32), :] = carbon[q]
            state_new[s, pl.ds(16 + q, 8, stride=32), :] = oxygen[q]

    def fractions_of_slots(s, at):
        held = [slots_ref[s, 0, me * 8 + k] for k in range(8)]
        bricks = [jnp.maximum(b, 0) for b in held]
        kept = [jnp.where(b >= 0, 1.0, 0.0) for b in held]

        def put_slot(k, value):
            placed_ref[at, pl.ds(k, 32, stride=8), :] = value.astype(F32) * kept[k]

        return bricks, put_slot

    def received_tile(s, at):
        bricks, put_slot = fractions_of_slots(s, at)
        return convolution(s, bricks, put_slot, at), lambda: None

    def own_tile(s, at):
        def put_own(b, value):
            values_ref[b] = value

        def finish():
            both = [values_ref[8 * cb : 8 * cb + 8].reshape(256, BX) for cb in range(2)]
            whole = dot(order[...], jnp.concatenate(both, axis=1))
            frac[...] = whole.astype(BF16).reshape(frac.shape)
            bricks, put_slot = fractions_of_slots(s, at)
            for k in range(8):
                put_slot(k, values_ref[bricks[k]])

        return convolution(s, list(range(16)), put_own, at), finish

    def process(tiles_and_kinds, at=0, pending=(), last=True):
        parts, behind = [], [diffusion(*p) for p in pending]
        for at, (s, kind) in enumerate(tiles_and_kinds, at):
            chunks, finish = kind(s, at)
            parts += [(c, None) for c in chunks[:-1]] + [(chunks[-1], (finish, s, at))]
        held = parts[0][0][0]()
        for index, ((_, fraction_part), end) in enumerate(parts):
            later = parts[index + 1][0][0]() if index + 1 < len(parts) else None
            fraction_part(held)
            held = later
            for steps in behind:
                for _ in range(2):
                    next(steps, None)
            if end is not None:
                finish, s, at = end
                finish()
                if last:
                    behind.append(diffusion(s, at))
        for steps in behind:
            for _ in steps:
                pass

    @pl.when(me > 0)
    def _():
        pl.semaphore_wait(beside, 1)
        for copy in edge_copies(me):
            copy.start()

    for k in range(2, n):

        @pl.when(me < k - 1)
        def _():
            pl.semaphore_wait(ready.at[k], 4)
            tile_copy(k).start()
            code_copy(k).start()
            for copy in edge_copies(k):
                copy.start()

    @pl.when(me > 0)
    def _():
        tile_copy(0).wait_send()

    for k in range(1, n - 1):

        @pl.when(k < me)
        def _():
            tile_copy(k).start()

    def source(step):
        return jnp.where(me < n // 2, step, n - 1 - step)

    assemble(source(0))
    load_state.wait()

    s0, s1, s2, s3 = (source(step) for step in range(n))
    assemble(s1)
    slots_copy(s0).wait()

    @pl.when(s0 == me)
    def _():
        process([(s0, own_tile)], at=3, last=False)

    @pl.when(s0 != me)
    def _():
        process([(s0, received_tile)], at=3, last=False)

    slots_copy(s1).wait()
    assemble(s3)
    assemble(s2)
    slots_copy(s2).wait()
    slots_copy(s3).wait()

    @pl.when(s1 == me)
    def _():
        process([(s1, own_tile), (s2, received_tile), (s3, received_tile)], pending=[(s0, 3)])

    @pl.when(s1 != me)
    def _():
        process([(s1, received_tile), (s2, received_tile), (s3, received_tile)], pending=[(s0, 3)])


    for k in range(n):

        @pl.when(k != me)
        def _():
            if k:
                tile_copy(k).wait_send()
            code_copy(k).wait_send()

        for copy in edge_copies(k):
            copy.wait_send()


def column_call(n, groups, density, operands):
    anywhere = pl.BlockSpec(memory_space=pltpu.HBM)
    inside = pl.BlockSpec(memory_space=pltpu.VMEM)
    remote = [pltpu.SemaphoreType.DMA((n,))] * 10
    return pl.pallas_call(
        functools.partial(column_kernel, n),
        out_shape=(
            pltpu.VMEM((2,) + density.shape, BF16),
            pltpu.VMEM((groups, 256, BX), F32),
        ),
        in_specs=[anywhere] * 8,
        out_specs=(inside, inside),
        scratch_shapes=[
            pltpu.VMEM((8, 27), BF16),
            pltpu.SMEM((8,), F32),
            pltpu.VMEM((16, 27), BF16),
            pltpu.SMEM((2,), F32),
            pltpu.SMEM((16,), jnp.int32),
            pltpu.VMEM((n,) + density.shape, BF16),
            pltpu.VMEM((16, BX), BF16),
            pltpu.VMEM((16, BX), BF16),
            pltpu.VMEM((1, BX), jnp.int32),
            pltpu.VMEM((n, 16, BX), BF16),
            pltpu.VMEM((n, 16, BX), BF16),
            pltpu.VMEM((n, 16, BX), BF16),
            pltpu.VMEM((n, 1, BX), jnp.int32),
            pltpu.VMEM((16, (2 * n + 2) * 48, BX), BF16),
            pltpu.VMEM((288, 208), BF16),
            pltpu.VMEM((96, 288), BF16),
            pltpu.VMEM((256, 256), BF16),
            pltpu.VMEM((16, 32, BX), BF16),
            pltpu.VMEM((groups, 256, BX), F32),
            pltpu.VMEM((groups, 128, BX), BF16),
            pltpu.VMEM((groups, 128, BX), F32),
        ] + remote + [pltpu.SemaphoreType.DMA((8,)), pltpu.SemaphoreType.REGULAR((n,)), pltpu.SemaphoreType.REGULAR,
            pltpu.VMEM(((2 * n + 2) * 48, BX), BF16),
            pltpu.VMEM((64, 32, BX), F32),
            pltpu.VMEM((4, 256, BX), F32),
            pltpu.SMEM((n, 1, BX), jnp.int32),
            pltpu.SemaphoreType.DMA((n,)),
        ],
        compiler_params=pltpu.CompilerParams(
            collective_id=1, has_side_effects=True,
            vmem_limit_bytes=(65344 - 128 - groups * 128) * 1024,
        ),
    )(*operands)


def exchange_call(sizes, capacity, groups, density, operands):
    n, slots, per = sizes[0], groups * 8, 8 * capacity
    anywhere = pl.BlockSpec(memory_space=pltpu.HBM)
    inside = pl.BlockSpec(memory_space=pltpu.VMEM)
    return pl.pallas_call(
        functools.partial(kernel, sizes, capacity),
        out_shape=(
            pltpu.VMEM((2,) + density.shape, BF16),
            pltpu.VMEM((groups, 256, BX), F32),
        ),
        in_specs=[anywhere] * 8,
        out_specs=(inside, inside),
        scratch_shapes=[
            pltpu.VMEM((8, 27), BF16),
            pltpu.SMEM((8,), F32),
            pltpu.VMEM((16, 27), BF16),
            pltpu.SMEM((2,), F32),
            pltpu.SMEM((16,), jnp.int32),
            pltpu.VMEM((8, 64, 512), BF16),
            pltpu.VMEM((272, 9 * KR), BF16),
            pltpu.VMEM((3, 192, 272), BF16),
            pltpu.VMEM((8 * 3 * KR, LANES), BF16),
            pltpu.VMEM((6, 272, LANES), BF16),
            pltpu.VMEM((n, 4, per, BX), BF16),
            pltpu.VMEM((n, 4, per, BX), BF16),
            pltpu.VMEM((groups, 256, BX), F32),
            pltpu.VMEM((groups, 128, BX), BF16),
            pltpu.VMEM((groups, 128, BX), F32),
            pltpu.VMEM((32, slots if capacity != 8 else 8, BX), F32),
            pltpu.SemaphoreType.DMA((26,)),
            pltpu.SemaphoreType.DMA((26,)),
            pltpu.SemaphoreType.DMA((n, 4)),
            pltpu.SemaphoreType.DMA((n, 4)),
            pltpu.SemaphoreType.DMA((9,)),
            pltpu.SemaphoreType.DMA((groups,)),
        ],
        compiler_params=pltpu.CompilerParams(
            collective_id=0, has_side_effects=True, vmem_limit_bytes=(65344 - 128 - groups * 128) * 1024
        ),
    )(*operands)


def write_out(frac, state, fractions, solutes_next, sem):
    copies = [
        pltpu.make_async_copy(frac, fractions, sem.at[0]),
        pltpu.make_async_copy(state, solutes_next, sem.at[1]),
    ]
    for copy in copies:
        copy.start()
    for copy in copies:
        copy.wait()


def per_device(
    sizes, density, first_kernel, first_bias, second_kernel, second_bias, owners, solutes, biomass
):
    n = sizes[0]
    slots = solutes.shape[3]
    capacity = slots // n
    anywhere = pl.BlockSpec(memory_space=pltpu.HBM)
    groups = slots // 8
    inside = pl.BlockSpec(memory_space=pltpu.VMEM)
    operands = (
        density,
        first_kernel.transpose(2, 1, 0).reshape(8, 27),
        first_bias,
        second_kernel.transpose(1, 2, 0).reshape(16, 27),
        second_bias,
        owners.reshape(-1),
        solutes.reshape(groups, 256, BX),
        biomass.reshape(groups, 128, BX),
    )
    if sizes == (4, 2, 2) and capacity == 8:
        frac, state_new = column_call(n, groups, density, operands)
    else:
        frac, state_new = exchange_call(sizes, capacity, groups, density, operands)
    fractions, solutes_next = pl.pallas_call(
        write_out,
        out_shape=(
            jax.ShapeDtypeStruct((2,) + density.shape, BF16),
            jax.ShapeDtypeStruct((groups, 256, BX), F32),
        ),
        in_specs=[inside, inside],
        out_specs=(anywhere, anywhere),
        scratch_shapes=[pltpu.SemaphoreType.DMA((2,))],
        compiler_params=pltpu.CompilerParams(vmem_limit_bytes=16 * 1024 * 1024),
    )(frac, state_new)
    return fractions, solutes_next.reshape(solutes.shape)


def solution(mesh):
    sizes = tuple(mesh.shape[axis] for axis in ("gz", "gy", "col"))
    return jax.shard_map(
        functools.partial(per_device, sizes),
        mesh=mesh,
        in_specs=(
            P(("cores", "gz"), "gy", "col"),
            P(),
            P(),
            P(),
            P(),
            P(("cores", "gz"), "gy", "col", None, None),
            P(("cores", "gz"), "gy", "col", None, None, None, None, None),
            P(("cores", "gz"), "gy", "col", None, None, None, None),
        ),
        out_specs=(
            P(None, ("cores", "gz"), "gy", "col"),
            P(("cores", "gz"), "gy", "col", None, None, None, None, None),
        ),
        check_vma=False,
    )
```
